32 devices in a mesh: ax: 8 (over y, x, core), th: 4 (over z).
Axes of the slice: x: 2, y: 2, z: 4, core: 2. Of those that a mesh axis runs over, the one named last changes fastest.
Arguments:
- populations: float32 [26, 16, 32, 1024], P(None, None, 'th', 'ax')
- wall_free: float32 [128, 32768], P(None, ('ax', 'th')), may hold values from 0 to 1
- wall_bound: float32 [128, 32768], P(None, ('ax', 'th')), may hold values from 0 to 0.5
- wall_propagator: float32 [128, 128], replicated
- bind_on: float32 [128], replicated, may hold values from 0.02 to 0.2
- bind_off: float32 [128], replicated, may hold values from 0.02 to 0.2
- iface_sector: int32 [32768, 1], P(('ax', 'th')), may hold values from 0 to 3; in each aligned block of 1024 rows (0 to 1023, 1024 to 2047, ...) at most 256 rows name the same one
- iface_line: int32 [32768], P(('ax', 'th')), may hold values from 0 to 1023
- strut_mask: int32 [32768], P(('ax', 'th')), may hold values 0 or 1
Outputs:
- drug_field: float32 [16, 32, 1024], P(None, 'th', 'ax')
- axial_flow: float32 [16, 32, 1024], P(None, 'th', 'ax')
- free_drug: float32 [128, 32768], P(None, ('ax', 'th'))
- bound_drug: float32 [128, 32768], P(None, ('ax', 'th'))
The draws below stay inside these ranges and needn't reach their ends.
Inputs may be any that keep to these rules, and one draw needn't show every extreme that they name: `iface_sector`: among the rows of one device at most 256 name one sector, and in some device exactly 256 do.
All inputs are finite; a program needn't handle non-finite values. No bound on the sum of `strut_mask` on one device may be relied on, other than what follows from the above.
Results may differ from the reference program's by a relative error of at most 0.00023.
Values sent between devices are 32-bit elements; how exact they have to be, the bound alone decides.
No kernel may reach another device: no remote copies, remote signals or barrier semaphores. Data moves between devices by JAX's collectives and lax.ppermute only.
A program may use at most 64 MiB of HBM per device.

```python
import math
import jax
import jax.numpy as jnp
import numpy as np
from jax import lax

CR = 16
CS = 8
CZ = 128
WR = 128
STEPS = 4
SUB = 2
NS = 32
NZ = 1024
SURF = 1024
CAP = 256
LINES = 32768
N_AX = 8
N_TH = 4


DRAW_VELOCITIES = [(0, 0, 0), (1, 0, 0), (-1, 0, 0), (0, 1, 0), (0, -1, 0), (0, 0, 1), (0, 0, -1), (1, 1, 0), (-1, -1, 0), (1, -1, 0), (-1, 1, 0), (1, 0, 1), (-1, 0, -1), (1, 0, -1), (-1, 0, 1), (0, 1, 1), (0, -1, -1), (0, 1, -1), (0, -1, 1), (0, 0, 0), (1, 0, 0), (-1, 0, 0), (0, 1, 0), (0, -1, 0), (0, 0, 1), (0, 0, -1)]


DRAW_WEIGHTS = [1.0 / 3.0] + [1.0 / 18.0] * 6 + [1.0 / 36.0] * 12 + [0.25] + [0.125] * 6


def draw_populations(key, part):
    keys = jax.random.split(key, 6)
    shape = (CR, NS, NZ)
    density = 1.0 + 0.1 * jax.random.uniform(keys[0], shape, jnp.float32, -1.0, 1.0)
    speed_z = 0.05 + 0.06 * jax.random.uniform(keys[1], shape, jnp.float32, -1.0, 1.0)
    speed_s = 0.06 * jax.random.uniform(keys[2], shape, jnp.float32, -1.0, 1.0)
    speed_r = 0.05 * jax.random.uniform(keys[3], shape, jnp.float32, -1.0, 1.0)
    concentration = jnp.exp(jax.random.uniform(keys[4], shape, jnp.float32, -1.6, 0.7))
    members = []
    speed_sq = speed_z * speed_z + speed_s * speed_s + speed_r * speed_r
    for member in range(26):
        step_z, step_s, step_r = DRAW_VELOCITIES[member]
        projected = step_z * speed_z + step_s * speed_s + step_r * speed_r
        if member < 19:
            members.append(DRAW_WEIGHTS[member] * density * (1.0 + 3.0 * projected + 4.5 * projected * projected - 1.5 * speed_sq))
        else:
            members.append(DRAW_WEIGHTS[member] * concentration * (1.0 + 4.0 * projected))
    noise = 1.0 + 0.05 * jax.random.uniform(keys[5], (26,) + shape, jnp.float32, -1.0, 1.0)
    return jnp.stack(members) * noise


def draw_wall_propagator(key, part):
    keys = jax.random.split(key, 2)
    across = jnp.arange(WR, dtype=jnp.int32)
    diagonal_mask = across[:, None] == across[None, :]
    diagonal = jax.random.uniform(keys[0], (WR,), jnp.float32, 0.45, 0.6)
    spread = jax.random.uniform(keys[1], (WR, WR), jnp.float32, 0.0, 0.6 / (WR - 1))
    return jnp.where(diagonal_mask, diagonal[:, None], spread)


def set_ends(result, rng, least, top_value):
    place = [jax.random.randint(jax.random.fold_in(rng, axis), (), 0, length) for axis, length in enumerate(result.shape)]
    main_axis = result.shape.index(max(result.shape))
    next_to = place[:main_axis] + [(place[main_axis] + 1) % result.shape[main_axis]] + place[main_axis + 1:]
    return result.at[tuple(place)].set(least).at[tuple(next_to)].set(top_value)


def block_levels(own_key, shape, cuts, smallest, largest):
    level, own = 1.0, jax.random.fold_in(own_key, 6)
    for dim, parts in cuts:
        steps = jnp.exp(jax.random.uniform(jax.random.fold_in(own, dim), (parts,), jnp.float32, smallest / len(cuts), largest / len(cuts)))
        level = level * jnp.repeat(steps, shape[dim] // parts).reshape([-1 if axis == dim else 1 for axis in range(len(shape))])
    return level


def routed_block(key, own, number, rows, number_of, top, reach, skew):
    order = jax.random.permutation(key, number_of)
    crowded, usual = shares(number_of, rows * top, reach, skew, True), shares(number_of, rows * top, reach, skew, False)
    places = jnp.arange(number_of)

    def named(sizes, turn):
        used = int((sizes > 0).sum())
        fixed = max(1, used // 4)
        shifted = fixed + (places - fixed + turn * (used - fixed)) % max(1, number_of - fixed)
        return jnp.zeros((number_of,), jnp.int32).at[order[jnp.where(places < fixed, places, shifted)]].set(jnp.asarray(sizes, jnp.int32))

    sizes = jnp.where(number % 4 == 0, named(crowded, number // 4), named(usual, number - number // 4 - 1))
    mixed = jax.random.permutation(jax.random.fold_in(own, 3), number_of)
    source_of, sink = mixed[0:number_of // 2 * 2:2], mixed[1:number_of // 2 * 2:2]
    margin = jnp.minimum(sizes[source_of] - 1, reach - sizes[sink]) // 2
    margin = jnp.where((source_of == order[0]) | (sink == order[0]) | (sizes[sink] == 0), 0, jnp.maximum(margin, 0))
    shifted = jax.random.randint(jax.random.fold_in(own, 4), (number_of // 2,), 0, 1 << 20) % (margin + 1)
    sizes = sizes.at[source_of].add(-shifted).at[sink].add(shifted)
    labels = jnp.searchsorted(jnp.cumsum(sizes), jnp.arange(rows * top), side="right").astype(jnp.int32)
    listing = labels.reshape(top, rows).T
    listing = listing[jax.random.permutation(jax.random.fold_in(own, 1), rows)]
    turn = jax.random.randint(jax.random.fold_in(own, 2), (rows, 1), 0, top)
    return jnp.take_along_axis(listing, (jnp.arange(top)[None, :] + turn) % top, axis=1)


def shares(number_of, total, most, slope, full):
    loads = [(1 << 20) // math.isqrt(rank ** slope) + 1 for rank in range(1, number_of + 1)]
    largest = most if full else min(most, max(-(-total // number_of), total * loads[0] // sum(loads)))
    least = 1 if total - largest >= number_of - 1 else 0
    counts, rest = [largest] + [least] * (number_of - 1), total - largest - least * (number_of - 1)
    while rest > 0:
        free = [i for i in range(1, number_of) if counts[i] < largest] or [i for i in range(1, number_of) if counts[i] < most]
        whole, left = sum([loads[i] for i in free]), rest
        for i in free:
            addition = min(most - counts[i], max(1, left * loads[i] // whole), rest)
            counts[i] = counts[i] + addition
            rest = rest - addition
    return np.array(counts)


def setup_inputs(seed: int = 0) -> dict:
    splits = jax.random.split(jax.random.key(seed), 10)
    populations = draw_populations(jax.random.fold_in(splits[9], 71), 0)
    wall_free = jnp.clip(1.0 * jax.random.uniform(splits[1], (WR, LINES), jnp.float32) ** block_levels(splits[1], (WR, LINES), ((1, 32),), -0.2, 0.2), 0.0, 1.0)
    wall_bound = jnp.clip(0.5 * jax.random.uniform(splits[2], (WR, LINES), jnp.float32) ** block_levels(splits[2], (WR, LINES), ((1, 32),), -0.2, 0.2), 0.0, 0.5)
    wall_propagator = draw_wall_propagator(jax.random.fold_in(splits[9], 71), 0)
    bind_on = jnp.clip(jnp.exp(jax.random.uniform(splits[4], (WR,), jnp.float32, math.log(0.02), math.log(0.2))), 0.02, 0.2)
    bind_off = jnp.clip(jnp.exp(jax.random.uniform(splits[5], (WR,), jnp.float32, math.log(0.02), math.log(0.2))), 0.02, 0.2)
    iface_sector_keys = jax.random.split(jax.random.fold_in(splits[6], 1), LINES // SURF)
    iface_sector_turns = jax.random.permutation(jax.random.fold_in(splits[6], 3), LINES // SURF)
    iface_sector = jax.vmap(lambda own, number: routed_block(jax.random.fold_in(splits[6], 2), own, number, SURF, N_TH, 1, CAP, 2))(iface_sector_keys, iface_sector_turns).reshape((LINES, 1))
    iface_line = set_ends(jax.random.randint(splits[7], (LINES,), 0, SURF), jax.random.fold_in(splits[7], 1), 0, SURF - 1).astype(jnp.int32)
    strut_mask = set_ends((jax.random.randint(splits[8], (LINES,), 0, 4) < 1).astype(jnp.int32), jax.random.fold_in(splits[8], 1), 0, 1)
    return dict(populations=populations, wall_free=wall_free, wall_bound=wall_bound, wall_propagator=wall_propagator, bind_on=bind_on, bind_off=bind_off, iface_sector=iface_sector, iface_line=iface_line, strut_mask=strut_mask)


VELOCITIES = [(0, 0, 0), (1, 0, 0), (-1, 0, 0), (0, 1, 0), (0, -1, 0), (0, 0, 1), (0, 0, -1),
              (1, 1, 0), (-1, -1, 0), (1, -1, 0), (-1, 1, 0), (1, 0, 1), (-1, 0, -1), (1, 0, -1), (-1, 0, 1),
              (0, 1, 1), (0, -1, -1), (0, 1, -1), (0, -1, 1),
              (0, 0, 0), (1, 0, 0), (-1, 0, 0), (0, 1, 0), (0, -1, 0), (0, 0, 1), (0, 0, -1)]
WEIGHTS = [1.0 / 3.0] + [1.0 / 18.0] * 6 + [1.0 / 36.0] * 12 + [0.25] + [0.125] * 6
OPPOSITE = [0, 2, 1, 4, 3, 6, 5, 8, 7, 10, 9, 12, 11, 14, 13, 16, 15, 18, 17, 19, 21, 20, 23, 22, 25, 24]
MIRROR = [0, 1, 2, 3, 4, 6, 5, 7, 8, 9, 10, 13, 14, 11, 12, 17, 18, 15, 16, 19, 20, 21, 22, 23, 25, 24]
RELAX_FLOW = 1.25
RELAX_DRUG = 1.1
PUSH_AXIAL = 0.0001
PERMEABILITY = 0.3
RELEASE_RATE = 0.5


def collide(state):
    table = jnp.array(VELOCITIES, jnp.float32)
    weights = jnp.array(WEIGHTS, jnp.float32)[:, None, None, None]
    flow = state[:19]
    drug = state[19:]
    density = jnp.sum(flow, axis=0)
    momentum = jnp.einsum("qd,qabc->dabc", table[:19], flow, precision=lax.Precision.HIGHEST)
    momentum = momentum.at[0].add(PUSH_AXIAL)
    velocity = momentum / density
    projected = jnp.einsum("qd,dabc->qabc", table, velocity, precision=lax.Precision.HIGHEST)
    speed_sq = jnp.sum(velocity * velocity, axis=0)
    blood_proj = projected[:19]
    flow_eq = weights[:19] * density * (1.0 + 3.0 * blood_proj + 4.5 * blood_proj * blood_proj - 1.5 * speed_sq)
    concentration = jnp.sum(drug, axis=0)
    drug_eq = weights[19:] * concentration * (1.0 + 4.0 * projected[19:])
    return jnp.concatenate([flow - RELAX_FLOW * (flow - flow_eq), drug - RELAX_DRUG * (drug - drug_eq)], axis=0)


def stream_padded(padded, post):
    radial = post.shape[1]
    across = post.shape[2]
    along = post.shape[3]
    ghost = padded[:, 0:1][jnp.array(MIRROR, jnp.int32)]
    extended = jnp.concatenate([ghost, padded, jnp.zeros_like(ghost)], axis=1)
    portions = []
    for member in range(26):
        step_z, step_s, step_r = VELOCITIES[member]
        portion = extended[member, 1 - step_r:1 - step_r + radial, 1 - step_s:1 - step_s + across, 1 - step_z:1 - step_z + along]
        if step_r == -1:
            portion = portion.at[radial - 1].set(post[OPPOSITE[member], radial - 1])
        portions.append(portion)
    return jnp.stack(portions)


def wall_update(free, bound, source, strut_part, wall_propagator, bind_on, bind_off):
    free = free.at[0].add(source + RELEASE_RATE * strut_part)
    for substep in range(SUB):
        free = jnp.dot(wall_propagator, free, precision=lax.Precision.HIGHEST, preferred_element_type=jnp.float32)
        rate = bind_on[:, None] * free * (1.0 - bound) - bind_off[:, None] * bound
        free = free - rate
        bound = bound + rate
    return free, bound


def axial_momentum(state):
    table = jnp.array(VELOCITIES, jnp.float32)
    return jnp.einsum("q,qabc->abc", table[:19, 0], state[:19], precision=lax.Precision.HIGHEST)


def reference(populations, wall_free, wall_bound, wall_propagator, bind_on, bind_off, iface_sector, iface_line, strut_mask):
    drug_weights = jnp.array(WEIGHTS[19:], jnp.float32)[:, None, None]
    rows = jnp.arange(LINES, dtype=jnp.int32)
    slab = rows // (N_TH * SURF)
    target = ((slab * N_TH + iface_sector[:, 0]) * SURF + iface_line).astype(jnp.int32)
    strut_part = strut_mask.astype(jnp.float32)
    open_row = PERMEABILITY * (1.0 - strut_part[target])
    state, free, bound = populations, wall_free, wall_bound
    for round_index in range(STEPS):
        surface = jnp.sum(state[19:, CR - 1], axis=0)
        surface_rows = surface.reshape(N_TH, CS, N_AX, CZ).transpose(2, 0, 1, 3).reshape(LINES)
        flux = open_row * (surface_rows - free[0, target])
        source = jnp.zeros((LINES,), jnp.float32).at[target].add(flux)
        flux_field = flux.reshape(N_AX, N_TH, CS, CZ).transpose(1, 2, 0, 3).reshape(NS, NZ)
        free, bound = wall_update(free, bound, source, strut_part, wall_propagator, bind_on, bind_off)
        state = state.at[19:, CR - 1].add(-drug_weights * flux_field)
        post = collide(state)
        padded = jnp.pad(post, ((0, 0), (0, 0), (1, 1), (1, 1)), mode="wrap")
        state = stream_padded(padded, post)
    return jnp.sum(state[19:], axis=0), axial_momentum(state), free, bound
```

```python
import functools

import jax
import jax.numpy as jnp
from jax import lax
from jax.experimental import pallas as pl
from jax.experimental.pallas import tpu as pltpu
from jax.sharding import PartitionSpec as P

STEPS = 4
SUB = 2

VELOCITIES = [
    (0, 0, 0), (1, 0, 0), (-1, 0, 0), (0, 1, 0), (0, -1, 0), (0, 0, 1), (0, 0, -1),
    (1, 1, 0), (-1, -1, 0), (1, -1, 0), (-1, 1, 0),
    (1, 0, 1), (-1, 0, -1), (1, 0, -1), (-1, 0, 1),
    (0, 1, 1), (0, -1, -1), (0, 1, -1), (0, -1, 1),
    (0, 0, 0), (1, 0, 0), (-1, 0, 0), (0, 1, 0), (0, -1, 0), (0, 0, 1), (0, 0, -1),
]
WEIGHTS = [1.0 / 3.0] + [1.0 / 18.0] * 6 + [1.0 / 36.0] * 12 + [0.25] + [0.125] * 6
OPPOSITE = [0, 2, 1, 4, 3, 6, 5, 8, 7, 10, 9, 12, 11, 14, 13, 16, 15, 18, 17, 19, 21, 20, 23, 22, 25, 24]
MIRROR = [0, 1, 2, 3, 4, 6, 5, 7, 8, 9, 10, 13, 14, 11, 12, 17, 18, 15, 16, 19, 20, 21, 22, 23, 25, 24]
SECTOR_RISING = [3, 7, 10, 15, 17, 22]
SECTOR_FALLING = [4, 8, 9, 16, 18, 23]
SLAB_RISING = [1, 7, 9, 11, 13, 20]
SLAB_FALLING = [2, 8, 10, 12, 14, 21]
PAIRS = [(1, 2), (3, 4), (5, 6), (7, 8), (9, 10), (11, 12), (13, 14), (15, 16), (17, 18)]
DRUG_PAIRS = [(20, 21), (22, 23), (24, 25)]
FLOWS = 19
MEMBERS = 26
RELAX_FLOW = 1.25
RELAX_DRUG = 1.1
PUSH_AXIAL = 0.0001
PERMEABILITY = 0.3
RELEASE_RATE = 0.5

F32 = jnp.float32
BF16 = jnp.bfloat16
VMEM = pltpu.VMEM


def shifted(block, axis, distance):
    count = lax.axis_size(axis)
    return lax.ppermute(block, axis, [((i - distance) % count, i) for i in range(count)])


def lanes(shape):
    return lax.broadcasted_iota(jnp.int32, shape, len(shape) - 1)


def sublanes(shape):
    return lax.broadcasted_iota(jnp.int32, shape, len(shape) - 2)


def split3(value):
    high = value.astype(BF16)
    rest = value - high.astype(F32)
    middle = rest.astype(BF16)
    low = (rest - middle.astype(F32)).astype(BF16)
    return high, middle, low


def one_hot_lines(low_row, width):
    shape = (width, low_row.shape[-1])
    return jnp.where(sublanes(shape) == low_row, 1.0, 0.0).astype(BF16)


def scatter_rows(value_rows, code_rows, groups, width):
    terms, hots = [], []
    for value, code in zip(value_rows, code_rows, strict=True):
        group = code // width
        shape = (groups, value.shape[-1])
        hit = sublanes(shape) == group
        terms.append(jnp.concatenate([jnp.where(hit, part.astype(F32), 0.0) for part in split3(value)], axis=0).astype(BF16))
        hots.append(one_hot_lines(code - group * width, width))
    left = jnp.concatenate(terms, axis=1)
    right = jnp.concatenate(hots, axis=1)
    total = lax.dot_general(left, right, (((1,), (1,)), ((), ())), preferred_element_type=F32)
    return total[:groups] + total[groups:2 * groups] + total[2 * groups:3 * groups]


def gather_rows(table, code_rows, width):
    groups = table.shape[0]
    left = jnp.concatenate(split3(table), axis=0)
    lows = [code - (code // width) * width for code in code_rows]
    right = jnp.concatenate([one_hot_lines(low, width) for low in lows], axis=1)
    picked = jnp.dot(left, right, preferred_element_type=F32)
    picked = picked[:groups] + picked[groups:2 * groups] + picked[2 * groups:3 * groups]
    results, start = [], 0
    for code in code_rows:
        count = code.shape[-1]
        hit = sublanes((groups, count)) == code // width
        results.append(jnp.sum(jnp.where(hit, picked[:, start:start + count], 0.0), axis=0, keepdims=True))
        start += count
    return results


def source_plane(member, level, radial):
    step_r = VELOCITIES[member][2]
    if step_r == 1:
        return ((MIRROR[member], 0) if level == 0 else (member, level - 1)), True
    if step_r == -1:
        return ((OPPOSITE[member], radial - 1), False) if level == radial - 1 else ((member, level + 1), True)
    return (member, level), True


def axial_shift(value, step, member, level, radial, behind, ahead):
    along = value.shape[-1]
    lane = lanes(value.shape)
    if step == 1:
        slot = SLAB_RISING.index(member) * radial + level
        return jnp.where(lane == 0, pltpu.roll(behind, (-slot) % along, 1), pltpu.roll(value, 1, 1))
    slot = SLAB_FALLING.index(member) * radial + level
    return jnp.where(lane == along - 1, pltpu.roll(ahead, (along - 1 - slot) % along, 1), pltpu.roll(value, along - 1, 1))


def streamed(post, member, level, radial, behind, ahead, below_row, above_row):
    (origin, depth), moves = source_plane(member, level, radial)
    value = post[origin, depth]
    if not moves:
        return value
    step_z, step_s, _ = VELOCITIES[member]
    across = value.shape[0]
    if step_z:
        value = axial_shift(value, step_z, origin, depth, radial, behind, ahead)
    if step_s == 1:
        row = below_row(SECTOR_RISING.index(origin) * radial + depth)
        value = jnp.where(sublanes(value.shape) == 0, row, pltpu.roll(value, 1, 0))
    elif step_s == -1:
        row = above_row(SECTOR_FALLING.index(origin) * radial + depth)
        value = jnp.where(sublanes(value.shape) == across - 1, row, pltpu.roll(value, across - 1, 0))
    return value


def collide(members):
    def total(component):
        up, down = None, None
        for member in range(1, FLOWS):
            factor = VELOCITIES[member][component]
            if factor > 0:
                up = members[member] if up is None else up + members[member]
            elif factor < 0:
                down = members[member] if down is None else down + members[member]
        return up - down

    density = members[0]
    for member in range(1, FLOWS):
        density = density + members[member]
    inverse = 1.0 / density
    velocity = [(total(0) + PUSH_AXIAL) * inverse, total(1) * inverse, total(2) * inverse]
    speed_sq = velocity[0] * velocity[0] + velocity[1] * velocity[1] + velocity[2] * velocity[2]
    base = 1.0 - 1.5 * speed_sq
    weighted = {}
    for weight in sorted(set(WEIGHTS[:FLOWS])):
        weighted[weight] = (RELAX_FLOW * weight) * density

    def projected(member):
        result = None
        for component in range(3):
            factor = VELOCITIES[member][component]
            if factor == 0:
                continue
            if result is None:
                result = velocity[component] if factor > 0 else -velocity[component]
            else:
                result = result + velocity[component] if factor > 0 else result - velocity[component]
        return result

    results = [None] * MEMBERS
    results[0] = (1.0 - RELAX_FLOW) * members[0] + weighted[WEIGHTS[0]] * base
    for first, second in PAIRS:
        along = projected(first)
        even = weighted[WEIGHTS[first]] * (base + 4.5 * along * along)
        odd = weighted[WEIGHTS[first]] * (3.0 * along)
        results[first] = (1.0 - RELAX_FLOW) * members[first] + (even + odd)
        results[second] = (1.0 - RELAX_FLOW) * members[second] + (even - odd)
    concentration = members[FLOWS]
    for member in range(FLOWS + 1, MEMBERS):
        concentration = concentration + members[member]
    rest = (RELAX_DRUG * WEIGHTS[FLOWS]) * concentration
    results[FLOWS] = (1.0 - RELAX_DRUG) * members[FLOWS] + rest
    even = (RELAX_DRUG * WEIGHTS[FLOWS + 1]) * concentration
    for first, second in DRUG_PAIRS:
        odd = even * (4.0 * projected(first))
        results[first] = (1.0 - RELAX_DRUG) * members[first] + (even + odd)
        results[second] = (1.0 - RELAX_DRUG) * members[second] + (even - odd)
    return results


def code_list(codes):
    return [codes[row:row + 1, :] for row in range(codes.shape[0])]


def pack_lines(row, width):
    return jnp.concatenate([row[:, start:start + width] for start in range(0, row.shape[-1], width)], axis=0)


def first_kernel(sectors, drug_ref, code_ref, strut_ref, free_ref, *outs):
    across, width = code_ref.shape
    codes = code_ref[...]
    surface = drug_ref[0, 0]
    for member in range(1, drug_ref.shape[0]):
        surface = surface + drug_ref[member, 0]
    rows = code_list(codes)
    groups = sectors * across
    sums = scatter_rows(code_list(surface), rows, groups, width)
    counts = scatter_rows(code_list(jnp.ones_like(surface)), rows, groups, width)
    first = pack_lines(free_ref[0:1, :], width)
    openness = PERMEABILITY * (1.0 - strut_ref[...].astype(F32))
    for rel in range(sectors):
        out = outs[rel]
        out[0:across] = sums[rel * across:(rel + 1) * across]
        out[across:2 * across] = counts[rel * across:(rel + 1) * across]
        out[2 * across:3 * across] = first
        out[3 * across:4 * across] = openness
        if rel in (1, sectors - 1):
            edge = codes[across - 1:across] if rel == 1 else codes[0:1]
            out[4 * across:5 * across] = jnp.broadcast_to(edge, (across, width)).astype(F32)


def step_kernel(sectors, first, *refs):
    refs = list(refs)
    post_ref, code_ref = refs[0], refs[1]
    inbox = refs[2:2 + sectors]
    refs = refs[2 + sectors:]
    if first:
        new_ref, rise_ref, fall_ref, open_ref = refs
    else:
        behind_ref, ahead_ref, open_ref, new_ref, rise_ref, fall_ref = refs
    radial, across, along = post_ref.shape[1:]
    codes = code_list(code_ref[...])
    offset = 2 * across if first else across
    table = jnp.concatenate([box[offset:offset + across, :] for box in inbox], axis=0)
    picked = jnp.concatenate(gather_rows(table, codes, along), axis=0)
    if first:
        table = jnp.concatenate([box[3 * across:4 * across, :] for box in inbox], axis=0)
        openness = jnp.concatenate(gather_rows(table, codes, along), axis=0)
        open_ref[...] = openness
    else:
        openness = open_ref[...]
        behind, ahead = behind_ref[...], ahead_ref[...]
        below, above = inbox[sectors - 1], inbox[1]
        start = 2 * across

        def below_row(row):
            return jnp.broadcast_to(below[start + row:start + row + 1, :], (across, along))

        def above_row(row):
            return jnp.broadcast_to(above[start + row:start + row + 1, :], (across, along))

    rise = jnp.zeros((across, along), F32)
    fall = jnp.zeros((across, along), F32)
    lane = lanes((across, along))
    for level in range(radial):
        if first:
            members = [post_ref[member, level] for member in range(MEMBERS)]
        else:
            members = [streamed(post_ref, member, level, radial, behind, ahead, below_row, above_row) for member in range(MEMBERS)]
        if level == radial - 1:
            surface = members[FLOWS]
            for member in range(FLOWS + 1, MEMBERS):
                surface = surface + members[member]
            flux = openness * (surface - picked)
            for member in range(FLOWS, MEMBERS):
                members[member] = members[member] - WEIGHTS[member] * flux
        results = collide(members)
        for member in range(MEMBERS):
            new_ref[member, level] = results[member]
        for place, member in enumerate(SLAB_RISING):
            slot = place * radial + level
            rise = jnp.where(lane == slot, pltpu.roll(results[member], (slot + 1) % along, 1), rise)
        for place, member in enumerate(SLAB_FALLING):
            slot = place * radial + level
            fall = jnp.where(lane == slot, pltpu.roll(results[member], slot, 1), fall)
    rise_ref[...] = rise
    fall_ref[...] = fall


def wall_kernel(sectors, free_ref, bound_ref, spread_ref, on_ref, off_ref, strut_ref, counts_ref, *refs):
    inbox, (new_free, new_bound, top_ref) = refs[:sectors], refs[sectors:]
    across, width = strut_ref.shape
    depth = spread_ref.shape[0]
    total = inbox[0][0:across, :]
    for box in inbox[1:]:
        total = total + box[0:across, :]
    strut = strut_ref[...].astype(F32)
    first = pack_lines(free_ref[0:1, :], width)
    added = (PERMEABILITY * (1.0 - strut)) * (total - counts_ref[...] * first) + RELEASE_RATE * strut
    spread = spread_ref[...]
    rate_on = jnp.transpose(jnp.broadcast_to(on_ref[...], (depth, depth)))
    rate_off = jnp.transpose(jnp.broadcast_to(off_ref[...], (depth, depth)))
    is_top = sublanes((depth, width)) == 0
    for row in range(across):
        place = slice(row * width, (row + 1) * width)
        free = free_ref[:, place] + jnp.where(is_top, added[row:row + 1, :], 0.0)
        bound = bound_ref[:, place]
        for _ in range(SUB):
            free = jnp.dot(spread, free, precision=lax.Precision.HIGHEST, preferred_element_type=F32)
            rate = rate_on * free * (1.0 - bound) - rate_off * bound
            free = free - rate
            bound = bound + rate
        new_free[:, place] = free
        new_bound[:, place] = bound
        top_ref[row:row + 1, :] = free[0:1, :]


def edge_rows(post_ref, behind, ahead, rows_up, rows_down):
    radial, across, along = post_ref.shape[1:]
    for place, member in enumerate(SECTOR_RISING):
        for level in range(radial):
            value = post_ref[member, level]
            if VELOCITIES[member][0]:
                value = axial_shift(value, VELOCITIES[member][0], member, level, radial, behind, ahead)
            rows_up(place * radial + level, value[across - 1:across, :])
    for place, member in enumerate(SECTOR_FALLING):
        for level in range(radial):
            value = post_ref[member, level]
            if VELOCITIES[member][0]:
                value = axial_shift(value, VELOCITIES[member][0], member, level, radial, behind, ahead)
            rows_down(place * radial + level, value[0:1, :])


def send_kernel(sectors, last, *refs):
    if last:
        post_ref, behind_ref, ahead_ref, up_ref, down_ref = refs
        start = 0
    else:
        post_ref, behind_ref, ahead_ref, code_ref, edges_ref, top_ref = refs[:6]
        outs = refs[6:]
        up_ref, down_ref = outs[1], outs[sectors - 1]
    radial, across, along = post_ref.shape[1:]
    behind, ahead = behind_ref[...], ahead_ref[...]
    if not last:
        start = 2 * across
        end = radial - 1
        row = sublanes((across, along))
        surface = post_ref[FLOWS, end] + post_ref[FLOWS + 5, end - 1] + post_ref[FLOWS + 5, end]
        surface = surface + axial_shift(post_ref[FLOWS + 1, end], 1, FLOWS + 1, end, radial, behind, ahead)
        surface = surface + axial_shift(post_ref[FLOWS + 2, end], -1, FLOWS + 2, end, radial, behind, ahead)
        rising = post_ref[FLOWS + 3, end]
        falling = post_ref[FLOWS + 4, end]
        surface = surface + jnp.where(row == 0, 0.0, pltpu.roll(rising, 1, 0))
        surface = surface + jnp.where(row == across - 1, 0.0, pltpu.roll(falling, across - 1, 0))
        values = code_list(surface) + [rising[across - 1:across, :], falling[0:1, :]]
        codes = code_list(code_ref[...]) + [edges_ref[0:1, :], edges_ref[1:2, :]]
        sums = scatter_rows(values, codes, sectors * across, along)
        top = top_ref[...]
        for rel in range(sectors):
            outs[rel][0:across] = sums[rel * across:(rel + 1) * across]
            outs[rel][across:2 * across] = top

    def rows_up(index, value):
        up_ref[start + index:start + index + 1, :] = value

    def rows_down(index, value):
        down_ref[start + index:start + index + 1, :] = value

    edge_rows(post_ref, behind, ahead, rows_up, rows_down)


def last_kernel(post_ref, behind_ref, ahead_ref, below, above, drug_ref, flow_ref):
    radial, across, along = post_ref.shape[1:]
    behind, ahead = behind_ref[...], ahead_ref[...]

    def below_row(row):
        return jnp.broadcast_to(below[row:row + 1, :], (across, along))

    def above_row(row):
        return jnp.broadcast_to(above[row:row + 1, :], (across, along))

    for level in range(radial):
        def member_of(member):
            return streamed(post_ref, member, level, radial, behind, ahead, below_row, above_row)

        drug = member_of(FLOWS)
        for member in range(FLOWS + 1, MEMBERS):
            drug = drug + member_of(member)
        drug_ref[level] = drug
        flow = None
        for member in range(FLOWS):
            factor = VELOCITIES[member][0]
            if factor:
                value = member_of(member)
                flow = (value if factor > 0 else -value) if flow is None else (flow + value if factor > 0 else flow - value)
        flow_ref[level] = flow


def kernel_call(body, name, outs, count, **kwargs):
    return pl.pallas_call(
        body,
        name=name,
        out_shape=[jax.ShapeDtypeStruct(shape, F32) for shape in outs],
        in_specs=[pl.BlockSpec(memory_space=VMEM)] * count,
        out_specs=[pl.BlockSpec(memory_space=VMEM)] * len(outs),
        compiler_params=pltpu.CompilerParams(vmem_limit_bytes=24 * 1024 * 1024),
        **kwargs,
    )


def per_device(populations, wall_free, wall_bound, wall_propagator, bind_on, bind_off, iface_sector, iface_line, strut_mask):
    members, radial, across, along = populations.shape
    sectors = lax.axis_size("th")
    surface_count = iface_line.shape[0]
    plane = (across, along)
    rims = len(SECTOR_RISING) * radial
    mine = lax.axis_index("th")
    rel = (iface_sector[:, 0] - mine) % sectors
    codes = (rel * surface_count + iface_line).reshape(plane)
    strut = strut_mask.reshape(plane)
    rate_on = bind_on.reshape(1, -1)
    rate_off = bind_off.reshape(1, -1)

    def exchange(boxes):
        inbox = [boxes[0]] + [None] * (sectors - 1)
        for hop in range(1, sectors):
            inbox[sectors - hop] = shifted(boxes[hop], "th", hop)
        return inbox

    sizes = [((5 if hop in (1, sectors - 1) else 4) * across, along) for hop in range(sectors)]
    drug = populations[FLOWS:, radial - 1:]
    boxes = kernel_call(functools.partial(first_kernel, sectors), "first", sizes, 4)(drug, codes, strut, wall_free)
    inbox = exchange(boxes)
    counts = inbox[0][across:2 * across]
    for box in inbox[1:]:
        counts = counts + box[across:2 * across]
    above_edge = inbox[1][4 * across:4 * across + 1].astype(jnp.int32)
    below_edge = inbox[sectors - 1][4 * across:4 * across + 1].astype(jnp.int32)
    limit = sectors * surface_count
    edges = jnp.concatenate([(above_edge + surface_count) % limit, (below_edge + limit - surface_count) % limit], axis=0)

    state, free, bound, openness = populations, wall_free, wall_bound, None
    behind = ahead = None
    for step in range(STEPS):
        first, last = step == 0, step == STEPS - 1
        outs = [populations.shape, plane, plane] + ([plane] if first else [])
        extra = [] if first else [behind, ahead, openness]
        results = kernel_call(functools.partial(step_kernel, sectors, first), "step", outs, 2 + sectors + len(extra))(
            state, codes, *inbox, *extra
        )
        state, rise, fall = results[:3]
        openness = results[3] if first else openness
        free, bound, top = kernel_call(
            functools.partial(wall_kernel, sectors), "wall", [wall_free.shape, wall_free.shape, plane], 7 + sectors
        )(free, bound, wall_propagator, rate_on, rate_off, strut, counts, *inbox)
        behind = shifted(rise, "ax", 1)
        ahead = shifted(fall, "ax", -1)
        if last:
            up, down = kernel_call(
                functools.partial(send_kernel, sectors, True), "send", [(rims, along)] * 2, 3
            )(state, behind, ahead)
            below, above = shifted(up, "th", 1), shifted(down, "th", -1)
        else:
            sizes = [(2 * across + (rims if hop in (1, sectors - 1) else 0), along) for hop in range(sectors)]
            boxes = kernel_call(functools.partial(send_kernel, sectors, False), "send", sizes, 6)(
                state, behind, ahead, codes, edges, top
            )
            inbox = exchange(boxes)
    drug_field, axial_flow = kernel_call(last_kernel, "last", [(radial,) + plane] * 2, 5)(state, behind, ahead, below, above)
    return drug_field, axial_flow, free, bound


def solution(mesh):
    placed = (
        P(None, None, "th", "ax"),
        P(None, ("ax", "th")),
        P(None, ("ax", "th")),
        P(),
        P(),
        P(),
        P(("ax", "th"), None),
        P(("ax", "th")),
        P(("ax", "th")),
    )
    return jax.shard_map(
        per_device,
        mesh=mesh,
        in_specs=placed,
        out_specs=(
            P(None, "th", "ax"),
            P(None, "th", "ax"),
            P(None, ("ax", "th")),
            P(None, ("ax", "th")),
        ),
        check_vma=False,
    )
```

```python
import functools

import jax
import jax.numpy as jnp
from jax import lax
from jax.experimental import pallas as pl
from jax.experimental.pallas import tpu as pltpu
from jax.sharding import PartitionSpec as P

STEPS = 4
SUB = 2

VELOCITIES = [
    (0, 0, 0), (1, 0, 0), (-1, 0, 0), (0, 1, 0), (0, -1, 0), (0, 0, 1), (0, 0, -1),
    (1, 1, 0), (-1, -1, 0), (1, -1, 0), (-1, 1, 0),
    (1, 0, 1), (-1, 0, -1), (1, 0, -1), (-1, 0, 1),
    (0, 1, 1), (0, -1, -1), (0, 1, -1), (0, -1, 1),
    (0, 0, 0), (1, 0, 0), (-1, 0, 0), (0, 1, 0), (0, -1, 0), (0, 0, 1), (0, 0, -1),
]
WEIGHTS = [1.0 / 3.0] + [1.0 / 18.0] * 6 + [1.0 / 36.0] * 12 + [0.25] + [0.125] * 6
OPPOSITE = [0, 2, 1, 4, 3, 6, 5, 8, 7, 10, 9, 12, 11, 14, 13, 16, 15, 18, 17, 19, 21, 20, 23, 22, 25, 24]
MIRROR = [0, 1, 2, 3, 4, 6, 5, 7, 8, 9, 10, 13, 14, 11, 12, 17, 18, 15, 16, 19, 20, 21, 22, 23, 25, 24]
SECTOR_RISING = [3, 7, 10, 15, 17, 22]
SECTOR_FALLING = [4, 8, 9, 16, 18, 23]
SLAB_RISING = [1, 7, 9, 11, 13, 20]
SLAB_FALLING = [2, 8, 10, 12, 14, 21]
PAIRS = [(1, 2), (3, 4), (5, 6), (7, 8), (9, 10), (11, 12), (13, 14), (15, 16), (17, 18)]
FLOWS = 19
MEMBERS = 26
RELAX_FLOW = 1.25
RELAX_DRUG = 1.1
PUSH_AXIAL = 0.0001
PERMEABILITY = 0.3
RELEASE_RATE = 0.5

F32 = jnp.float32
BF16 = jnp.bfloat16
VMEM = pltpu.VMEM


def shifted(block, axis, distance):
    count = lax.axis_size(axis)
    return lax.ppermute(block, axis, [((i - distance) % count, i) for i in range(count)])


def lanes(shape):
    return lax.broadcasted_iota(jnp.int32, shape, len(shape) - 1)


def sublanes(shape):
    return lax.broadcasted_iota(jnp.int32, shape, len(shape) - 2)


def split3(value):
    high = value.astype(BF16)
    rest = value - high.astype(F32)
    middle = rest.astype(BF16)
    low = (rest - middle.astype(F32)).astype(BF16)
    return high, middle, low


def one_hot_lines(low_row, width):
    shape = (width, low_row.shape[-1])
    return jnp.where(sublanes(shape) == low_row, 1.0, 0.0).astype(BF16)


def scatter_rows(value_rows, code_rows, groups, width):
    terms, hots = [], []
    for value, code in zip(value_rows, code_rows, strict=True):
        group = code // width
        shape = (groups, value.shape[-1])
        hit = sublanes(shape) == group
        terms.append(jnp.concatenate([jnp.where(hit, part.astype(F32), 0.0) for part in split3(value)], axis=0).astype(BF16))
        hots.append(one_hot_lines(code - group * width, width))
    left = jnp.concatenate(terms, axis=1)
    right = jnp.concatenate(hots, axis=1)
    total = lax.dot_general(left, right, (((1,), (1,)), ((), ())), preferred_element_type=F32)
    return total[:groups] + total[groups:2 * groups] + total[2 * groups:3 * groups]


def gather_rows(table, code_rows, width):
    groups = table.shape[0]
    left = jnp.concatenate(split3(table), axis=0)
    lows = [code - (code // width) * width for code in code_rows]
    right = jnp.concatenate([one_hot_lines(low, width) for low in lows], axis=1)
    picked = jnp.dot(left, right, preferred_element_type=F32)
    picked = picked[:groups] + picked[groups:2 * groups] + picked[2 * groups:3 * groups]
    results, start = [], 0
    for code in code_rows:
        count = code.shape[-1]
        hit = sublanes((groups, count)) == code // width
        results.append(jnp.sum(jnp.where(hit, picked[:, start:start + count], 0.0), axis=0, keepdims=True))
        start += count
    return results


def source_plane(member, level, radial):
    step_r = VELOCITIES[member][2]
    if step_r == 1:
        return ((MIRROR[member], 0) if level == 0 else (member, level - 1)), True
    if step_r == -1:
        return ((OPPOSITE[member], radial - 1), False) if level == radial - 1 else ((member, level + 1), True)
    return (member, level), True


class Planes:
    def __init__(self, ref, radial, across):
        self.ref, self.radial, self.across = ref, radial, across

    def base(self, member, level):
        return (member * self.radial + level) * self.across

    def get(self, member, level):
        return self.ref[pl.ds(self.base(member, level), self.across), :]

    def put(self, member, level, value):
        self.ref[pl.ds(self.base(member, level), self.across), :] = value

    def rows(self, member, level, count, row):
        return self.ref[pl.ds(self.base(member, level) + row, count, stride=self.across), :]

    def put_rows(self, member, level, count, row, value):
        self.ref[pl.ds(self.base(member, level) + row, count, stride=self.across), :] = value


def axial_shift(value, step, member, level, radial, behind, ahead):
    along = value.shape[-1]
    lane = lanes(value.shape)
    if step == 1:
        slot = SLAB_RISING.index(member) * radial + level
        return jnp.where(lane == 0, pltpu.roll(behind, (-slot) % along, 1), pltpu.roll(value, 1, 1))
    slot = SLAB_FALLING.index(member) * radial + level
    return jnp.where(lane == along - 1, pltpu.roll(ahead, (along - 1 - slot) % along, 1), pltpu.roll(value, along - 1, 1))


def streamed(post, member, level, behind, ahead):
    radial, across = post.radial, post.across
    (origin, depth), moves = source_plane(member, level, radial)
    value = post.get(origin, depth)
    if not moves:
        return value
    step_z, step_s, _ = VELOCITIES[member]
    if step_z:
        value = axial_shift(value, step_z, origin, depth, radial, behind, ahead)
    if step_s:
        value = pltpu.roll(value, step_s % across, 0)
    return value


def incoming_rows(box, start, places, state, member, level, count, row):
    radial = state.radial
    step_r = VELOCITIES[member][2]
    here = start + places.index(member) * radial + level
    value = box[here - step_r:here - step_r + count, :]
    if step_r == 1 and level == 0:
        mirrored = start + places.index(MIRROR[member]) * radial
        value = jnp.where(sublanes(value.shape) == 0, box[mirrored:mirrored + 1, :], value)
    if step_r == -1 and level + count == radial:
        value = jnp.where(sublanes(value.shape) == count - 1, state.rows(member, level, count, row), value)
    return value


def relax_flow(members):
    def total(component):
        up, down = None, None
        for member in range(1, FLOWS):
            factor = VELOCITIES[member][component]
            if factor > 0:
                up = members[member] if up is None else up + members[member]
            elif factor < 0:
                down = members[member] if down is None else down + members[member]
        return up - down

    density = members[0]
    for member in range(1, FLOWS):
        density = density + members[member]
    inverse = 1.0 / density
    velocity = [(total(0) + PUSH_AXIAL) * inverse, total(1) * inverse, total(2) * inverse]
    speed_sq = velocity[0] * velocity[0] + velocity[1] * velocity[1] + velocity[2] * velocity[2]
    base = 1.0 - 1.5 * speed_sq
    weighted = {}
    for weight in sorted(set(WEIGHTS[:FLOWS])):
        weighted[weight] = (RELAX_FLOW * weight) * density

    def projected(member):
        result = None
        for component in range(3):
            factor = VELOCITIES[member][component]
            if factor == 0:
                continue
            if result is None:
                result = velocity[component] if factor > 0 else -velocity[component]
            else:
                result = result + velocity[component] if factor > 0 else result - velocity[component]
        return result

    results = [None] * FLOWS
    results[0] = (1.0 - RELAX_FLOW) * members[0] + weighted[WEIGHTS[0]] * base
    for first, second in PAIRS:
        along = projected(first)
        even = weighted[WEIGHTS[first]] * (base + 4.5 * along * along)
        odd = weighted[WEIGHTS[first]] * (3.0 * along)
        results[first] = (1.0 - RELAX_FLOW) * members[first] + (even + odd)
        results[second] = (1.0 - RELAX_FLOW) * members[second] + (even - odd)
    return results, velocity


def relax_drug(members, velocity):
    concentration = members[0]
    for member in members[1:]:
        concentration = concentration + member
    rest = (RELAX_DRUG * WEIGHTS[FLOWS]) * concentration
    results = [(1.0 - RELAX_DRUG) * members[0] + rest]
    even = (RELAX_DRUG * WEIGHTS[FLOWS + 1]) * concentration
    for component in range(3):
        odd = even * (4.0 * velocity[component])
        results.append((1.0 - RELAX_DRUG) * members[1 + 2 * component] + (even + odd))
        results.append((1.0 - RELAX_DRUG) * members[2 + 2 * component] + (even - odd))
    return results


def code_list(codes):
    return [codes[row:row + 1, :] for row in range(codes.shape[0])]


def pack_lines(row, width):
    return jnp.concatenate([row[:, start:start + width] for start in range(0, row.shape[-1], width)], axis=0)


def first_kernel(sectors, pops_ref, sector_ref, line_ref, strut_ref, free_ref, *refs):
    code_ref, boxes = refs[0], refs[1:1 + sectors]
    drug, sector, line, strut, top, sems = refs[1 + sectors:]
    across, width = code_ref.shape
    count = drug.shape[0]
    radial = pops_ref.shape[1]
    copies = [
        pltpu.make_async_copy(pops_ref.at[FLOWS:FLOWS + count, radial - 1], drug, sems.at[0]),
        pltpu.make_async_copy(sector_ref, sector, sems.at[1]),
        pltpu.make_async_copy(line_ref, line, sems.at[2]),
        pltpu.make_async_copy(strut_ref, strut, sems.at[3]),
        pltpu.make_async_copy(free_ref.at[0:across, :], top, sems.at[4]),
    ]
    for copy in copies:
        copy.start()
    for copy in copies:
        copy.wait()
    relative = sector[...] - lax.axis_index("th")
    relative = jnp.where(relative < 0, relative + sectors, relative)
    codes = relative * (across * width) + line[...]
    code_ref[...] = codes
    surface = drug[0]
    for member in range(1, count):
        surface = surface + drug[member]
    rows = code_list(codes)
    groups = sectors * across
    sums = scatter_rows(code_list(surface), rows, groups, width)
    counts = scatter_rows(code_list(jnp.ones_like(surface)), rows, groups, width)
    first = pack_lines(top[0:1, :], width)
    openness = PERMEABILITY * (1.0 - strut[...].astype(F32))
    for rel in range(sectors):
        out = boxes[rel]
        out[0:across] = sums[rel * across:(rel + 1) * across]
        out[across:2 * across] = counts[rel * across:(rel + 1) * across]
        out[2 * across:3 * across] = first
        out[3 * across:4 * across] = openness
        if rel in (1, sectors - 1):
            edge = codes[across - 1:across] if rel == 1 else codes[0:1]
            out[4 * across:5 * across] = jnp.broadcast_to(edge, (across, width)).astype(F32)


def bulk_kernel(first, radial, across, *refs):
    if first:
        state_ref, post_ref, speed_ref = refs
    else:
        old_ref, behind_ref, ahead_ref, state_ref, post_ref, speed_ref = refs
        old = Planes(old_ref, radial, across)
        behind, ahead = behind_ref[...], ahead_ref[...]
    state, post = Planes(state_ref, radial, across), Planes(post_ref, radial, across)
    for level in range(radial):
        if first:
            members = [state.get(member, level) for member in range(MEMBERS)]
        else:
            members = [streamed(old, member, level, behind, ahead) for member in range(MEMBERS)]
            for member in range(MEMBERS):
                state.put(member, level, members[member])
        results, velocity = relax_flow(members[:FLOWS])
        if level == radial - 1:
            for component in range(3):
                speed_ref[component * across:(component + 1) * across, :] = velocity[component]
        else:
            results = results + relax_drug(members[FLOWS:], velocity)
        for member, value in enumerate(results):
            post.put(member, level, value)


def flux_kernel(sectors, first, radial, *refs):
    refs = list(refs)
    state_ref, bulk_ref, speed_ref, code_ref = refs[:4]
    inbox = refs[4:4 + sectors]
    refs = refs[4 + sectors:]
    if first:
        post_ref, rise_ref, fall_ref, open_ref, counts_ref, edges_ref = refs
    else:
        open_ref, post_ref, rise_ref, fall_ref = refs
    del bulk_ref
    across, along = code_ref.shape
    end = radial - 1
    state, post = Planes(state_ref, radial, across), Planes(post_ref, radial, across)
    codes = code_list(code_ref[...])
    offset = 2 * across if first else across
    table = jnp.concatenate([box[offset:offset + across, :] for box in inbox], axis=0)
    picked = jnp.concatenate(gather_rows(table, codes, along), axis=0)
    below, above = inbox[sectors - 1], inbox[1]
    if first:
        table = jnp.concatenate([box[3 * across:4 * across, :] for box in inbox], axis=0)
        openness = jnp.concatenate(gather_rows(table, codes, along), axis=0)
        open_ref[...] = openness
        counts = inbox[0][across:2 * across, :]
        for box in inbox[1:]:
            counts = counts + box[across:2 * across, :]
        counts_ref[...] = counts
        count, limit = across * along, sectors * across * along
        up = above[4 * across:5 * across, :].astype(jnp.int32) + count
        down = below[4 * across:5 * across, :].astype(jnp.int32) - count
        up = jnp.where(up >= limit, up - limit, up)
        down = jnp.where(down < 0, down + limit, down)
        edges_ref[...] = jnp.where(sublanes(up.shape) == 0, up, down)
    else:
        openness = open_ref[...]
    start = 2 * across
    row = sublanes((across, along))
    drugs = [state.get(member, end) for member in range(FLOWS, MEMBERS)]
    if not first:
        last = start + SECTOR_RISING.index(FLOWS + 3) * radial + end
        drugs[3] = jnp.where(row == 0, below[last:last + 1, :], drugs[3])
        last = start + SECTOR_FALLING.index(FLOWS + 4) * radial + end
        drugs[4] = jnp.where(row == across - 1, above[last:last + 1, :], drugs[4])
    surface = drugs[0]
    for drug in drugs[1:]:
        surface = surface + drug
    flux = openness * (surface - picked)
    drugs = [drug - WEIGHTS[FLOWS + place] * flux for place, drug in enumerate(drugs)]
    velocity = [speed_ref[component * across:(component + 1) * across, :] for component in range(3)]
    for place, value in enumerate(relax_drug(drugs, velocity)):
        post.put(FLOWS + place, end, value)
    if not first:
        block = across
        for side, box, places in ((0, below, SECTOR_RISING), (across - 1, above, SECTOR_FALLING)):
            moving = 1 if side == 0 else -1
            for level in range(0, radial, block):
                members = []
                for member in range(MEMBERS):
                    if VELOCITIES[member][1] == moving:
                        value = incoming_rows(box, start, places, state, member, level, block, side)
                    else:
                        value = state.rows(member, level, block, side)
                    if member >= FLOWS and level + block == radial:
                        lowered = value - WEIGHTS[member] * flux[side:side + 1, :]
                        value = jnp.where(sublanes(value.shape) == block - 1, lowered, value)
                    members.append(value)
                results, velocity = relax_flow(members[:FLOWS])
                results = results + relax_drug(members[FLOWS:], velocity)
                for member, value in enumerate(results):
                    post.put_rows(member, level, block, side, value)
    rise = jnp.zeros((across, along), F32)
    fall = jnp.zeros((across, along), F32)
    lane = lanes((across, along))
    for level in range(radial):
        for place, member in enumerate(SLAB_RISING):
            slot = place * radial + level
            rise = jnp.where(lane == slot, pltpu.roll(post.get(member, level), (slot + 1) % along, 1), rise)
        for place, member in enumerate(SLAB_FALLING):
            slot = place * radial + level
            fall = jnp.where(lane == slot, pltpu.roll(post.get(member, level), slot, 1), fall)
    rise_ref[...] = rise
    fall_ref[...] = fall


def wall_kernel(sectors, free_ref, bound_ref, spread_ref, on_ref, off_ref, strut_ref, counts_ref, *refs):
    inbox, (new_free, new_bound, top_ref) = refs[:sectors], refs[sectors:]
    across, width = strut_ref.shape
    depth = spread_ref.shape[0]
    total = inbox[0][0:across, :]
    for box in inbox[1:]:
        total = total + box[0:across, :]
    strut = strut_ref[...].astype(F32)
    first = pack_lines(free_ref[0:1, :], width)
    added = (PERMEABILITY * (1.0 - strut)) * (total - counts_ref[...] * first) + RELEASE_RATE * strut
    spread = spread_ref[...]
    rate_on = jnp.transpose(jnp.broadcast_to(on_ref[...], (depth, depth)))
    rate_off = jnp.transpose(jnp.broadcast_to(off_ref[...], (depth, depth)))
    is_top = sublanes((depth, width)) == 0
    for row in range(across):
        place = slice(row * width, (row + 1) * width)
        free = free_ref[:, place] + jnp.where(is_top, added[row:row + 1, :], 0.0)
        bound = bound_ref[:, place]
        for _ in range(SUB):
            free = jnp.dot(spread, free, precision=lax.Precision.HIGHEST, preferred_element_type=F32)
            rate = rate_on * free * (1.0 - bound) - rate_off * bound
            free = free - rate
            bound = bound + rate
        new_free[:, place] = free
        new_bound[:, place] = bound
        top_ref[row:row + 1, :] = free[0:1, :]


def send_kernel(sectors, radial, post_ref, behind_ref, ahead_ref, code_ref, edges_ref, top_ref, *outs):
    across, along = code_ref.shape
    post = Planes(post_ref, radial, across)
    behind, ahead = behind_ref[...], ahead_ref[...]
    end = radial - 1
    row = sublanes((across, along))
    surface = post.get(FLOWS, end) + post.get(FLOWS + 5, end - 1) + post.get(FLOWS + 5, end)
    surface = surface + axial_shift(post.get(FLOWS + 1, end), 1, FLOWS + 1, end, radial, behind, ahead)
    surface = surface + axial_shift(post.get(FLOWS + 2, end), -1, FLOWS + 2, end, radial, behind, ahead)
    rising = post.get(FLOWS + 3, end)
    falling = post.get(FLOWS + 4, end)
    surface = surface + jnp.where(row == 0, 0.0, pltpu.roll(rising, 1, 0))
    surface = surface + jnp.where(row == across - 1, 0.0, pltpu.roll(falling, across - 1, 0))
    values = code_list(surface) + [rising[across - 1:across, :], falling[0:1, :]]
    codes = code_list(code_ref[...]) + [edges_ref[0:1, :], edges_ref[1:2, :]]
    sums = scatter_rows(values, codes, sectors * across, along)
    top = top_ref[...]
    for rel in range(sectors):
        outs[rel][0:across] = sums[rel * across:(rel + 1) * across]
        outs[rel][across:2 * across] = top
    start = 2 * across
    for out, places, side in ((outs[1], SECTOR_RISING, across - 1), (outs[sectors - 1], SECTOR_FALLING, 0)):
        for place, member in enumerate(places):
            step = VELOCITIES[member][0]
            base = start + place * radial
            if step:
                for level in range(radial):
                    value = axial_shift(post.get(member, level), step, member, level, radial, behind, ahead)
                    out[base + level:base + level + 1, :] = value[side:side + 1, :]
            else:
                out[base:base + radial, :] = post.rows(member, 0, radial, side)


def last_send_kernel(radial, across, post_ref, behind_ref, ahead_ref, up_ref, down_ref):
    post = Planes(post_ref, radial, across)
    behind, ahead = behind_ref[...], ahead_ref[...]
    for out, drug, plus, minus, side in ((up_ref, FLOWS + 3, 7, 10, across - 1), (down_ref, FLOWS + 4, 9, 8, 0)):
        out[0:radial, :] = post.rows(drug, 0, radial, side)
        for level in range(radial):
            value = axial_shift(post.get(plus, level), 1, plus, level, radial, behind, ahead)
            value = value - axial_shift(post.get(minus, level), -1, minus, level, radial, behind, ahead)
            out[radial + level:radial + level + 1, :] = value[side:side + 1, :]


def fields_kernel(radial, across, post_ref, behind_ref, ahead_ref, drug_ref, flow_ref):
    post = Planes(post_ref, radial, across)
    behind, ahead = behind_ref[...], ahead_ref[...]
    for level in range(radial):
        def member_of(member):
            value = streamed(post, member, level, behind, ahead)
            step = VELOCITIES[member][1]
            if step:
                edge = 0 if step > 0 else across - 1
                value = jnp.where(sublanes(value.shape) == edge, 0.0, value)
            return value

        drug = member_of(FLOWS)
        for member in range(FLOWS + 1, MEMBERS):
            drug = drug + member_of(member)
        drug_ref[level] = drug
        flow = None
        for member in range(FLOWS):
            factor = VELOCITIES[member][0]
            if factor:
                value = member_of(member)
                flow = (value if factor > 0 else -value) if flow is None else (flow + value if factor > 0 else flow - value)
        flow_ref[level] = flow


def last_kernel(drug_part, flow_part, below, above, drug_ref, flow_ref):
    radial, across, along = drug_ref.shape
    row = sublanes((across, along))
    for part, out, base in ((drug_part, drug_ref, 0), (flow_part, flow_ref, radial)):
        for level in range(radial):
            place = base + level
            value = part[level] + jnp.where(row == 0, below[place:place + 1, :], 0.0)
            out[level] = value + jnp.where(row == across - 1, above[place:place + 1, :], 0.0)


def kernel_call(body, name, outs, count, micros, aliases=None):
    shapes = [out if isinstance(out, jax.ShapeDtypeStruct) else jax.ShapeDtypeStruct(out, F32) for out in outs]
    return pl.pallas_call(
        body,
        name=name,
        out_shape=shapes,
        in_specs=[pl.BlockSpec(memory_space=VMEM)] * count,
        out_specs=[pl.BlockSpec(memory_space=VMEM)] * len(outs),
        input_output_aliases=aliases or {},
        cost_estimate=pl.CostEstimate(flops=0, bytes_accessed=int(micros * 3.0e6), transcendentals=0),
        compiler_params=pltpu.CompilerParams(vmem_limit_bytes=24 * 1024 * 1024),
    )


def first_call(sectors, populations, sector, line, strut, free):
    members, radial, across, along = populations.shape
    plane = (across, along)
    sizes = [((5 if hop in (1, sectors - 1) else 4) * across, along) for hop in range(sectors)]
    return pl.pallas_call(
        functools.partial(first_kernel, sectors),
        name="first",
        out_shape=[jax.ShapeDtypeStruct(plane, jnp.int32)] + [jax.ShapeDtypeStruct(size, F32) for size in sizes],
        in_specs=[pl.BlockSpec(memory_space=pltpu.HBM)] * 5,
        out_specs=[pl.BlockSpec(memory_space=VMEM)] * (1 + sectors),
        scratch_shapes=[
            VMEM((members - FLOWS, across, along), F32),
            VMEM(plane, jnp.int32),
            VMEM(plane, jnp.int32),
            VMEM(plane, jnp.int32),
            VMEM((across, free.shape[1]), F32),
            pltpu.SemaphoreType.DMA((5,)),
        ],
    )(populations, sector, line, strut, free)


def per_device(populations, wall_free, wall_bound, wall_propagator, bind_on, bind_off, iface_sector, iface_line, strut_mask):
    members, radial, across, along = populations.shape
    sectors = lax.axis_size("th")
    plane = (across, along)
    flat = (members * radial * across, along)
    rims = len(SECTOR_RISING) * radial
    strut = strut_mask.reshape(plane)
    rate_on = bind_on.reshape(1, -1)
    rate_off = bind_off.reshape(1, -1)

    def exchange(boxes):
        inbox = [boxes[0]] + [None] * (sectors - 1)
        for hop in range(1, sectors):
            inbox[sectors - hop] = shifted(boxes[hop], "th", hop)
        return inbox

    codes, *boxes = first_call(sectors, populations, iface_sector.reshape(plane), iface_line.reshape(plane), strut, wall_free)
    inbox = exchange(boxes)
    state = populations.reshape(flat)
    speeds = (3 * across, along)
    bulk, speed = kernel_call(functools.partial(bulk_kernel, True, radial, across), "bulk", [flat, speeds], 1, 1.5)(state)
    free, bound = wall_free, wall_bound
    openness = counts = edges = None
    for step in range(STEPS):
        first, last = step == 0, step == STEPS - 1
        outs = [flat, plane, plane]
        if first:
            outs = outs + [plane, plane, jax.ShapeDtypeStruct(plane, jnp.int32)]
        extra = [] if first else [openness]
        results = kernel_call(
            functools.partial(flux_kernel, sectors, first, radial), "flux", outs, 4 + sectors + len(extra), 0.8, {1: 0}
        )(state, bulk, speed, codes, *inbox, *extra)
        post, rise, fall = results[:3]
        if first:
            openness, counts, edges = results[3:]
        behind = shifted(rise, "ax", 1)
        ahead = shifted(fall, "ax", -1)
        free, bound, top = kernel_call(
            functools.partial(wall_kernel, sectors), "wall", [wall_free.shape, wall_free.shape, plane], 7 + sectors, 1.3
        )(free, bound, wall_propagator, rate_on, rate_off, strut, counts, *inbox)
        if last:
            continue
        sizes = [(2 * across + (rims if hop in (1, sectors - 1) else 0), along) for hop in range(sectors)]
        boxes = kernel_call(functools.partial(send_kernel, sectors, radial), "send", sizes, 6, 0.3)(
            post, behind, ahead, codes, edges, top
        )
        inbox = exchange(boxes)
        state, bulk, speed = kernel_call(
            functools.partial(bulk_kernel, False, radial, across), "bulk", [flat, flat, speeds], 3, 2.0
        )(post, behind, ahead)
    up, down = kernel_call(
        functools.partial(last_send_kernel, radial, across), "send", [(2 * radial, along)] * 2, 3, 0.2
    )(post, behind, ahead)
    below, above = shifted(up, "th", 1), shifted(down, "th", -1)
    parts = kernel_call(
        functools.partial(fields_kernel, radial, across), "fields", [(radial,) + plane] * 2, 3, 1.0
    )(post, behind, ahead)
    drug_field, axial_flow = kernel_call(last_kernel, "last", [(radial,) + plane] * 2, 4, 0.3)(*parts, below, above)
    return drug_field, axial_flow, free, bound


def solution(mesh):
    placed = (
        P(None, None, "th", "ax"),
        P(None, ("ax", "th")),
        P(None, ("ax", "th")),
        P(),
        P(),
        P(),
        P(("ax", "th"), None),
        P(("ax", "th")),
        P(("ax", "th")),
    )
    return jax.shard_map(
        per_device,
        mesh=mesh,
        in_specs=placed,
        out_specs=(
            P(None, "th", "ax"),
            P(None, "th", "ax"),
            P(None, ("ax", "th")),
            P(None, ("ax", "th")),
        ),
        check_vma=False,
    )
```

```python
import functools

import jax
import jax.numpy as jnp
from jax import lax
from jax.experimental import pallas as pl
from jax.experimental.pallas import tpu as pltpu
from jax.sharding import PartitionSpec as P


STEPS = 4
SUB = 2

VELOCITIES = [
    (0, 0, 0), (1, 0, 0), (-1, 0, 0), (0, 1, 0), (0, -1, 0), (0, 0, 1), (0, 0, -1),
    (1, 1, 0), (-1, -1, 0), (1, -1, 0), (-1, 1, 0),
    (1, 0, 1), (-1, 0, -1), (1, 0, -1), (-1, 0, 1),
    (0, 1, 1), (0, -1, -1), (0, 1, -1), (0, -1, 1),
    (0, 0, 0), (1, 0, 0), (-1, 0, 0), (0, 1, 0), (0, -1, 0), (0, 0, 1), (0, 0, -1),
]
WEIGHTS = [1.0 / 3.0] + [1.0 / 18.0] * 6 + [1.0 / 36.0] * 12 + [0.25] + [0.125] * 6
OPPOSITE = [0, 2, 1, 4, 3, 6, 5, 8, 7, 10, 9, 12, 11, 14, 13, 16, 15, 18, 17, 19, 21, 20, 23, 22, 25, 24]
MIRROR = [0, 1, 2, 3, 4, 6, 5, 7, 8, 9, 10, 13, 14, 11, 12, 17, 18, 15, 16, 19, 20, 21, 22, 23, 25, 24]
SECTOR_RISING = [3, 7, 10, 15, 17, 22]
SECTOR_FALLING = [4, 8, 9, 16, 18, 23]
SLAB_RISING = [1, 7, 9, 11, 13, 20]
SLAB_FALLING = [2, 8, 10, 12, 14, 21]
PAIRS = [(1, 2), (3, 4), (5, 6), (7, 8), (9, 10), (11, 12), (13, 14), (15, 16), (17, 18)]
FLOWS = 19
MEMBERS = 26
RELAX_FLOW = 1.25
RELAX_DRUG = 1.1
PUSH_AXIAL = 0.0001
PERMEABILITY = 0.3
RELEASE_RATE = 0.5

F32 = jnp.float32
BF16 = jnp.bfloat16
VMEM = pltpu.VMEM


def shifted(block, axis, distance):
    count = lax.axis_size(axis)
    return lax.ppermute(block, axis, [((i - distance) % count, i) for i in range(count)])


def paired(inner, outer):
    count = lax.axis_size("ax")
    near = [(i, i ^ 1) for i in range(count)]
    far = [(i, (i + 1) % count if i % 2 else (i - 1) % count) for i in range(count)]
    return lax.ppermute(inner, "ax", near), lax.ppermute(outer, "ax", far)


def by_parity(even, odd):
    return jnp.where(lax.axis_index("ax") % 2 == 0, even, odd)


def axial_rims(inner_ref, outer_ref):
    inner, outer = inner_ref[...], outer_ref[...]
    return by_parity(outer, inner), by_parity(inner, outer)


def lanes(shape):
    return lax.broadcasted_iota(jnp.int32, shape, len(shape) - 1)


def sublanes(shape):
    return lax.broadcasted_iota(jnp.int32, shape, len(shape) - 2)


def split3(value):
    high = value.astype(BF16)
    rest = value - high.astype(F32)
    middle = rest.astype(BF16)
    low = (rest - middle.astype(F32)).astype(BF16)
    return high, middle, low


def one_hot_lines(low_row, width):
    shape = (width, low_row.shape[-1])
    return jnp.where(sublanes(shape) == low_row, 1.0, 0.0).astype(BF16)


def scatter_rows(value_rows, code_rows, groups, width):
    terms, hots = [], []
    for value, code in zip(value_rows, code_rows, strict=True):
        group = code // width
        shape = (groups, value.shape[-1])
        hit = sublanes(shape) == group
        terms.append(jnp.concatenate([jnp.where(hit, part.astype(F32), 0.0) for part in split3(value)], axis=0).astype(BF16))
        hots.append(one_hot_lines(code - group * width, width))
    left = jnp.concatenate(terms, axis=1)
    right = jnp.concatenate(hots, axis=1)
    total = lax.dot_general(left, right, (((1,), (1,)), ((), ())), preferred_element_type=F32)
    return total[:groups] + total[groups:2 * groups] + total[2 * groups:3 * groups]


def gather_rows(table, code_rows, width):
    groups = table.shape[0]
    left = jnp.concatenate(split3(table), axis=0)
    lows = [code - (code // width) * width for code in code_rows]
    right = jnp.concatenate([one_hot_lines(low, width) for low in lows], axis=1)
    picked = jnp.dot(left, right, preferred_element_type=F32)
    picked = picked[:groups] + picked[groups:2 * groups] + picked[2 * groups:3 * groups]
    results, start = [], 0
    for code in code_rows:
        count = code.shape[-1]
        hit = sublanes((groups, count)) == code // width
        results.append(jnp.sum(jnp.where(hit, picked[:, start:start + count], 0.0), axis=0, keepdims=True))
        start += count
    return results


def source_plane(member, level, radial):
    step_r = VELOCITIES[member][2]
    if step_r == 1:
        return ((MIRROR[member], 0) if level == 0 else (member, level - 1)), True
    if step_r == -1:
        return ((OPPOSITE[member], radial - 1), False) if level == radial - 1 else ((member, level + 1), True)
    return (member, level), True


class Planes:
    def __init__(self, ref, radial, across):
        self.ref, self.radial, self.across = ref, radial, across

    def base(self, member, level):
        return (member * self.radial + level) * self.across

    def get(self, member, level):
        return self.ref[pl.ds(self.base(member, level), self.across), :]

    def put(self, member, level, value):
        self.ref[pl.ds(self.base(member, level), self.across), :] = value

    def rows(self, member, level, count, row):
        return self.ref[pl.ds(self.base(member, level) + row, count, stride=self.across), :]

    def put_rows(self, member, level, count, row, value):
        self.ref[pl.ds(self.base(member, level) + row, count, stride=self.across), :] = value


def axial_shift(value, step, member, level, radial, behind, ahead):
    along = value.shape[-1]
    lane = lanes(value.shape)
    if step == 1:
        slot = SLAB_RISING.index(member) * radial + level
        return jnp.where(lane == 0, pltpu.roll(behind, (-slot) % along, 1), pltpu.roll(value, 1, 1))
    slot = SLAB_FALLING.index(member) * radial + level
    return jnp.where(lane == along - 1, pltpu.roll(ahead, (along - 1 - slot) % along, 1), pltpu.roll(value, along - 1, 1))


def streamed(post, member, level, behind, ahead):
    radial, across = post.radial, post.across
    (origin, depth), moves = source_plane(member, level, radial)
    value = post.get(origin, depth)
    if not moves:
        return value
    step_z, step_s, _ = VELOCITIES[member]
    if step_z:
        value = axial_shift(value, step_z, origin, depth, radial, behind, ahead)
    if step_s:
        value = pltpu.roll(value, step_s % across, 0)
    return value


def incoming_rows(box, start, places, state, member, level, count, row):
    radial = state.radial
    step_r = VELOCITIES[member][2]
    here = start + places.index(member) * radial + level
    value = box[here - step_r:here - step_r + count, :]
    if step_r == 1 and level == 0:
        mirrored = start + places.index(MIRROR[member]) * radial
        value = jnp.where(sublanes(value.shape) == 0, box[mirrored:mirrored + 1, :], value)
    if step_r == -1 and level + count == radial:
        value = jnp.where(sublanes(value.shape) == count - 1, state.rows(member, level, count, row), value)
    return value


def relax_flow(members):
    def total(component):
        up, down = None, None
        for member in range(1, FLOWS):
            factor = VELOCITIES[member][component]
            if factor > 0:
                up = members[member] if up is None else up + members[member]
            elif factor < 0:
                down = members[member] if down is None else down + members[member]
        return up - down

    density = members[0]
    for member in range(1, FLOWS):
        density = density + members[member]
    inverse = 1.0 / density
    velocity = [(total(0) + PUSH_AXIAL) * inverse, total(1) * inverse, total(2) * inverse]
    speed_sq = velocity[0] * velocity[0] + velocity[1] * velocity[1] + velocity[2] * velocity[2]
    base = 1.0 - 1.5 * speed_sq
    weighted = {}
    for weight in sorted(set(WEIGHTS[:FLOWS])):
        weighted[weight] = (RELAX_FLOW * weight) * density

    def projected(member):
        result = None
        for component in range(3):
            factor = VELOCITIES[member][component]
            if factor == 0:
                continue
            if result is None:
                result = velocity[component] if factor > 0 else -velocity[component]
            else:
                result = result + velocity[component] if factor > 0 else result - velocity[component]
        return result

    results = [None] * FLOWS
    results[0] = (1.0 - RELAX_FLOW) * members[0] + weighted[WEIGHTS[0]] * base
    for first, second in PAIRS:
        along = projected(first)
        even = weighted[WEIGHTS[first]] * (base + 4.5 * along * along)
        odd = weighted[WEIGHTS[first]] * (3.0 * along)
        results[first] = (1.0 - RELAX_FLOW) * members[first] + (even + odd)
        results[second] = (1.0 - RELAX_FLOW) * members[second] + (even - odd)
    return results, velocity


def relax_drug(members, velocity):
    concentration = members[0]
    for member in members[1:]:
        concentration = concentration + member
    rest = (RELAX_DRUG * WEIGHTS[FLOWS]) * concentration
    results = [(1.0 - RELAX_DRUG) * members[0] + rest]
    even = (RELAX_DRUG * WEIGHTS[FLOWS + 1]) * concentration
    for component in range(3):
        odd = even * (4.0 * velocity[component])
        results.append((1.0 - RELAX_DRUG) * members[1 + 2 * component] + (even + odd))
        results.append((1.0 - RELAX_DRUG) * members[2 + 2 * component] + (even - odd))
    return results


def code_list(codes):
    return [codes[row:row + 1, :] for row in range(codes.shape[0])]


def pack_lines(row, width):
    return jnp.concatenate([row[:, start:start + width] for start in range(0, row.shape[-1], width)], axis=0)


def first_kernel(sectors, pops_ref, sector_ref, line_ref, strut_ref, free_ref, *refs):
    code_ref, boxes = refs[0], refs[1:1 + sectors]
    drug, sector, line, strut, top, sems = refs[1 + sectors:]
    across, width = code_ref.shape
    count = drug.shape[0]
    radial = pops_ref.shape[1]
    copies = [
        pltpu.make_async_copy(pops_ref.at[FLOWS:FLOWS + count, radial - 1], drug, sems.at[0]),
        pltpu.make_async_copy(sector_ref, sector, sems.at[1]),
        pltpu.make_async_copy(line_ref, line, sems.at[2]),
        pltpu.make_async_copy(strut_ref, strut, sems.at[3]),
        pltpu.make_async_copy(free_ref.at[0:across, :], top, sems.at[4]),
    ]
    for copy in copies:
        copy.start()
    for copy in copies:
        copy.wait()
    relative = sector[...] - lax.axis_index("th")
    relative = jnp.where(relative < 0, relative + sectors, relative)
    codes = relative * (across * width) + line[...]
    code_ref[...] = codes
    surface = drug[0]
    for member in range(1, count):
        surface = surface + drug[member]
    rows = code_list(codes)
    groups = sectors * across
    sums = scatter_rows(code_list(surface), rows, groups, width)
    counts = scatter_rows(code_list(jnp.ones_like(surface)), rows, groups, width)
    first = pack_lines(top[0:1, :], width)
    openness = PERMEABILITY * (1.0 - strut[...].astype(F32))
    for rel in range(sectors):
        out = boxes[rel]
        out[0:across] = sums[rel * across:(rel + 1) * across]
        out[across:2 * across] = counts[rel * across:(rel + 1) * across]
        out[2 * across:3 * across] = first
        out[3 * across:4 * across] = openness
        if rel in (1, sectors - 1):
            edge = codes[across - 1:across] if rel == 1 else codes[0:1]
            out[4 * across:5 * across] = jnp.broadcast_to(edge, (across, width)).astype(F32)


def bulk_kernel(first, radial, across, *refs):
    if first:
        state_ref, post_ref, speed_ref = refs
    else:
        old_ref, inner_ref, outer_ref, state_ref, post_ref, speed_ref = refs
        old = Planes(old_ref, radial, across)
        behind, ahead = axial_rims(inner_ref, outer_ref)
    state, post = Planes(state_ref, radial, across), Planes(post_ref, radial, across)
    for level in range(radial):
        if first:
            members = [state.get(member, level) for member in range(MEMBERS)]
        else:
            members = [streamed(old, member, level, behind, ahead) for member in range(MEMBERS)]
            for member in range(MEMBERS):
                state.put(member, level, members[member])
        results, velocity = relax_flow(members[:FLOWS])
        if level == radial - 1:
            for component in range(3):
                speed_ref[component * across:(component + 1) * across, :] = velocity[component]
        else:
            results = results + relax_drug(members[FLOWS:], velocity)
        for member, value in enumerate(results):
            post.put(member, level, value)


def flux_kernel(sectors, first, radial, *refs):
    refs = list(refs)
    state_ref, bulk_ref, speed_ref, code_ref = refs[:4]
    inbox = refs[4:4 + sectors]
    refs = refs[4 + sectors:]
    if first:
        post_ref, inner_ref, outer_ref, open_ref, counts_ref, edges_ref = refs
    else:
        open_ref, post_ref, inner_ref, outer_ref = refs
    del bulk_ref
    across, along = code_ref.shape
    end = radial - 1
    state, post = Planes(state_ref, radial, across), Planes(post_ref, radial, across)
    codes = code_list(code_ref[...])
    offset = 2 * across if first else across
    table = jnp.concatenate([box[offset:offset + across, :] for box in inbox], axis=0)
    picked = jnp.concatenate(gather_rows(table, codes, along), axis=0)
    below, above = inbox[sectors - 1], inbox[1]
    if first:
        table = jnp.concatenate([box[3 * across:4 * across, :] for box in inbox], axis=0)
        openness = jnp.concatenate(gather_rows(table, codes, along), axis=0)
        open_ref[...] = openness
        counts = inbox[0][across:2 * across, :]
        for box in inbox[1:]:
            counts = counts + box[across:2 * across, :]
        counts_ref[...] = counts
        count, limit = across * along, sectors * across * along
        up = above[4 * across:5 * across, :].astype(jnp.int32) + count
        down = below[4 * across:5 * across, :].astype(jnp.int32) - count
        up = jnp.where(up >= limit, up - limit, up)
        down = jnp.where(down < 0, down + limit, down)
        edges_ref[...] = jnp.where(sublanes(up.shape) == 0, up, down)
    else:
        openness = open_ref[...]
    start = 2 * across
    row = sublanes((across, along))
    drugs = [state.get(member, end) for member in range(FLOWS, MEMBERS)]
    if not first:
        last = start + SECTOR_RISING.index(FLOWS + 3) * radial + end
        drugs[3] = jnp.where(row == 0, below[last:last + 1, :], drugs[3])
        last = start + SECTOR_FALLING.index(FLOWS + 4) * radial + end
        drugs[4] = jnp.where(row == across - 1, above[last:last + 1, :], drugs[4])
    surface = drugs[0]
    for drug in drugs[1:]:
        surface = surface + drug
    flux = openness * (surface - picked)
    drugs = [drug - WEIGHTS[FLOWS + place] * flux for place, drug in enumerate(drugs)]
    velocity = [speed_ref[component * across:(component + 1) * across, :] for component in range(3)]
    for place, value in enumerate(relax_drug(drugs, velocity)):
        post.put(FLOWS + place, end, value)
    if not first:
        block = across
        for side, box, places in ((0, below, SECTOR_RISING), (across - 1, above, SECTOR_FALLING)):
            moving = 1 if side == 0 else -1
            for level in range(0, radial, block):
                members = []
                for member in range(MEMBERS):
                    if VELOCITIES[member][1] == moving:
                        value = incoming_rows(box, start, places, state, member, level, block, side)
                    else:
                        value = state.rows(member, level, block, side)
                    if member >= FLOWS and level + block == radial:
                        lowered = value - WEIGHTS[member] * flux[side:side + 1, :]
                        value = jnp.where(sublanes(value.shape) == block - 1, lowered, value)
                    members.append(value)
                results, velocity = relax_flow(members[:FLOWS])
                results = results + relax_drug(members[FLOWS:], velocity)
                for member, value in enumerate(results):
                    post.put_rows(member, level, block, side, value)
    rise = jnp.zeros((across, along), F32)
    fall = jnp.zeros((across, along), F32)
    lane = lanes((across, along))
    for level in range(radial):
        for place, member in enumerate(SLAB_RISING):
            slot = place * radial + level
            rise = jnp.where(lane == slot, pltpu.roll(post.get(member, level), (slot + 1) % along, 1), rise)
        for place, member in enumerate(SLAB_FALLING):
            slot = place * radial + level
            fall = jnp.where(lane == slot, pltpu.roll(post.get(member, level), slot, 1), fall)
    inner_ref[...] = by_parity(rise, fall)
    outer_ref[...] = by_parity(fall, rise)


def wall_kernel(sectors, free_ref, bound_ref, spread_ref, on_ref, off_ref, strut_ref, counts_ref, *refs):
    inbox, (new_free, new_bound, top_ref) = refs[:sectors], refs[sectors:]
    across, width = strut_ref.shape
    depth = spread_ref.shape[0]
    total = inbox[0][0:across, :]
    for box in inbox[1:]:
        total = total + box[0:across, :]
    strut = strut_ref[...].astype(F32)
    first = pack_lines(free_ref[0:1, :], width)
    added = (PERMEABILITY * (1.0 - strut)) * (total - counts_ref[...] * first) + RELEASE_RATE * strut
    spread = spread_ref[...]
    rate_on = jnp.transpose(jnp.broadcast_to(on_ref[...], (depth, depth)))
    rate_off = jnp.transpose(jnp.broadcast_to(off_ref[...], (depth, depth)))
    is_top = sublanes((depth, width)) == 0
    for row in range(across):
        place = slice(row * width, (row + 1) * width)
        free = free_ref[:, place] + jnp.where(is_top, added[row:row + 1, :], 0.0)
        bound = bound_ref[:, place]
        for _ in range(SUB):
            free = jnp.dot(spread, free, precision=lax.Precision.HIGHEST, preferred_element_type=F32)
            rate = rate_on * free * (1.0 - bound) - rate_off * bound
            free = free - rate
            bound = bound + rate
        new_free[:, place] = free
        new_bound[:, place] = bound
        top_ref[row:row + 1, :] = free[0:1, :]


def send_kernel(sectors, radial, post_ref, inner_ref, outer_ref, code_ref, edges_ref, top_ref, *outs):
    across, along = code_ref.shape
    post = Planes(post_ref, radial, across)
    behind, ahead = axial_rims(inner_ref, outer_ref)
    end = radial - 1
    row = sublanes((across, along))
    surface = post.get(FLOWS, end) + post.get(FLOWS + 5, end - 1) + post.get(FLOWS + 5, end)
    surface = surface + axial_shift(post.get(FLOWS + 1, end), 1, FLOWS + 1, end, radial, behind, ahead)
    surface = surface + axial_shift(post.get(FLOWS + 2, end), -1, FLOWS + 2, end, radial, behind, ahead)
    rising = post.get(FLOWS + 3, end)
    falling = post.get(FLOWS + 4, end)
    surface = surface + jnp.where(row == 0, 0.0, pltpu.roll(rising, 1, 0))
    surface = surface + jnp.where(row == across - 1, 0.0, pltpu.roll(falling, across - 1, 0))
    values = code_list(surface) + [rising[across - 1:across, :], falling[0:1, :]]
    codes = code_list(code_ref[...]) + [edges_ref[0:1, :], edges_ref[1:2, :]]
    sums = scatter_rows(values, codes, sectors * across, along)
    top = top_ref[...]
    for rel in range(sectors):
        outs[rel][0:across] = sums[rel * across:(rel + 1) * across]
        outs[rel][across:2 * across] = top
    start = 2 * across
    for out, places, side in ((outs[1], SECTOR_RISING, across - 1), (outs[sectors - 1], SECTOR_FALLING, 0)):
        for place, member in enumerate(places):
            step = VELOCITIES[member][0]
            base = start + place * radial
            if step:
                for level in range(radial):
                    value = axial_shift(post.get(member, level), step, member, level, radial, behind, ahead)
                    out[base + level:base + level + 1, :] = value[side:side + 1, :]
            else:
                out[base:base + radial, :] = post.rows(member, 0, radial, side)


def last_send_kernel(radial, across, post_ref, inner_ref, outer_ref, up_ref, down_ref):
    post = Planes(post_ref, radial, across)
    behind, ahead = axial_rims(inner_ref, outer_ref)
    for out, drug, plus, minus, side in ((up_ref, FLOWS + 3, 7, 10, across - 1), (down_ref, FLOWS + 4, 9, 8, 0)):
        out[0:radial, :] = post.rows(drug, 0, radial, side)
        for level in range(radial):
            value = axial_shift(post.get(plus, level), 1, plus, level, radial, behind, ahead)
            value = value - axial_shift(post.get(minus, level), -1, minus, level, radial, behind, ahead)
            out[radial + level:radial + level + 1, :] = value[side:side + 1, :]


def fields_kernel(radial, across, post_ref, inner_ref, outer_ref, drug_ref, flow_ref):
    post = Planes(post_ref, radial, across)
    behind, ahead = axial_rims(inner_ref, outer_ref)
    for level in range(radial):
        def member_of(member):
            value = streamed(post, member, level, behind, ahead)
            step = VELOCITIES[member][1]
            if step:
                edge = 0 if step > 0 else across - 1
                value = jnp.where(sublanes(value.shape) == edge, 0.0, value)
            return value

        drug = member_of(FLOWS)
        for member in range(FLOWS + 1, MEMBERS):
            drug = drug + member_of(member)
        drug_ref[level] = drug
        flow = None
        for member in range(FLOWS):
            factor = VELOCITIES[member][0]
            if factor:
                value = member_of(member)
                flow = (value if factor > 0 else -value) if flow is None else (flow + value if factor > 0 else flow - value)
        flow_ref[level] = flow


def last_kernel(drug_part, flow_part, below, above, drug_ref, flow_ref):
    radial, across, along = drug_ref.shape
    row = sublanes((across, along))
    for part, out, base in ((drug_part, drug_ref, 0), (flow_part, flow_ref, radial)):
        for level in range(radial):
            place = base + level
            value = part[level] + jnp.where(row == 0, below[place:place + 1, :], 0.0)
            out[level] = value + jnp.where(row == across - 1, above[place:place + 1, :], 0.0)


def kernel_call(body, outs, count, micros, aliases=None):
    shapes = [out if isinstance(out, jax.ShapeDtypeStruct) else jax.ShapeDtypeStruct(out, F32) for out in outs]
    return pl.pallas_call(
        body,
        out_shape=shapes,
        in_specs=[pl.BlockSpec(memory_space=VMEM)] * count,
        out_specs=[pl.BlockSpec(memory_space=VMEM)] * len(outs),
        input_output_aliases=aliases or {},
        cost_estimate=pl.CostEstimate(flops=0, bytes_accessed=int(micros * 3.0e6), transcendentals=0),
        compiler_params=pltpu.CompilerParams(vmem_limit_bytes=24 * 1024 * 1024),
    )


def first_call(sectors, populations, sector, line, strut, free):
    members, _, across, along = populations.shape
    plane = (across, along)
    sizes = [((5 if hop in (1, sectors - 1) else 4) * across, along) for hop in range(sectors)]
    return pl.pallas_call(
        functools.partial(first_kernel, sectors),
        name="first",
        out_shape=[jax.ShapeDtypeStruct(plane, jnp.int32)] + [jax.ShapeDtypeStruct(size, F32) for size in sizes],
        in_specs=[pl.BlockSpec(memory_space=pltpu.HBM)] * 5,
        out_specs=[pl.BlockSpec(memory_space=VMEM)] * (1 + sectors),
        scratch_shapes=[
            VMEM((members - FLOWS, across, along), F32),
            VMEM(plane, jnp.int32),
            VMEM(plane, jnp.int32),
            VMEM(plane, jnp.int32),
            VMEM((across, free.shape[1]), F32),
            pltpu.SemaphoreType.DMA((5,)),
        ],
    )(populations, sector, line, strut, free)


def per_device(populations, wall_free, wall_bound, wall_propagator, bind_on, bind_off, iface_sector, iface_line, strut_mask):
    members, radial, across, along = populations.shape
    sectors = lax.axis_size("th")
    plane = (across, along)
    flat = (members * radial * across, along)
    rims = len(SECTOR_RISING) * radial
    strut = strut_mask.reshape(plane)
    rate_on = bind_on.reshape(1, -1)
    rate_off = bind_off.reshape(1, -1)

    def exchange(boxes):
        inbox = [boxes[0]] + [None] * (sectors - 1)
        for hop in range(1, sectors):
            inbox[sectors - hop] = shifted(boxes[hop], "th", hop)
        return inbox

    codes, *boxes = first_call(sectors, populations, iface_sector.reshape(plane), iface_line.reshape(plane), strut, wall_free)
    inbox = exchange(boxes)
    state = populations.reshape(flat)
    speeds = (3 * across, along)
    bulk, speed = kernel_call(functools.partial(bulk_kernel, True, radial, across), [flat, speeds], 1, 1.5)(state)
    free, bound = wall_free, wall_bound
    openness = counts = edges = None
    for step in range(STEPS):
        first, last = step == 0, step == STEPS - 1
        outs = [flat, plane, plane]
        if first:
            outs = outs + [plane, plane, jax.ShapeDtypeStruct(plane, jnp.int32)]
        extra = [] if first else [openness]
        results = kernel_call(
            functools.partial(flux_kernel, sectors, first, radial), outs, 4 + sectors + len(extra), 0.8, {1: 0}
        )(state, bulk, speed, codes, *inbox, *extra)
        post = results[0]
        if first:
            openness, counts, edges = results[3:]
        inner, outer = paired(*results[1:3])
        free, bound, top = kernel_call(
            functools.partial(wall_kernel, sectors), [wall_free.shape, wall_free.shape, plane], 7 + sectors, 1.3
        )(free, bound, wall_propagator, rate_on, rate_off, strut, counts, *inbox)
        if last:
            continue
        sizes = [(2 * across + (rims if hop in (1, sectors - 1) else 0), along) for hop in range(sectors)]
        boxes = kernel_call(functools.partial(send_kernel, sectors, radial), sizes, 6, 0.3)(
            post, inner, outer, codes, edges, top
        )
        inbox = exchange(boxes)
        state, bulk, speed = kernel_call(
            functools.partial(bulk_kernel, False, radial, across), [flat, flat, speeds], 3, 2.0
        )(post, inner, outer)
    up, down = kernel_call(
        functools.partial(last_send_kernel, radial, across), [(2 * radial, along)] * 2, 3, 0.2
    )(post, inner, outer)
    below = shifted(up, "th", 1)
    above = shifted(down, "th", -1)
    parts = kernel_call(
        functools.partial(fields_kernel, radial, across), [(radial,) + plane] * 2, 3, 1.0
    )(post, inner, outer)
    drug_field, axial_flow = kernel_call(last_kernel, [(radial,) + plane] * 2, 4, 0.3)(*parts, below, above)
    return drug_field, axial_flow, free, bound


def solution(mesh):
    placed = (
        P(None, None, "th", "ax"),
        P(None, ("ax", "th")),
        P(None, ("ax", "th")),
        P(),
        P(),
        P(),
        P(("ax", "th"), None),
        P(("ax", "th")),
        P(("ax", "th")),
    )
    return jax.shard_map(
        per_device,
        mesh=mesh,
        in_specs=placed,
        out_specs=(
            P(None, "th", "ax"),
            P(None, "th", "ax"),
            P(None, ("ax", "th")),
            P(None, ("ax", "th")),
        ),
        check_vma=False,
    )
```

```python
import functools

import jax
import jax.numpy as jnp
from jax import lax
from jax.experimental import pallas as pl
from jax.experimental.pallas import tpu as pltpu
from jax.sharding import PartitionSpec as P


STEPS = 4
SUB = 2

VELOCITIES = [
    (0, 0, 0), (1, 0, 0), (-1, 0, 0), (0, 1, 0), (0, -1, 0), (0, 0, 1), (0, 0, -1),
    (1, 1, 0), (-1, -1, 0), (1, -1, 0), (-1, 1, 0),
    (1, 0, 1), (-1, 0, -1), (1, 0, -1), (-1, 0, 1),
    (0, 1, 1), (0, -1, -1), (0, 1, -1), (0, -1, 1),
    (0, 0, 0), (1, 0, 0), (-1, 0, 0), (0, 1, 0), (0, -1, 0), (0, 0, 1), (0, 0, -1),
]
WEIGHTS = [1.0 / 3.0] + [1.0 / 18.0] * 6 + [1.0 / 36.0] * 12 + [0.25] + [0.125] * 6
OPPOSITE = [0, 2, 1, 4, 3, 6, 5, 8, 7, 10, 9, 12, 11, 14, 13, 16, 15, 18, 17, 19, 21, 20, 23, 22, 25, 24]
MIRROR = [0, 1, 2, 3, 4, 6, 5, 7, 8, 9, 10, 13, 14, 11, 12, 17, 18, 15, 16, 19, 20, 21, 22, 23, 25, 24]
SECTOR_RISING = [3, 7, 10, 15, 17, 22]
SECTOR_FALLING = [4, 8, 9, 16, 18, 23]
SLAB_RISING = [1, 7, 9, 11, 13, 20]
SLAB_FALLING = [2, 8, 10, 12, 14, 21]
LEVEL_KEPT = [0, 3, 4, 5, 6, 15, 16, 17, 18, 19, 22, 23, 24, 25]
RISE_SLOTS = [(m, 0) for m in SLAB_RISING] + [(m, 0) for m in LEVEL_KEPT] + [(m, 1) for m in SLAB_RISING] + [(14, 0)]
FALL_SLOTS = [(m, 0) for m in SLAB_FALLING] + [(m, 0) for m in LEVEL_KEPT] + [(m, 1) for m in SLAB_FALLING] + [(11, 0)]
PAIRS = [(1, 2), (3, 4), (5, 6), (7, 8), (9, 10), (11, 12), (13, 14), (15, 16), (17, 18)]
FLOWS = 19
MEMBERS = 26
RELAX_FLOW = 1.25
RELAX_DRUG = 1.1
PUSH_AXIAL = 0.0001
PERMEABILITY = 0.3
RELEASE_RATE = 0.5

F32 = jnp.float32
BF16 = jnp.bfloat16
VMEM = pltpu.VMEM


def shifted(block, axis, distance):
    count = lax.axis_size(axis)
    return lax.ppermute(block, axis, [((i - distance) % count, i) for i in range(count)])


def paired(inner, outer):
    count = lax.axis_size("ax")
    near = [(i, i ^ 1) for i in range(count)]
    far = [(i, (i + 1) % count if i % 2 else (i - 1) % count) for i in range(count)]
    return lax.ppermute(inner, "ax", near), lax.ppermute(outer, "ax", far)


def by_parity(even, odd):
    return jnp.where(lax.axis_index("ax") % 2 == 0, even, odd)


def axial_rims(packed, first_ref, second_ref, across):
    first, second = first_ref[0:across, :], second_ref[0:across, :]
    if not packed:
        return first, second
    return by_parity(second, first), by_parity(first, second)


def lanes(shape):
    return lax.broadcasted_iota(jnp.int32, shape, len(shape) - 1)


def sublanes(shape):
    return lax.broadcasted_iota(jnp.int32, shape, len(shape) - 2)


def split3(value):
    high = value.astype(BF16)
    rest = value - high.astype(F32)
    middle = rest.astype(BF16)
    low = (rest - middle.astype(F32)).astype(BF16)
    return high, middle, low


def one_hot_lines(low_row, width):
    shape = (width, low_row.shape[-1])
    return jnp.where(sublanes(shape) == low_row, 1.0, 0.0).astype(BF16)


def scatter_rows(value_rows, code_rows, groups, width):
    terms, hots = [], []
    for value, code in zip(value_rows, code_rows, strict=True):
        group = code // width
        shape = (groups, value.shape[-1])
        hit = sublanes(shape) == group
        terms.append(jnp.concatenate([jnp.where(hit, part.astype(F32), 0.0) for part in split3(value)], axis=0).astype(BF16))
        hots.append(one_hot_lines(code - group * width, width))
    left = jnp.concatenate(terms, axis=1)
    right = jnp.concatenate(hots, axis=1)
    total = lax.dot_general(left, right, (((1,), (1,)), ((), ())), preferred_element_type=F32)
    return total[:groups] + total[groups:2 * groups] + total[2 * groups:3 * groups]


def gather_rows(table, code_rows, width):
    groups = table.shape[0]
    left = jnp.concatenate(split3(table), axis=0)
    lows = [code - (code // width) * width for code in code_rows]
    right = jnp.concatenate([one_hot_lines(low, width) for low in lows], axis=1)
    picked = jnp.dot(left, right, preferred_element_type=F32)
    picked = picked[:groups] + picked[groups:2 * groups] + picked[2 * groups:3 * groups]
    results, start = [], 0
    for code in code_rows:
        count = code.shape[-1]
        hit = sublanes((groups, count)) == code // width
        results.append(jnp.sum(jnp.where(hit, picked[:, start:start + count], 0.0), axis=0, keepdims=True))
        start += count
    return results


def source_plane(member, level, radial):
    step_r = VELOCITIES[member][2]
    if step_r == 1:
        return ((MIRROR[member], 0) if level == 0 else (member, level - 1)), True
    if step_r == -1:
        return ((OPPOSITE[member], radial - 1), False) if level == radial - 1 else ((member, level + 1), True)
    return (member, level), True


class Planes:
    def __init__(self, ref, radial, across):
        self.ref, self.radial, self.across = ref, radial, across

    def base(self, member, level):
        return (member * self.radial + level) * self.across

    def get(self, member, level):
        return self.ref[pl.ds(self.base(member, level), self.across), :]

    def put(self, member, level, value):
        self.ref[pl.ds(self.base(member, level), self.across), :] = value

    def rows(self, member, level, count, row):
        return self.ref[pl.ds(self.base(member, level) + row, count, stride=self.across), :]

    def put_rows(self, member, level, count, row, value):
        self.ref[pl.ds(self.base(member, level) + row, count, stride=self.across), :] = value


def axial_shift(value, step, member, level, radial, behind, ahead):
    along = value.shape[-1]
    lane = lanes(value.shape)
    if step == 1:
        slot = SLAB_RISING.index(member) * radial + level
        return jnp.where(lane == 0, pltpu.roll(behind, (-slot) % along, 1), pltpu.roll(value, 1, 1))
    slot = SLAB_FALLING.index(member) * radial + level
    return jnp.where(lane == along - 1, pltpu.roll(ahead, (along - 1 - slot) % along, 1), pltpu.roll(value, along - 1, 1))


def streamed(post, member, level, behind, ahead):
    radial, across = post.radial, post.across
    (origin, depth), moves = source_plane(member, level, radial)
    value = post.get(origin, depth)
    if not moves:
        return value
    step_z, step_s, _ = VELOCITIES[member]
    if step_z:
        value = axial_shift(value, step_z, origin, depth, radial, behind, ahead)
    if step_s:
        value = pltpu.roll(value, step_s % across, 0)
    return value


def incoming_rows(box, start, places, state, member, level, count, row):
    radial = state.radial
    step_r = VELOCITIES[member][2]
    here = start + places.index(member) * radial + level
    value = box[here - step_r:here - step_r + count, :]
    if step_r == 1 and level == 0:
        mirrored = start + places.index(MIRROR[member]) * radial
        value = jnp.where(sublanes(value.shape) == 0, box[mirrored:mirrored + 1, :], value)
    if step_r == -1 and level + count == radial:
        value = jnp.where(sublanes(value.shape) == count - 1, state.rows(member, level, count, row), value)
    return value


def relax_flow(members):
    def total(component):
        up, down = None, None
        for member in range(1, FLOWS):
            factor = VELOCITIES[member][component]
            if factor > 0:
                up = members[member] if up is None else up + members[member]
            elif factor < 0:
                down = members[member] if down is None else down + members[member]
        return up - down

    density = members[0]
    for member in range(1, FLOWS):
        density = density + members[member]
    inverse = 1.0 / density
    velocity = [(total(0) + PUSH_AXIAL) * inverse, total(1) * inverse, total(2) * inverse]
    speed_sq = velocity[0] * velocity[0] + velocity[1] * velocity[1] + velocity[2] * velocity[2]
    base = 1.0 - 1.5 * speed_sq
    weighted = {}
    for weight in sorted(set(WEIGHTS[:FLOWS])):
        weighted[weight] = (RELAX_FLOW * weight) * density

    def projected(member):
        result = None
        for component in range(3):
            factor = VELOCITIES[member][component]
            if factor == 0:
                continue
            if result is None:
                result = velocity[component] if factor > 0 else -velocity[component]
            else:
                result = result + velocity[component] if factor > 0 else result - velocity[component]
        return result

    results = [None] * FLOWS
    results[0] = (1.0 - RELAX_FLOW) * members[0] + weighted[WEIGHTS[0]] * base
    for first, second in PAIRS:
        along = projected(first)
        even = weighted[WEIGHTS[first]] * (base + 4.5 * along * along)
        odd = weighted[WEIGHTS[first]] * (3.0 * along)
        results[first] = (1.0 - RELAX_FLOW) * members[first] + (even + odd)
        results[second] = (1.0 - RELAX_FLOW) * members[second] + (even - odd)
    return results, velocity


def relax_drug(members, velocity):
    concentration = members[0]
    for member in members[1:]:
        concentration = concentration + member
    rest = (RELAX_DRUG * WEIGHTS[FLOWS]) * concentration
    results = [(1.0 - RELAX_DRUG) * members[0] + rest]
    even = (RELAX_DRUG * WEIGHTS[FLOWS + 1]) * concentration
    for component in range(3):
        odd = even * (4.0 * velocity[component])
        results.append((1.0 - RELAX_DRUG) * members[1 + 2 * component] + (even + odd))
        results.append((1.0 - RELAX_DRUG) * members[2 + 2 * component] + (even - odd))
    return results


def code_list(codes):
    return [codes[row:row + 1, :] for row in range(codes.shape[0])]


def pack_lines(row, width):
    return jnp.concatenate([row[:, start:start + width] for start in range(0, row.shape[-1], width)], axis=0)


def first_kernel(sectors, pops_ref, sector_ref, line_ref, strut_ref, free_ref, *refs):
    code_ref, boxes = refs[0], refs[1:1 + sectors]
    drug, sector, line, strut, top, sems = refs[1 + sectors:]
    across, width = code_ref.shape
    count = drug.shape[0]
    radial = pops_ref.shape[1]
    copies = [
        pltpu.make_async_copy(pops_ref.at[FLOWS:FLOWS + count, radial - 1], drug, sems.at[0]),
        pltpu.make_async_copy(sector_ref, sector, sems.at[1]),
        pltpu.make_async_copy(line_ref, line, sems.at[2]),
        pltpu.make_async_copy(strut_ref, strut, sems.at[3]),
        pltpu.make_async_copy(free_ref.at[0:across, :], top, sems.at[4]),
    ]
    for copy in copies:
        copy.start()
    for copy in copies:
        copy.wait()
    relative = sector[...] - lax.axis_index("th")
    relative = jnp.where(relative < 0, relative + sectors, relative)
    codes = relative * (across * width) + line[...]
    code_ref[...] = codes
    surface = drug[0]
    for member in range(1, count):
        surface = surface + drug[member]
    rows = code_list(codes)
    groups = sectors * across
    sums = scatter_rows(code_list(surface), rows, groups, width)
    counts = scatter_rows(code_list(jnp.ones_like(surface)), rows, groups, width)
    first = pack_lines(top[0:1, :], width)
    openness = PERMEABILITY * (1.0 - strut[...].astype(F32))
    for rel in range(sectors):
        out = boxes[rel]
        out[0:across] = sums[rel * across:(rel + 1) * across]
        out[across:2 * across] = counts[rel * across:(rel + 1) * across]
        out[2 * across:3 * across] = first
        out[3 * across:4 * across] = openness
        if rel in (1, sectors - 1):
            edge = codes[across - 1:across] if rel == 1 else codes[0:1]
            out[4 * across:5 * across] = jnp.broadcast_to(edge, (across, width)).astype(F32)


def bulk_kernel(first, packed, radial, across, *refs):
    if first:
        state_ref, post_ref, speed_ref = refs
    else:
        old_ref, inner_ref, outer_ref, state_ref, post_ref, speed_ref = refs
        old = Planes(old_ref, radial, across)
        behind, ahead = axial_rims(packed, inner_ref, outer_ref, across)
    state, post = Planes(state_ref, radial, across), Planes(post_ref, radial, across)
    for level in range(radial):
        if first:
            members = [state.get(member, level) for member in range(MEMBERS)]
        else:
            members = [streamed(old, member, level, behind, ahead) for member in range(MEMBERS)]
            for member in range(MEMBERS):
                state.put(member, level, members[member])
        results, velocity = relax_flow(members[:FLOWS])
        if level == radial - 1:
            for component in range(3):
                speed_ref[component * across:(component + 1) * across, :] = velocity[component]
        else:
            results = results + relax_drug(members[FLOWS:], velocity)
        for member, value in enumerate(results):
            post.put(member, level, value)


def rim_tiles(post, slots, rising):
    radial, across = post.radial, post.across
    along = post.ref.shape[-1]
    each = along // radial
    lane = lanes((across, along))
    tiles = []
    for place, (member, column) in enumerate(slots):
        if place % each == 0:
            tiles.append(jnp.zeros((across, along), F32))
        origin = along - 1 - column if rising else column
        only_last = place == len(slots) - 1
        for level in range(radial - 1 if only_last else 0, radial):
            slot = (place % each) * radial + level
            value = pltpu.roll(post.get(member, level), (slot - origin) % along, 1)
            tiles[-1] = jnp.where(lane == slot, value, tiles[-1])
    return tiles


class Ghosts:
    def __init__(self, radial, across, along, behind, ahead, rise, fall):
        self.radial, self.across, self.along = radial, across, along
        self.behind, self.ahead, self.rise, self.fall = behind, ahead, rise, fall
        lane = lanes((across, along))
        self.is_behind = lane < radial
        self.level = jnp.where(self.is_behind, lane, lane - radial)

    def pick(self, message, slot, target):
        each = self.along // self.radial
        tile = message[(slot // each) * self.across:(slot // each + 1) * self.across, :]
        return pltpu.roll(tile, (target - (slot % each) * self.radial) % self.along, 1)

    def join(self, first, second):
        return jnp.where(self.is_behind, self.pick(*first, 0), self.pick(*second, self.radial))

    def arriving(self, member):
        step = VELOCITIES[member][0]
        rise, fall = RISE_SLOTS.index, FALL_SLOTS.index
        if step == 1:
            return self.join((self.behind, rise((member, 1))), (self.rise, rise((member, 0))))
        if step == -1:
            return self.join((self.fall, fall((member, 0))), (self.ahead, fall((member, 1))))
        return self.join((self.behind, rise((member, 0))), (self.ahead, fall((member, 0))))

    def own(self, member):
        return self.join((self.behind, RISE_SLOTS.index((member, 0))), (self.ahead, FALL_SLOTS.index((member, 0))))

    def risen(self, member):
        value = self.arriving(member)
        step = VELOCITIES[member][2]
        if step == 1:
            return jnp.where(self.level == 0, self.arriving(MIRROR[member]), pltpu.roll(value, 1, 1))
        if step == -1:
            return pltpu.roll(value, self.along - 1, 1)
        return value

    def streamed(self, member, below_rows, above_rows):
        value = self.risen(member)
        row = sublanes(value.shape)
        step = VELOCITIES[member][1]
        if step == 1:
            place = SECTOR_RISING.index(member)
            value = jnp.where(row == 0, below_rows[place:place + 1, :], pltpu.roll(value, 1, 0))
        elif step == -1:
            place = SECTOR_FALLING.index(member)
            value = jnp.where(row == self.across - 1, above_rows[place:place + 1, :], pltpu.roll(value, self.across - 1, 0))
        if VELOCITIES[member][2] == -1:
            value = jnp.where(self.level == self.radial - 1, self.own(OPPOSITE[member]), value)
        return value


def gather_cells(table, codes, width):
    group = codes // width
    low = codes - group * width
    row = jnp.zeros(codes.shape, F32)
    for place in range(table.shape[0]):
        row = jnp.where(group == place, table[place:place + 1, :], row)
    return jnp.sum(jnp.where(lanes(codes.shape) == low, row, 0.0), axis=1, keepdims=True)


def table_of(inbox, start, across):
    return jnp.concatenate([box[start:start + across, :] for box in inbox], axis=0)


def flux_kernel(sectors, step, radial, *refs):
    first, odd = step == 0, step % 2 == 1
    refs = list(refs)
    state_ref, bulk_ref, speed_ref, code_ref, strut_ref, coef_ref, on_ref, off_ref = refs[:8]
    inbox = refs[8:8 + sectors]
    refs = refs[8 + sectors:]
    open_ref = counts_ref = ghost_code_ref = ghost_open_ref = None
    if not first:
        open_ref, counts_ref = refs[:2]
        refs = refs[2:]
    if odd:
        sent_refs, got_refs = refs[:2], refs[2:4]
        refs = refs[4:]
        if step > 1:
            ghost_code_ref, ghost_open_ref = refs[:2]
            refs = refs[2:]
    post_ref, one_ref, two_ref, added_ref, top_ref = refs[:5]
    refs = refs[5:]
    del bulk_ref
    across, along = code_ref.shape
    plane = (across, along)
    end = radial - 1
    state, post = Planes(state_ref, radial, across), Planes(post_ref, radial, across)
    codes = code_list(code_ref[...])
    below, above = inbox[sectors - 1], inbox[1]
    base = 2 * across if first else across
    picked = jnp.concatenate(gather_rows(table_of(inbox, base, across), codes, along), axis=0)
    if first:
        openness = jnp.concatenate(gather_rows(table_of(inbox, 3 * across, across), codes, along), axis=0)
        counts = inbox[0][across:2 * across, :]
        for box in inbox[1:]:
            counts = counts + box[across:2 * across, :]
        refs[0][...] = openness
        refs[1][...] = counts
        count, limit = across * along, sectors * across * along
        up = above[4 * across:5 * across, :].astype(jnp.int32) + count
        down = below[4 * across:5 * across, :].astype(jnp.int32) - count
        up = jnp.where(up >= limit, up - limit, up)
        down = jnp.where(down < 0, down + limit, down)
        refs[2][...] = jnp.where(sublanes(plane) == 0, up, down)
    else:
        openness, counts = open_ref[...], counts_ref[...]
    total = inbox[0][0:across, :]
    for box in inbox[1:]:
        total = total + box[0:across, :]
    strut = strut_ref[...].astype(F32)
    shut = PERMEABILITY * (1.0 - strut)
    added = shut * (total - counts * inbox[0][base:base + across, :]) + RELEASE_RATE * strut
    added_ref[...] = added
    free = coef_ref[0:across, :] + added * coef_ref[across:2 * across, :]
    bound = coef_ref[2 * across:3 * across, :] + added * coef_ref[3 * across:4 * across, :]
    top = free - (on_ref[0:1, 0:1] * free * (1.0 - bound) - off_ref[0:1, 0:1] * bound)
    top_ref[...] = top
    start = rims_start(step, across)
    row = sublanes(plane)
    drugs = [state.get(member, end) for member in range(FLOWS, MEMBERS)]
    if not first:
        last = start + SECTOR_RISING.index(FLOWS + 3) * radial + end
        drugs[3] = jnp.where(row == 0, below[last:last + 1, :], drugs[3])
        last = start + SECTOR_FALLING.index(FLOWS + 4) * radial + end
        drugs[4] = jnp.where(row == across - 1, above[last:last + 1, :], drugs[4])
    surface = drugs[0]
    for drug in drugs[1:]:
        surface = surface + drug
    flux = openness * (surface - picked)
    drugs = [drug - WEIGHTS[FLOWS + place] * flux for place, drug in enumerate(drugs)]
    velocity = [speed_ref[component * across:(component + 1) * across, :] for component in range(3)]
    for place, value in enumerate(relax_drug(drugs, velocity)):
        post.put(FLOWS + place, end, value)
    if not first:
        block = across
        for side, box, places in ((0, below, SECTOR_RISING), (across - 1, above, SECTOR_FALLING)):
            moving = 1 if side == 0 else -1
            for level in range(0, radial, block):
                members = []
                for member in range(MEMBERS):
                    if VELOCITIES[member][1] == moving:
                        value = incoming_rows(box, start, places, state, member, level, block, side)
                    else:
                        value = state.rows(member, level, block, side)
                    if member >= FLOWS and level + block == radial:
                        lowered = value - WEIGHTS[member] * flux[side:side + 1, :]
                        value = jnp.where(sublanes(value.shape) == block - 1, lowered, value)
                    members.append(value)
                results, velocity = relax_flow(members[:FLOWS])
                results = results + relax_drug(members[FLOWS:], velocity)
                for member, value in enumerate(results):
                    post.put_rows(member, level, block, side, value)
    if not odd:
        rise = rim_tiles(post, RISE_SLOTS, True) + [top]
        fall = rim_tiles(post, FALL_SLOTS, False) + [top]
        if first:
            own = code_ref[...].astype(F32)
            rise = rise + [shut, pltpu.roll(own, 1, 1)]
            fall = fall + [shut, own]
        for place, (up, down) in enumerate(zip(rise, fall, strict=True)):
            one_ref[place * across:(place + 1) * across, :] = by_parity(up, down)
            two_ref[place * across:(place + 1) * across, :] = by_parity(down, up)
        return
    rise, fall = by_parity(sent_refs[0][...], sent_refs[1][...]), by_parity(sent_refs[1][...], sent_refs[0][...])
    behind, ahead = by_parity(got_refs[1][...], got_refs[0][...]), by_parity(got_refs[0][...], got_refs[1][...])
    ghosts = Ghosts(radial, across, along, behind, ahead, rise, fall)
    tables = [table_of(inbox, (2 + side) * across, across) for side in range(2)]
    if step == 1:
        place = code_place(radial, across, along)
        sides = [message[place:place + across, 0:1].astype(jnp.int32) for message in (behind, ahead)]
        sides = [jnp.broadcast_to(side, plane) for side in sides]
        opens = [gather_cells(table_of(inbox, (4 + side) * across, across), sides[side], along) for side in range(2)]
        for side in range(2):
            refs[0][side * across:(side + 1) * across, :] = sides[side]
            refs[1][side * across:(side + 1) * across, :] = jnp.broadcast_to(opens[side], plane)
    else:
        sides = [ghost_code_ref[side * across:(side + 1) * across, :] for side in range(2)]
        opens = [ghost_open_ref[side * across:(side + 1) * across, 0:1] for side in range(2)]
    tops = [gather_cells(tables[side], sides[side], along) for side in range(2)]
    ghost_start = start + len(SECTOR_RISING) * radial
    below_rows = below[ghost_start:ghost_start + across, :]
    above_rows = above[ghost_start:ghost_start + across, :]
    members = [ghosts.streamed(member, below_rows, above_rows) for member in range(MEMBERS)]
    surface = members[FLOWS]
    for member in range(FLOWS + 1, MEMBERS):
        surface = surface + members[member]
    ghost_flux = jnp.where(ghosts.is_behind, opens[0] * (surface - tops[0]), opens[1] * (surface - tops[1]))
    ghost_flux = jnp.where(ghosts.level == end, ghost_flux, 0.0)
    members = members[:FLOWS] + [members[member] - WEIGHTS[member] * ghost_flux for member in range(FLOWS, MEMBERS)]
    results, velocity = relax_flow(members[:FLOWS])
    results = results + relax_drug(members[FLOWS:], velocity)
    lane = lanes(plane)
    behind, ahead = jnp.zeros(plane, F32), jnp.zeros(plane, F32)
    for place in range(len(SLAB_RISING)):
        here = (lane >= place * radial) & (lane < (place + 1) * radial)
        behind = jnp.where(here, pltpu.roll(results[SLAB_RISING[place]], (place * radial) % along, 1), behind)
        ahead = jnp.where(here, pltpu.roll(results[SLAB_FALLING[place]], ((place - 1) * radial) % along, 1), ahead)
    one_ref[...] = behind
    two_ref[...] = ahead


def code_place(radial, across, along):
    return (rim_rows(radial, across, along) // across + 2) * across


def rim_rows(radial, across, along):
    return -(-len(RISE_SLOTS) // (along // radial)) * across


def rims_start(step, across):
    return (6 if step == 1 else 4 if step % 2 else 2) * across


def wall_rates(spread_ref, on_ref, off_ref):
    depth = spread_ref.shape[0]
    shape = (depth, depth)
    rate_on = jnp.transpose(jnp.broadcast_to(on_ref[...], shape))
    rate_off = jnp.transpose(jnp.broadcast_to(off_ref[...], shape))
    entry = jnp.broadcast_to(spread_ref[:, 0:1], shape)
    top = jnp.transpose(jnp.broadcast_to(spread_ref[0:1, :], shape))
    return rate_on, rate_off, entry, top


def plan_ahead(spread, rates, free, bound):
    rate_on, rate_off, entry, top = rates
    moved = jnp.dot(spread, free, precision=lax.Precision.HIGHEST, preferred_element_type=F32)
    rate = rate_on * moved * (1.0 - bound) - rate_off * bound
    gain = rate_on * entry * (1.0 - bound)
    first = jnp.sum(top * (moved - rate), axis=0, keepdims=True)
    slope = jnp.sum(top * (entry - gain), axis=0, keepdims=True)
    return moved, (first, slope, bound[0:1, :] + rate[0:1, :], gain[0:1, :])


def plan_kernel(free_ref, bound_ref, spread_ref, on_ref, off_ref, moved_ref, coef_ref):
    rates = wall_rates(spread_ref, on_ref, off_ref)
    width = coef_ref.shape[1]
    across = coef_ref.shape[0] // 4
    for row in range(across):
        place = slice(row * width, (row + 1) * width)
        moved, parts = plan_ahead(spread_ref[...], rates, free_ref[:, place], bound_ref[:, place])
        moved_ref[:, place] = moved
        for index, part in enumerate(parts):
            coef_ref[index * across + row:index * across + row + 1, :] = part


def wall_kernel(last, moved_ref, bound_ref, added_ref, spread_ref, on_ref, off_ref, *outs):
    rates = wall_rates(spread_ref, on_ref, off_ref)
    rate_on, rate_off, entry, _ = rates
    across, width = added_ref.shape
    spread = spread_ref[...]
    for row in range(across):
        place = slice(row * width, (row + 1) * width)
        free = moved_ref[:, place] + entry * added_ref[row:row + 1, :]
        bound = bound_ref[:, place]
        for substep in range(SUB):
            if substep:
                free = jnp.dot(spread, free, precision=lax.Precision.HIGHEST, preferred_element_type=F32)
            rate = rate_on * free * (1.0 - bound) - rate_off * bound
            free = free - rate
            bound = bound + rate
        outs[1][:, place] = bound
        if last:
            outs[0][:, place] = free
        else:
            moved, parts = plan_ahead(spread, rates, free, bound)
            outs[0][:, place] = moved
            for index, part in enumerate(parts):
                outs[2][index * across + row:index * across + row + 1, :] = part


def send_kernel(sectors, step, radial, *refs):
    packed = step % 2 == 0
    post_ref, one_ref, two_ref, code_ref, edges_ref, top_ref = refs[:6]
    refs = refs[6:]
    if packed:
        sent_refs, outs = refs[:2], refs[2:]
    else:
        outs = refs
    across, along = code_ref.shape
    post = Planes(post_ref, radial, across)
    behind, ahead = axial_rims(packed, one_ref, two_ref, across)
    end = radial - 1
    row = sublanes((across, along))
    surface = post.get(FLOWS, end) + post.get(FLOWS + 5, end - 1) + post.get(FLOWS + 5, end)
    surface = surface + axial_shift(post.get(FLOWS + 1, end), 1, FLOWS + 1, end, radial, behind, ahead)
    surface = surface + axial_shift(post.get(FLOWS + 2, end), -1, FLOWS + 2, end, radial, behind, ahead)
    rising = post.get(FLOWS + 3, end)
    falling = post.get(FLOWS + 4, end)
    surface = surface + jnp.where(row == 0, 0.0, pltpu.roll(rising, 1, 0))
    surface = surface + jnp.where(row == across - 1, 0.0, pltpu.roll(falling, across - 1, 0))
    values = code_list(surface) + [rising[across - 1:across, :], falling[0:1, :]]
    codes = code_list(code_ref[...]) + [edges_ref[0:1, :], edges_ref[1:2, :]]
    sums = scatter_rows(values, codes, sectors * across, along)
    parts = [top_ref[...]]
    if packed:
        whole_behind = by_parity(two_ref[...], one_ref[...])
        whole_ahead = by_parity(one_ref[...], two_ref[...])
        skip = rim_rows(radial, across, along)
        for index in range(2 if step == 0 else 1):
            place = skip + index * across
            parts = parts + [whole_behind[place:place + across, :], whole_ahead[place:place + across, :]]
    for rel in range(sectors):
        outs[rel][0:across] = sums[rel * across:(rel + 1) * across]
        for index, part in enumerate(parts):
            outs[rel][(1 + index) * across:(2 + index) * across] = part
    start = rims_start(step + 1, across)
    for out, places, side in ((outs[1], SECTOR_RISING, across - 1), (outs[sectors - 1], SECTOR_FALLING, 0)):
        for place, member in enumerate(places):
            moving = VELOCITIES[member][0]
            base = start + place * radial
            if moving:
                for level in range(radial):
                    value = axial_shift(post.get(member, level), moving, member, level, radial, behind, ahead)
                    out[base + level:base + level + 1, :] = value[side:side + 1, :]
            else:
                out[base:base + radial, :] = post.rows(member, 0, radial, side)
    if packed:
        rise, fall = by_parity(sent_refs[0][...], sent_refs[1][...]), by_parity(sent_refs[1][...], sent_refs[0][...])
        ghosts = Ghosts(radial, across, along, whole_behind, whole_ahead, rise, fall)
        base = start + len(SECTOR_RISING) * radial
        for out, places, side in ((outs[1], SECTOR_RISING, across - 1), (outs[sectors - 1], SECTOR_FALLING, 0)):
            for place, member in enumerate(places):
                out[base + place:base + place + 1, :] = ghosts.risen(member)[side:side + 1, :]
            for place in range(len(places), across):
                out[base + place:base + place + 1, :] = jnp.zeros((1, along), F32)


def last_send_kernel(radial, across, post_ref, inner_ref, outer_ref, up_ref, down_ref):
    post = Planes(post_ref, radial, across)
    behind, ahead = axial_rims(False, inner_ref, outer_ref, across)
    for out, drug, plus, minus, side in ((up_ref, FLOWS + 3, 7, 10, across - 1), (down_ref, FLOWS + 4, 9, 8, 0)):
        out[0:radial, :] = post.rows(drug, 0, radial, side)
        for level in range(radial):
            value = axial_shift(post.get(plus, level), 1, plus, level, radial, behind, ahead)
            value = value - axial_shift(post.get(minus, level), -1, minus, level, radial, behind, ahead)
            out[radial + level:radial + level + 1, :] = value[side:side + 1, :]


def fields_kernel(radial, across, post_ref, inner_ref, outer_ref, drug_ref, flow_ref):
    post = Planes(post_ref, radial, across)
    behind, ahead = axial_rims(False, inner_ref, outer_ref, across)
    for level in range(radial):
        def member_of(member):
            value = streamed(post, member, level, behind, ahead)
            step = VELOCITIES[member][1]
            if step:
                edge = 0 if step > 0 else across - 1
                value = jnp.where(sublanes(value.shape) == edge, 0.0, value)
            return value

        drug = member_of(FLOWS)
        for member in range(FLOWS + 1, MEMBERS):
            drug = drug + member_of(member)
        drug_ref[level] = drug
        flow = None
        for member in range(FLOWS):
            factor = VELOCITIES[member][0]
            if factor:
                value = member_of(member)
                flow = (value if factor > 0 else -value) if flow is None else (flow + value if factor > 0 else flow - value)
        flow_ref[level] = flow


def last_kernel(drug_part, flow_part, below, above, drug_ref, flow_ref):
    radial, across, along = drug_ref.shape
    row = sublanes((across, along))
    for part, out, base in ((drug_part, drug_ref, 0), (flow_part, flow_ref, radial)):
        for level in range(radial):
            place = base + level
            value = part[level] + jnp.where(row == 0, below[place:place + 1, :], 0.0)
            out[level] = value + jnp.where(row == across - 1, above[place:place + 1, :], 0.0)


def kernel_call(body, outs, count, micros, aliases=None):
    shapes = [out if isinstance(out, jax.ShapeDtypeStruct) else jax.ShapeDtypeStruct(out, F32) for out in outs]
    return pl.pallas_call(
        body,
        out_shape=shapes,
        in_specs=[pl.BlockSpec(memory_space=VMEM)] * count,
        out_specs=[pl.BlockSpec(memory_space=VMEM)] * len(outs),
        input_output_aliases=aliases or {},
        cost_estimate=pl.CostEstimate(flops=0, bytes_accessed=int(micros * 3.0e6), transcendentals=0),
        compiler_params=pltpu.CompilerParams(vmem_limit_bytes=24 * 1024 * 1024),
    )


def first_call(sectors, populations, sector, line, strut, free):
    members, _, across, along = populations.shape
    plane = (across, along)
    sizes = [((5 if hop in (1, sectors - 1) else 4) * across, along) for hop in range(sectors)]
    return pl.pallas_call(
        functools.partial(first_kernel, sectors),
        name="first",
        out_shape=[jax.ShapeDtypeStruct(plane, jnp.int32)] + [jax.ShapeDtypeStruct(size, F32) for size in sizes],
        in_specs=[pl.BlockSpec(memory_space=pltpu.HBM)] * 5,
        out_specs=[pl.BlockSpec(memory_space=VMEM)] * (1 + sectors),
        scratch_shapes=[
            VMEM((members - FLOWS, across, along), F32),
            VMEM(plane, jnp.int32),
            VMEM(plane, jnp.int32),
            VMEM(plane, jnp.int32),
            VMEM((across, free.shape[1]), F32),
            pltpu.SemaphoreType.DMA((5,)),
        ],
    )(populations, sector, line, strut, free)


def per_device(populations, wall_free, wall_bound, wall_propagator, bind_on, bind_off, iface_sector, iface_line, strut_mask):
    members, radial, across, along = populations.shape
    sectors = lax.axis_size("th")
    plane = (across, along)
    flat = (members * radial * across, along)
    rims = len(SECTOR_RISING) * radial
    strut = strut_mask.reshape(plane)
    rate_on = bind_on.reshape(1, -1)
    rate_off = bind_off.reshape(1, -1)

    def exchange(boxes):
        inbox = [boxes[0]] + [None] * (sectors - 1)
        for hop in range(1, sectors):
            inbox[sectors - hop] = shifted(boxes[hop], "th", hop)
        return inbox

    codes, *boxes = first_call(sectors, populations, iface_sector.reshape(plane), iface_line.reshape(plane), strut, wall_free)
    inbox = exchange(boxes)
    state = populations.reshape(flat)
    speeds = (3 * across, along)
    four = (4 * across, along)
    two = (2 * across, along)
    rim = rim_rows(radial, across, along)
    shapes = wall_free.shape
    bulk, speed = kernel_call(functools.partial(bulk_kernel, True, True, radial, across), [flat, speeds], 1, 1.5)(state)
    moved, coefs = kernel_call(plan_kernel, [shapes, four], 5, 1.0)(
        wall_free, wall_bound, wall_propagator, rate_on, rate_off
    )
    bound = wall_bound
    fixed, ghost = [], []
    edges = sent = got = None
    for step in range(STEPS):
        odd, last = step % 2 == 1, step == STEPS - 1
        if odd:
            pair = [plane, plane]
        else:
            pair = [(rim + (3 if step == 0 else 1) * across, along)] * 2
        outs = [flat] + pair + [plane, plane]
        if step == 0:
            outs = outs + [plane, plane, jax.ShapeDtypeStruct(plane, jnp.int32)]
        if step == 1:
            outs = outs + [jax.ShapeDtypeStruct(two, jnp.int32), two]
        extra = fixed + ([*sent, *got, *ghost] if odd else [])
        post, one, other, added, top, *rest = kernel_call(
            functools.partial(flux_kernel, sectors, step, radial), outs, 8 + sectors + len(extra), 0.8, {1: 0}
        )(state, bulk, speed, codes, strut, coefs, rate_on, rate_off, *inbox, *extra)
        if step == 0:
            fixed, edges = rest[:2], rest[2]
        if step == 1:
            ghost = rest
        if odd:
            rims_in, own = [one, other], []
        else:
            sent = [one, other]
            got = paired(*sent)
            rims_in, own = [*got], sent
        results = kernel_call(
            functools.partial(wall_kernel, last), [shapes, shapes] + ([] if last else [four]), 6, 1.5
        )(moved, bound, added, wall_propagator, rate_on, rate_off)
        if last:
            free, bound = results
            continue
        moved, bound, coefs = results
        start = rims_start(step + 1, across)
        long = start + rims + (0 if odd else across)
        sizes = [(long if hop in (1, sectors - 1) else start, along) for hop in range(sectors)]
        boxes = kernel_call(
            functools.partial(send_kernel, sectors, step, radial), sizes, 6 + len(own), 0.3
        )(post, *rims_in, codes, edges, top, *own)
        inbox = exchange(boxes)
        state, bulk, speed = kernel_call(
            functools.partial(bulk_kernel, False, not odd, radial, across), [flat, flat, speeds], 3, 2.0
        )(post, *rims_in)
    up, down = kernel_call(
        functools.partial(last_send_kernel, radial, across), [(2 * radial, along)] * 2, 3, 0.2
    )(post, *rims_in)
    below = shifted(up, "th", 1)
    above = shifted(down, "th", -1)
    parts = kernel_call(
        functools.partial(fields_kernel, radial, across), [(radial,) + plane] * 2, 3, 1.0
    )(post, *rims_in)
    drug_field, axial_flow = kernel_call(last_kernel, [(radial,) + plane] * 2, 4, 0.3)(*parts, below, above)
    return drug_field, axial_flow, free, bound


def solution(mesh):
    placed = (
        P(None, None, "th", "ax"),
        P(None, ("ax", "th")),
        P(None, ("ax", "th")),
        P(),
        P(),
        P(),
        P(("ax", "th"), None),
        P(("ax", "th")),
        P(("ax", "th")),
    )
    return jax.shard_map(
        per_device,
        mesh=mesh,
        in_specs=placed,
        out_specs=(
            P(None, "th", "ax"),
            P(None, "th", "ax"),
            P(None, ("ax", "th")),
            P(None, ("ax", "th")),
        ),
        check_vma=False,
    )
```

```python
import functools

import jax
import jax.numpy as jnp
from jax import lax
from jax.experimental import pallas as pl
from jax.experimental.pallas import tpu as pltpu
from jax.sharding import PartitionSpec as P


STEPS = 4
SUB = 2

VELOCITIES = [
    (0, 0, 0), (1, 0, 0), (-1, 0, 0), (0, 1, 0), (0, -1, 0), (0, 0, 1), (0, 0, -1),
    (1, 1, 0), (-1, -1, 0), (1, -1, 0), (-1, 1, 0),
    (1, 0, 1), (-1, 0, -1), (1, 0, -1), (-1, 0, 1),
    (0, 1, 1), (0, -1, -1), (0, 1, -1), (0, -1, 1),
    (0, 0, 0), (1, 0, 0), (-1, 0, 0), (0, 1, 0), (0, -1, 0), (0, 0, 1), (0, 0, -1),
]
WEIGHTS = [1.0 / 3.0] + [1.0 / 18.0] * 6 + [1.0 / 36.0] * 12 + [0.25] + [0.125] * 6
OPPOSITE = [0, 2, 1, 4, 3, 6, 5, 8, 7, 10, 9, 12, 11, 14, 13, 16, 15, 18, 17, 19, 21, 20, 23, 22, 25, 24]
MIRROR = [0, 1, 2, 3, 4, 6, 5, 7, 8, 9, 10, 13, 14, 11, 12, 17, 18, 15, 16, 19, 20, 21, 22, 23, 25, 24]
SECTOR_RISING = [3, 7, 10, 15, 17, 22]
SECTOR_FALLING = [4, 8, 9, 16, 18, 23]
SLAB_RISING = [1, 7, 9, 11, 13, 20]
SLAB_FALLING = [2, 8, 10, 12, 14, 21]
LEVEL_KEPT = [0, 3, 4, 5, 6, 15, 16, 17, 18, 19, 22, 23, 24, 25]
RISE_SLOTS = [(m, 0) for m in SLAB_RISING] + [(m, 0) for m in LEVEL_KEPT] + [(m, 1) for m in SLAB_RISING] + [(14, 0)]
FALL_SLOTS = [(m, 0) for m in SLAB_FALLING] + [(m, 0) for m in LEVEL_KEPT] + [(m, 1) for m in SLAB_FALLING] + [(11, 0)]
PAIRS = [(1, 2), (3, 4), (5, 6), (7, 8), (9, 10), (11, 12), (13, 14), (15, 16), (17, 18)]
FLOWS = 19
MEMBERS = 26
RELAX_FLOW = 1.25
RELAX_DRUG = 1.1
PUSH_AXIAL = 0.0001
PERMEABILITY = 0.3
RELEASE_RATE = 0.5

F32 = jnp.float32
BF16 = jnp.bfloat16
VMEM = pltpu.VMEM


def shifted(block, axis, distance):
    count = lax.axis_size(axis)
    return lax.ppermute(block, axis, [((i - distance) % count, i) for i in range(count)])


def paired(inner, outer):
    count = lax.axis_size("ax")
    near = [(i, i ^ 1) for i in range(count)]
    far = [(i, (i + 1) % count if i % 2 else (i - 1) % count) for i in range(count)]
    return lax.ppermute(inner, "ax", near), lax.ppermute(outer, "ax", far)


def by_parity(even, odd):
    return jnp.where(lax.axis_index("ax") % 2 == 0, even, odd)


def axial_rims(packed, first_ref, second_ref, across):
    first, second = first_ref[0:across, :], second_ref[0:across, :]
    if not packed:
        return first, second
    return by_parity(second, first), by_parity(first, second)


def lanes(shape):
    return lax.broadcasted_iota(jnp.int32, shape, len(shape) - 1)


def sublanes(shape):
    return lax.broadcasted_iota(jnp.int32, shape, len(shape) - 2)


def split3(value):
    high = value.astype(BF16)
    rest = value - high.astype(F32)
    middle = rest.astype(BF16)
    low = (rest - middle.astype(F32)).astype(BF16)
    return high, middle, low


def one_hot_lines(low_row, width):
    shape = (width, low_row.shape[-1])
    return jnp.where(sublanes(shape) == low_row, 1.0, 0.0).astype(BF16)


def scatter_rows(value_rows, code_rows, groups, width):
    terms, hots = [], []
    for value, code in zip(value_rows, code_rows, strict=True):
        group = code // width
        shape = (groups, value.shape[-1])
        hit = sublanes(shape) == group
        terms.append(jnp.concatenate([jnp.where(hit, part.astype(F32), 0.0) for part in split3(value)], axis=0).astype(BF16))
        hots.append(one_hot_lines(code - group * width, width))
    left = jnp.concatenate(terms, axis=1)
    right = jnp.concatenate(hots, axis=1)
    total = lax.dot_general(left, right, (((1,), (1,)), ((), ())), preferred_element_type=F32)
    return total[:groups] + total[groups:2 * groups] + total[2 * groups:3 * groups]


def gather_rows(table, code_rows, width):
    groups = table.shape[0]
    left = jnp.concatenate(split3(table), axis=0)
    lows = [code - (code // width) * width for code in code_rows]
    right = jnp.concatenate([one_hot_lines(low, width) for low in lows], axis=1)
    picked = jnp.dot(left, right, preferred_element_type=F32)
    picked = picked[:groups] + picked[groups:2 * groups] + picked[2 * groups:3 * groups]
    results, start = [], 0
    for code in code_rows:
        count = code.shape[-1]
        hit = sublanes((groups, count)) == code // width
        results.append(jnp.sum(jnp.where(hit, picked[:, start:start + count], 0.0), axis=0, keepdims=True))
        start += count
    return results


def source_plane(member, level, radial):
    step_r = VELOCITIES[member][2]
    if step_r == 1:
        return ((MIRROR[member], 0) if level == 0 else (member, level - 1)), True
    if step_r == -1:
        return ((OPPOSITE[member], radial - 1), False) if level == radial - 1 else ((member, level + 1), True)
    return (member, level), True


class Planes:
    def __init__(self, ref, radial, across):
        self.ref, self.radial, self.across = ref, radial, across

    def base(self, member, level):
        return (member * self.radial + level) * self.across

    def get(self, member, level):
        return self.ref[pl.ds(self.base(member, level), self.across), :]

    def put(self, member, level, value):
        self.ref[pl.ds(self.base(member, level), self.across), :] = value

    def rows(self, member, level, count, row):
        return self.ref[pl.ds(self.base(member, level) + row, count, stride=self.across), :]

    def put_rows(self, member, level, count, row, value):
        self.ref[pl.ds(self.base(member, level) + row, count, stride=self.across), :] = value


def axial_shift(value, step, member, level, radial, behind, ahead):
    along = value.shape[-1]
    lane = lanes(value.shape)
    if step == 1:
        slot = SLAB_RISING.index(member) * radial + level
        return jnp.where(lane == 0, pltpu.roll(behind, (-slot) % along, 1), pltpu.roll(value, 1, 1))
    slot = SLAB_FALLING.index(member) * radial + level
    return jnp.where(lane == along - 1, pltpu.roll(ahead, (along - 1 - slot) % along, 1), pltpu.roll(value, along - 1, 1))


def streamed(post, member, level, behind, ahead):
    radial, across = post.radial, post.across
    (origin, depth), moves = source_plane(member, level, radial)
    value = post.get(origin, depth)
    if not moves:
        return value
    step_z, step_s, _ = VELOCITIES[member]
    if step_z:
        value = axial_shift(value, step_z, origin, depth, radial, behind, ahead)
    if step_s:
        value = pltpu.roll(value, step_s % across, 0)
    return value


def incoming_rows(box, start, places, state, member, level, count, row):
    radial = state.radial
    step_r = VELOCITIES[member][2]
    here = start + places.index(member) * radial + level
    value = box[here - step_r:here - step_r + count, :]
    if step_r == 1 and level == 0:
        mirrored = start + places.index(MIRROR[member]) * radial
        value = jnp.where(sublanes(value.shape) == 0, box[mirrored:mirrored + 1, :], value)
    if step_r == -1 and level + count == radial:
        value = jnp.where(sublanes(value.shape) == count - 1, state.rows(member, level, count, row), value)
    return value


def relax_flow(members):
    def total(component):
        up, down = None, None
        for member in range(1, FLOWS):
            factor = VELOCITIES[member][component]
            if factor > 0:
                up = members[member] if up is None else up + members[member]
            elif factor < 0:
                down = members[member] if down is None else down + members[member]
        return up - down

    density = members[0]
    for member in range(1, FLOWS):
        density = density + members[member]
    inverse = 1.0 / density
    velocity = [(total(0) + PUSH_AXIAL) * inverse, total(1) * inverse, total(2) * inverse]
    speed_sq = velocity[0] * velocity[0] + velocity[1] * velocity[1] + velocity[2] * velocity[2]
    base = 1.0 - 1.5 * speed_sq
    weighted = {}
    for weight in sorted(set(WEIGHTS[:FLOWS])):
        weighted[weight] = (RELAX_FLOW * weight) * density

    def projected(member):
        result = None
        for component in range(3):
            factor = VELOCITIES[member][component]
            if factor == 0:
                continue
            if result is None:
                result = velocity[component] if factor > 0 else -velocity[component]
            else:
                result = result + velocity[component] if factor > 0 else result - velocity[component]
        return result

    results = [None] * FLOWS
    results[0] = (1.0 - RELAX_FLOW) * members[0] + weighted[WEIGHTS[0]] * base
    for first, second in PAIRS:
        along = projected(first)
        even = weighted[WEIGHTS[first]] * (base + 4.5 * along * along)
        odd = weighted[WEIGHTS[first]] * (3.0 * along)
        results[first] = (1.0 - RELAX_FLOW) * members[first] + (even + odd)
        results[second] = (1.0 - RELAX_FLOW) * members[second] + (even - odd)
    return results, velocity


def relax_drug(members, velocity):
    concentration = members[0]
    for member in members[1:]:
        concentration = concentration + member
    rest = (RELAX_DRUG * WEIGHTS[FLOWS]) * concentration
    results = [(1.0 - RELAX_DRUG) * members[0] + rest]
    even = (RELAX_DRUG * WEIGHTS[FLOWS + 1]) * concentration
    for component in range(3):
        odd = even * (4.0 * velocity[component])
        results.append((1.0 - RELAX_DRUG) * members[1 + 2 * component] + (even + odd))
        results.append((1.0 - RELAX_DRUG) * members[2 + 2 * component] + (even - odd))
    return results


def code_list(codes):
    return [codes[row:row + 1, :] for row in range(codes.shape[0])]


def pack_lines(row, width):
    return jnp.concatenate([row[:, start:start + width] for start in range(0, row.shape[-1], width)], axis=0)


def first_kernel(sectors, pops_ref, sector_ref, line_ref, strut_ref, free_ref, *refs):
    code_ref, boxes = refs[0], refs[1:1 + sectors]
    drug, sector, line, strut, top, sems = refs[1 + sectors:]
    across, width = code_ref.shape
    count = drug.shape[0]
    radial = pops_ref.shape[1]
    copies = [
        pltpu.make_async_copy(pops_ref.at[FLOWS:FLOWS + count, radial - 1], drug, sems.at[0]),
        pltpu.make_async_copy(sector_ref, sector, sems.at[1]),
        pltpu.make_async_copy(line_ref, line, sems.at[2]),
        pltpu.make_async_copy(strut_ref, strut, sems.at[3]),
        pltpu.make_async_copy(free_ref.at[0:across, :], top, sems.at[4]),
    ]
    for copy in copies:
        copy.start()
    for copy in copies:
        copy.wait()
    relative = sector[...] - lax.axis_index("th")
    relative = jnp.where(relative < 0, relative + sectors, relative)
    codes = relative * (across * width) + line[...]
    code_ref[...] = codes
    surface = drug[0]
    for member in range(1, count):
        surface = surface + drug[member]
    rows = code_list(codes)
    groups = sectors * across
    sums = scatter_rows(code_list(surface), rows, groups, width)
    counts = scatter_rows(code_list(jnp.ones_like(surface)), rows, groups, width)
    first = pack_lines(top[0:1, :], width)
    openness = PERMEABILITY * (1.0 - strut[...].astype(F32))
    for rel in range(sectors):
        out = boxes[rel]
        out[0:across] = sums[rel * across:(rel + 1) * across]
        out[across:2 * across] = counts[rel * across:(rel + 1) * across]
        out[2 * across:3 * across] = first
        out[3 * across:4 * across] = openness
        if rel in (1, sectors - 1):
            edge = codes[across - 1:across] if rel == 1 else codes[0:1]
            out[4 * across:5 * across] = jnp.broadcast_to(edge, (across, width)).astype(F32)


def bulk_kernel(first, packed, rims_too, radial, across, *refs):
    if rims_too:
        refs, rim_refs = refs[:-2], refs[-2:]
    if first:
        state_ref, post_ref, speed_ref = refs
    else:
        old_ref, inner_ref, outer_ref, state_ref, post_ref, speed_ref = refs
        old = Planes(old_ref, radial, across)
        behind, ahead = axial_rims(packed, inner_ref, outer_ref, across)
    state, post = Planes(state_ref, radial, across), Planes(post_ref, radial, across)
    for level in range(radial):
        if first:
            members = [state.get(member, level) for member in range(MEMBERS)]
        else:
            members = [streamed(old, member, level, behind, ahead) for member in range(MEMBERS)]
            for member in range(MEMBERS):
                state.put(member, level, members[member])
        results, velocity = relax_flow(members[:FLOWS])
        if level == radial - 1:
            for component in range(3):
                speed_ref[component * across:(component + 1) * across, :] = velocity[component]
        else:
            results = results + relax_drug(members[FLOWS:], velocity)
        for member, value in enumerate(results):
            post.put(member, level, value)
    if rims_too:
        for ref, slots, rising in ((rim_refs[0], RISE_SLOTS, True), (rim_refs[1], FALL_SLOTS, False)):
            for place, tile in enumerate(rim_tiles(post, slots, rising)):
                ref[place * across:(place + 1) * across, :] = tile


def slot_origin(column, along, rising):
    return along - 1 - column if rising else column


def rim_tiles(post, slots, rising):
    radial, across = post.radial, post.across
    along = post.ref.shape[-1]
    each = along // radial
    lane = lanes((across, along))
    tiles = []
    for place, (member, column) in enumerate(slots):
        if place % each == 0:
            tiles.append(jnp.zeros((across, along), F32))
        only_last = place == len(slots) - 1
        for level in range(radial - 1 if only_last else 0, radial - 1 if member >= FLOWS else radial):
            slot = (place % each) * radial + level
            value = pltpu.roll(post.get(member, level), (slot - slot_origin(column, along, rising)) % along, 1)
            tiles[-1] = jnp.where(lane == slot, value, tiles[-1])
    return tiles


def finished_tiles(ref, slots, rising, radial, across, drugs, fixed_rows):
    along = ref.shape[-1]
    each = along // radial
    lane, row = lanes((across, along)), sublanes((across, along))
    tiles = []
    for start in range(0, len(slots), each):
        tile = ref[(start // each) * across:(start // each + 1) * across, :]
        here = slots[start:start + each]
        for place, (member, column) in enumerate(here):
            if member >= FLOWS:
                slot = place * radial + radial - 1
                value = pltpu.roll(drugs[member - FLOWS], (slot - slot_origin(column, along, rising)) % along, 1)
                tile = jnp.where(lane == slot, value, tile)
        for side in sorted({side for side, _, _ in fixed_rows}):
            spread = jnp.zeros((across, along), F32)
            for other, level, blocks in fixed_rows:
                if other != side:
                    continue
                for place, (member, column) in enumerate(here):
                    origin = slot_origin(column, along, rising)
                    value = jnp.broadcast_to(blocks[member][:, origin:origin + 1], (across, along))
                    spread = jnp.where(lane - row == place * radial + level, value, spread)
            tile = jnp.where(row == side, jnp.sum(spread, axis=0, keepdims=True), tile)
        tiles.append(tile)
    return tiles


class Ghosts:
    def __init__(self, radial, across, along, behind, ahead, rise, fall):
        self.radial, self.across, self.along = radial, across, along
        self.behind, self.ahead, self.rise, self.fall = behind, ahead, rise, fall
        lane = lanes((across, along))
        self.is_behind = lane < radial
        self.level = jnp.where(self.is_behind, lane, lane - radial)

    def pick(self, message, slot, target):
        each = self.along // self.radial
        tile = message[(slot // each) * self.across:(slot // each + 1) * self.across, :]
        return pltpu.roll(tile, (target - (slot % each) * self.radial) % self.along, 1)

    def join(self, first, second):
        return jnp.where(self.is_behind, self.pick(*first, 0), self.pick(*second, self.radial))

    def arriving(self, member):
        step = VELOCITIES[member][0]
        rise, fall = RISE_SLOTS.index, FALL_SLOTS.index
        if step == 1:
            return self.join((self.behind, rise((member, 1))), (self.rise, rise((member, 0))))
        if step == -1:
            return self.join((self.fall, fall((member, 0))), (self.ahead, fall((member, 1))))
        return self.join((self.behind, rise((member, 0))), (self.ahead, fall((member, 0))))

    def own(self, member):
        return self.join((self.behind, RISE_SLOTS.index((member, 0))), (self.ahead, FALL_SLOTS.index((member, 0))))

    def risen(self, member):
        value = self.arriving(member)
        step = VELOCITIES[member][2]
        if step == 1:
            return jnp.where(self.level == 0, self.arriving(MIRROR[member]), pltpu.roll(value, 1, 1))
        if step == -1:
            return pltpu.roll(value, self.along - 1, 1)
        return value

    def streamed(self, member, below_rows, above_rows):
        value = self.risen(member)
        row = sublanes(value.shape)
        step = VELOCITIES[member][1]
        if step == 1:
            place = SECTOR_RISING.index(member)
            value = jnp.where(row == 0, below_rows[place:place + 1, :], pltpu.roll(value, 1, 0))
        elif step == -1:
            place = SECTOR_FALLING.index(member)
            value = jnp.where(row == self.across - 1, above_rows[place:place + 1, :], pltpu.roll(value, self.across - 1, 0))
        if VELOCITIES[member][2] == -1:
            value = jnp.where(self.level == self.radial - 1, self.own(OPPOSITE[member]), value)
        return value


def gather_cells(table, codes, width):
    group = codes // width
    low = codes - group * width
    row = jnp.zeros(codes.shape, F32)
    for place in range(table.shape[0]):
        row = jnp.where(group == place, table[place:place + 1, :], row)
    return jnp.sum(jnp.where(lanes(codes.shape) == low, row, 0.0), axis=1, keepdims=True)


def table_of(inbox, start, across):
    return jnp.concatenate([box[start:start + across, :] for box in inbox], axis=0)


def flux_kernel(sectors, step, radial, *refs):
    first, odd = step == 0, step % 2 == 1
    refs = list(refs)
    state_ref, bulk_ref, speed_ref, code_ref, strut_ref, coef_ref, on_ref, off_ref = refs[:8]
    inbox = refs[8:8 + sectors]
    refs = refs[8 + sectors:]
    open_ref = counts_ref = ghost_code_ref = ghost_open_ref = None
    if not first:
        open_ref, counts_ref = refs[:2]
        refs = refs[2:]
    if not odd:
        rim_refs, refs = refs[:2], refs[2:]
    if odd:
        sent_refs, got_refs = refs[:2], refs[2:4]
        refs = refs[4:]
        if step > 1:
            ghost_code_ref, ghost_open_ref = refs[:2]
            refs = refs[2:]
    last = step == STEPS - 1
    post_ref, one_ref, two_ref, added_ref = refs[:4]
    refs = refs[4:]
    if not last:
        top_ref, refs = refs[0], refs[1:]
    del bulk_ref
    across, along = code_ref.shape
    plane = (across, along)
    end = radial - 1
    state, post = Planes(state_ref, radial, across), Planes(post_ref, radial, across)
    codes = code_list(code_ref[...])
    below, above = inbox[sectors - 1], inbox[1]
    base = 2 * across if first else across
    picked = jnp.concatenate(gather_rows(table_of(inbox, base, across), codes, along), axis=0)
    if first:
        openness = jnp.concatenate(gather_rows(table_of(inbox, 3 * across, across), codes, along), axis=0)
        counts = inbox[0][across:2 * across, :]
        for box in inbox[1:]:
            counts = counts + box[across:2 * across, :]
        refs[0][...] = openness
        refs[1][...] = counts
        count, limit = across * along, sectors * across * along
        up = above[4 * across:5 * across, :].astype(jnp.int32) + count
        down = below[4 * across:5 * across, :].astype(jnp.int32) - count
        up = jnp.where(up >= limit, up - limit, up)
        down = jnp.where(down < 0, down + limit, down)
        refs[2][...] = jnp.where(sublanes(plane) == 0, up, down)
    else:
        openness, counts = open_ref[...], counts_ref[...]
    total = inbox[0][0:across, :]
    for box in inbox[1:]:
        total = total + box[0:across, :]
    strut = strut_ref[...].astype(F32)
    shut = PERMEABILITY * (1.0 - strut)
    added = shut * (total - counts * inbox[0][base:base + across, :]) + RELEASE_RATE * strut
    added_ref[...] = added
    if not last:
        free = coef_ref[0:across, :] + added * coef_ref[across:2 * across, :]
        bound = coef_ref[2 * across:3 * across, :] + added * coef_ref[3 * across:4 * across, :]
        top = free - (on_ref[0:1, 0:1] * free * (1.0 - bound) - off_ref[0:1, 0:1] * bound)
        top_ref[...] = top
    start = rims_start(step, across)
    row = sublanes(plane)
    drugs = [state.get(member, end) for member in range(FLOWS, MEMBERS)]
    if not first:
        place = start + SECTOR_RISING.index(FLOWS + 3) * radial + end
        drugs[3] = jnp.where(row == 0, below[place:place + 1, :], drugs[3])
        place = start + SECTOR_FALLING.index(FLOWS + 4) * radial + end
        drugs[4] = jnp.where(row == across - 1, above[place:place + 1, :], drugs[4])
    surface = drugs[0]
    for drug in drugs[1:]:
        surface = surface + drug
    flux = openness * (surface - picked)
    drugs = [drug - WEIGHTS[FLOWS + place] * flux for place, drug in enumerate(drugs)]
    velocity = [speed_ref[component * across:(component + 1) * across, :] for component in range(3)]
    drugs = relax_drug(drugs, velocity)
    for place, value in enumerate(drugs):
        post.put(FLOWS + place, end, value)
    fixed_rows = []
    if not first:
        block = across
        for side, box, places in ((0, below, SECTOR_RISING), (across - 1, above, SECTOR_FALLING)):
            moving = 1 if side == 0 else -1
            for level in range(0, radial, block):
                members = []
                for member in range(MEMBERS):
                    if VELOCITIES[member][1] == moving:
                        value = incoming_rows(box, start, places, state, member, level, block, side)
                    else:
                        value = state.rows(member, level, block, side)
                    if member >= FLOWS and level + block == radial:
                        lowered = value - WEIGHTS[member] * flux[side:side + 1, :]
                        value = jnp.where(sublanes(value.shape) == block - 1, lowered, value)
                    members.append(value)
                results, velocity = relax_flow(members[:FLOWS])
                results = results + relax_drug(members[FLOWS:], velocity)
                for member, value in enumerate(results):
                    post.put_rows(member, level, block, side, value)
                fixed_rows.append((side, level, results))
    if not odd:
        rise = finished_tiles(rim_refs[0], RISE_SLOTS, True, radial, across, drugs, fixed_rows) + [top]
        fall = finished_tiles(rim_refs[1], FALL_SLOTS, False, radial, across, drugs, fixed_rows) + [top]
        if first:
            own = code_ref[...].astype(F32)
            rise = rise + [shut, pltpu.roll(own, 1, 1)]
            fall = fall + [shut, own]
        for place, (up, down) in enumerate(zip(rise, fall, strict=True)):
            one_ref[place * across:(place + 1) * across, :] = by_parity(up, down)
            two_ref[place * across:(place + 1) * across, :] = by_parity(down, up)
        return
    rise, fall = by_parity(sent_refs[0][...], sent_refs[1][...]), by_parity(sent_refs[1][...], sent_refs[0][...])
    behind, ahead = by_parity(got_refs[1][...], got_refs[0][...]), by_parity(got_refs[0][...], got_refs[1][...])
    ghosts = Ghosts(radial, across, along, behind, ahead, rise, fall)
    tables = [table_of(inbox, (2 + side) * across, across) for side in range(2)]
    if step == 1:
        place = code_place(radial, across, along)
        sides = [message[place:place + across, 0:1].astype(jnp.int32) for message in (behind, ahead)]
        sides = [jnp.broadcast_to(side, plane) for side in sides]
        opens = [gather_cells(table_of(inbox, (4 + side) * across, across), sides[side], along) for side in range(2)]
        for side in range(2):
            refs[0][side * across:(side + 1) * across, :] = sides[side]
            refs[1][side * across:(side + 1) * across, :] = jnp.broadcast_to(opens[side], plane)
    else:
        sides = [ghost_code_ref[side * across:(side + 1) * across, :] for side in range(2)]
        opens = [ghost_open_ref[side * across:(side + 1) * across, 0:1] for side in range(2)]
    tops = [gather_cells(tables[side], sides[side], along) for side in range(2)]
    ghost_start = start + len(SECTOR_RISING) * radial
    below_rows = below[ghost_start:ghost_start + across, :]
    above_rows = above[ghost_start:ghost_start + across, :]
    members = [ghosts.streamed(member, below_rows, above_rows) for member in range(MEMBERS)]
    surface = members[FLOWS]
    for member in range(FLOWS + 1, MEMBERS):
        surface = surface + members[member]
    ghost_flux = jnp.where(ghosts.is_behind, opens[0] * (surface - tops[0]), opens[1] * (surface - tops[1]))
    ghost_flux = jnp.where(ghosts.level == end, ghost_flux, 0.0)
    members = members[:FLOWS] + [members[member] - WEIGHTS[member] * ghost_flux for member in range(FLOWS, MEMBERS)]
    results, velocity = relax_flow(members[:FLOWS])
    results = results + relax_drug(members[FLOWS:], velocity)
    lane = lanes(plane)
    behind, ahead = jnp.zeros(plane, F32), jnp.zeros(plane, F32)
    for place in range(len(SLAB_RISING)):
        here = (lane >= place * radial) & (lane < (place + 1) * radial)
        behind = jnp.where(here, pltpu.roll(results[SLAB_RISING[place]], (place * radial) % along, 1), behind)
        ahead = jnp.where(here, pltpu.roll(results[SLAB_FALLING[place]], ((place - 1) * radial) % along, 1), ahead)
    one_ref[...] = behind
    two_ref[...] = ahead


def code_place(radial, across, along):
    return (rim_rows(radial, across, along) // across + 2) * across


def rim_rows(radial, across, along):
    return -(-len(RISE_SLOTS) // (along // radial)) * across


def rims_start(step, across):
    return (6 if step == 1 else 4 if step % 2 else 2) * across


def wall_rates(spread_ref, on_ref, off_ref, width):
    depth = spread_ref.shape[0]
    shape = (depth, depth)
    rate_on = jnp.transpose(jnp.broadcast_to(on_ref[...], shape))[:, 0:1]
    rate_off = jnp.transpose(jnp.broadcast_to(off_ref[...], shape))[:, 0:1]
    top = jnp.transpose(jnp.broadcast_to(spread_ref[0:1, :], shape))[:, 0:1]
    return [jnp.broadcast_to(column, (depth, width)) for column in (rate_on, rate_off, spread_ref[:, 0:1], top)]


def split2(value):
    high = value.astype(BF16)
    return high, (value - high.astype(F32)).astype(BF16)


def left_terms(spread):
    high, low = split2(spread)
    return jnp.concatenate([high, high, low], axis=1)


def product(left, free):
    high, low = split2(free)
    return jnp.dot(left, jnp.concatenate([high, low, high], axis=0), preferred_element_type=F32)


def plan_ahead(left, rates, free, bound):
    rate_on, rate_off, entry, top = rates
    moved = product(left, free)
    rate = rate_on * moved * (1.0 - bound) - rate_off * bound
    gain = rate_on * entry * (1.0 - bound)
    first = jnp.sum(top * (moved - rate), axis=0, keepdims=True)
    slope = jnp.sum(top * (entry - gain), axis=0, keepdims=True)
    return moved, (first, slope, bound[0:1, :] + rate[0:1, :], gain[0:1, :])


def put_coefs(coef_ref, across, width, row, parts):
    for index, part in enumerate(parts):
        for step in range(part.shape[1] // width):
            place = index * across + row + step
            coef_ref[place:place + 1, :] = part[:, step * width:(step + 1) * width]


TOGETHER = 2


def plan_kernel(free_ref, bound_ref, spread_ref, on_ref, off_ref, moved_ref, coef_ref):
    width = coef_ref.shape[1]
    across = coef_ref.shape[0] // 4
    rates = wall_rates(spread_ref, on_ref, off_ref, TOGETHER * width)
    left = left_terms(spread_ref[...])
    for row in range(0, across, TOGETHER):
        place = slice(row * width, (row + TOGETHER) * width)
        moved, parts = plan_ahead(left, rates, free_ref[:, place], bound_ref[:, place])
        moved_ref[:, place] = moved
        put_coefs(coef_ref, across, width, row, parts)


def wall_kernel(last, moved_ref, bound_ref, added_ref, spread_ref, on_ref, off_ref, *outs):
    across, width = added_ref.shape
    rates = wall_rates(spread_ref, on_ref, off_ref, TOGETHER * width)
    rate_on, rate_off, entry, _ = rates
    left = left_terms(spread_ref[...])
    for row in range(0, across, TOGETHER):
        place = slice(row * width, (row + TOGETHER) * width)
        added = jnp.concatenate([added_ref[row + step:row + step + 1, :] for step in range(TOGETHER)], axis=1)
        free = moved_ref[:, place] + entry * added
        bound = bound_ref[:, place]
        for substep in range(SUB):
            if substep:
                free = product(left, free)
            rate = rate_on * free * (1.0 - bound) - rate_off * bound
            free = free - rate
            bound = bound + rate
        outs[1][:, place] = bound
        if last:
            outs[0][:, place] = free
        else:
            moved, parts = plan_ahead(left, rates, free, bound)
            outs[0][:, place] = moved
            put_coefs(outs[2], across, width, row, parts)


def send_kernel(sectors, step, radial, *refs):
    packed = step % 2 == 0
    post_ref, one_ref, two_ref, code_ref, edges_ref, top_ref = refs[:6]
    refs = refs[6:]
    if packed:
        sent_refs, outs = refs[:2], refs[2:]
    else:
        outs = refs
    across, along = code_ref.shape
    post = Planes(post_ref, radial, across)
    behind, ahead = axial_rims(packed, one_ref, two_ref, across)
    end = radial - 1
    row = sublanes((across, along))
    surface = post.get(FLOWS, end) + post.get(FLOWS + 5, end - 1) + post.get(FLOWS + 5, end)
    surface = surface + axial_shift(post.get(FLOWS + 1, end), 1, FLOWS + 1, end, radial, behind, ahead)
    surface = surface + axial_shift(post.get(FLOWS + 2, end), -1, FLOWS + 2, end, radial, behind, ahead)
    rising = post.get(FLOWS + 3, end)
    falling = post.get(FLOWS + 4, end)
    surface = surface + jnp.where(row == 0, 0.0, pltpu.roll(rising, 1, 0))
    surface = surface + jnp.where(row == across - 1, 0.0, pltpu.roll(falling, across - 1, 0))
    values = code_list(surface) + [rising[across - 1:across, :], falling[0:1, :]]
    codes = code_list(code_ref[...]) + [edges_ref[0:1, :], edges_ref[1:2, :]]
    sums = scatter_rows(values, codes, sectors * across, along)
    parts = [top_ref[...]]
    if packed:
        whole_behind = by_parity(two_ref[...], one_ref[...])
        whole_ahead = by_parity(one_ref[...], two_ref[...])
        skip = rim_rows(radial, across, along)
        for index in range(2 if step == 0 else 1):
            place = skip + index * across
            parts = parts + [whole_behind[place:place + across, :], whole_ahead[place:place + across, :]]
    for rel in range(sectors):
        outs[rel][0:across] = sums[rel * across:(rel + 1) * across]
        for index, part in enumerate(parts):
            outs[rel][(1 + index) * across:(2 + index) * across] = part
    start = rims_start(step + 1, across)
    for out, places, side in ((outs[1], SECTOR_RISING, across - 1), (outs[sectors - 1], SECTOR_FALLING, 0)):
        for place, member in enumerate(places):
            moving = VELOCITIES[member][0]
            base = start + place * radial
            if moving:
                for level in range(radial):
                    value = axial_shift(post.get(member, level), moving, member, level, radial, behind, ahead)
                    out[base + level:base + level + 1, :] = value[side:side + 1, :]
            else:
                out[base:base + radial, :] = post.rows(member, 0, radial, side)
    if packed:
        rise, fall = by_parity(sent_refs[0][...], sent_refs[1][...]), by_parity(sent_refs[1][...], sent_refs[0][...])
        ghosts = Ghosts(radial, across, along, whole_behind, whole_ahead, rise, fall)
        base = start + len(SECTOR_RISING) * radial
        for out, places, side in ((outs[1], SECTOR_RISING, across - 1), (outs[sectors - 1], SECTOR_FALLING, 0)):
            for place, member in enumerate(places):
                out[base + place:base + place + 1, :] = ghosts.risen(member)[side:side + 1, :]
            for place in range(len(places), across):
                out[base + place:base + place + 1, :] = jnp.zeros((1, along), F32)


def last_send_kernel(radial, across, post_ref, inner_ref, outer_ref, up_ref, down_ref):
    post = Planes(post_ref, radial, across)
    behind, ahead = axial_rims(False, inner_ref, outer_ref, across)
    for out, drug, plus, minus, side in ((up_ref, FLOWS + 3, 7, 10, across - 1), (down_ref, FLOWS + 4, 9, 8, 0)):
        out[0:radial, :] = post.rows(drug, 0, radial, side)
        for level in range(radial):
            value = axial_shift(post.get(plus, level), 1, plus, level, radial, behind, ahead)
            value = value - axial_shift(post.get(minus, level), -1, minus, level, radial, behind, ahead)
            out[radial + level:radial + level + 1, :] = value[side:side + 1, :]


def fields_kernel(radial, across, post_ref, inner_ref, outer_ref, drug_ref, flow_ref):
    post = Planes(post_ref, radial, across)
    behind, ahead = axial_rims(False, inner_ref, outer_ref, across)
    for level in range(radial):
        def member_of(member):
            value = streamed(post, member, level, behind, ahead)
            step = VELOCITIES[member][1]
            if step:
                edge = 0 if step > 0 else across - 1
                value = jnp.where(sublanes(value.shape) == edge, 0.0, value)
            return value

        drug = member_of(FLOWS)
        for member in range(FLOWS + 1, MEMBERS):
            drug = drug + member_of(member)
        drug_ref[level] = drug
        flow = None
        for member in range(FLOWS):
            factor = VELOCITIES[member][0]
            if factor:
                value = member_of(member)
                flow = (value if factor > 0 else -value) if flow is None else (flow + value if factor > 0 else flow - value)
        flow_ref[level] = flow


def last_kernel(drug_part, flow_part, below, above, drug_ref, flow_ref):
    radial, across, along = drug_ref.shape
    row = sublanes((across, along))
    for part, out, base in ((drug_part, drug_ref, 0), (flow_part, flow_ref, radial)):
        for level in range(radial):
            place = base + level
            value = part[level] + jnp.where(row == 0, below[place:place + 1, :], 0.0)
            out[level] = value + jnp.where(row == across - 1, above[place:place + 1, :], 0.0)


def kernel_call(body, outs, count, micros, aliases=None):
    shapes = [out if isinstance(out, jax.ShapeDtypeStruct) else jax.ShapeDtypeStruct(out, F32) for out in outs]
    return pl.pallas_call(
        body,
        out_shape=shapes,
        in_specs=[pl.BlockSpec(memory_space=VMEM)] * count,
        out_specs=[pl.BlockSpec(memory_space=VMEM)] * len(outs),
        input_output_aliases=aliases or {},
        cost_estimate=pl.CostEstimate(flops=0, bytes_accessed=int(micros * 3.0e6), transcendentals=0),
        compiler_params=pltpu.CompilerParams(vmem_limit_bytes=24 * 1024 * 1024),
    )


def first_call(sectors, populations, sector, line, strut, free):
    members, _, across, along = populations.shape
    plane = (across, along)
    sizes = [((5 if hop in (1, sectors - 1) else 4) * across, along) for hop in range(sectors)]
    return pl.pallas_call(
        functools.partial(first_kernel, sectors),
        name="first",
        out_shape=[jax.ShapeDtypeStruct(plane, jnp.int32)] + [jax.ShapeDtypeStruct(size, F32) for size in sizes],
        in_specs=[pl.BlockSpec(memory_space=pltpu.HBM)] * 5,
        out_specs=[pl.BlockSpec(memory_space=VMEM)] * (1 + sectors),
        scratch_shapes=[
            VMEM((members - FLOWS, across, along), F32),
            VMEM(plane, jnp.int32),
            VMEM(plane, jnp.int32),
            VMEM(plane, jnp.int32),
            VMEM((across, free.shape[1]), F32),
            pltpu.SemaphoreType.DMA((5,)),
        ],
    )(populations, sector, line, strut, free)


def per_device(populations, wall_free, wall_bound, wall_propagator, bind_on, bind_off, iface_sector, iface_line, strut_mask):
    members, radial, across, along = populations.shape
    sectors = lax.axis_size("th")
    plane = (across, along)
    flat = (members * radial * across, along)
    rims = len(SECTOR_RISING) * radial
    strut = strut_mask.reshape(plane)
    rate_on = bind_on.reshape(1, -1)
    rate_off = bind_off.reshape(1, -1)

    def exchange(boxes):
        inbox = [boxes[0]] + [None] * (sectors - 1)
        for hop in range(1, sectors):
            inbox[sectors - hop] = shifted(boxes[hop], "th", hop)
        return inbox

    codes, *boxes = first_call(sectors, populations, iface_sector.reshape(plane), iface_line.reshape(plane), strut, wall_free)
    inbox = exchange(boxes)
    state = populations.reshape(flat)
    speeds = (3 * across, along)
    four = (4 * across, along)
    two = (2 * across, along)
    rim = rim_rows(radial, across, along)
    shapes = wall_free.shape
    bulk, speed, *tiles = kernel_call(
        functools.partial(bulk_kernel, True, True, True, radial, across), [flat, speeds, (rim, along), (rim, along)], 1, 1.5
    )(state)
    moved, coefs = kernel_call(plan_kernel, [shapes, four], 5, 1.0)(
        wall_free, wall_bound, wall_propagator, rate_on, rate_off
    )
    bound = wall_bound
    fixed, ghost = [], []
    edges = sent = got = None
    for step in range(STEPS):
        odd, last = step % 2 == 1, step == STEPS - 1
        if odd:
            pair = [plane, plane]
        else:
            pair = [(rim + (3 if step == 0 else 1) * across, along)] * 2
        outs = [flat] + pair + [plane] * (1 if last else 2)
        if step == 0:
            outs = outs + [plane, plane, jax.ShapeDtypeStruct(plane, jnp.int32)]
        if step == 1:
            outs = outs + [jax.ShapeDtypeStruct(two, jnp.int32), two]
        extra = fixed + ([*sent, *got, *ghost] if odd else tiles)
        post, one, other, added, *rest = kernel_call(
            functools.partial(flux_kernel, sectors, step, radial), outs, 8 + sectors + len(extra), 0.8, {1: 0}
        )(state, bulk, speed, codes, strut, coefs, rate_on, rate_off, *inbox, *extra)
        if not last:
            top, *rest = rest
        if step == 0:
            fixed, edges = rest[:2], rest[2]
        if step == 1:
            ghost = rest
        if odd:
            rims_in, own = [one, other], []
        else:
            sent = [one, other]
            got = paired(*sent)
            rims_in, own = [*got], sent
        results = kernel_call(
            functools.partial(wall_kernel, last), [shapes, shapes] + ([] if last else [four]), 6, 1.5
        )(moved, bound, added, wall_propagator, rate_on, rate_off)
        if last:
            free, bound = results
            continue
        moved, bound, coefs = results
        start = rims_start(step + 1, across)
        long = start + rims + (0 if odd else across)
        sizes = [(long if hop in (1, sectors - 1) else start, along) for hop in range(sectors)]
        boxes = kernel_call(
            functools.partial(send_kernel, sectors, step, radial), sizes, 6 + len(own), 0.3
        )(post, *rims_in, codes, edges, top, *own)
        inbox = exchange(boxes)
        outs = [flat, flat, speeds] + ([(rim, along)] * 2 if odd else [])
        state, bulk, speed, *tiles = kernel_call(
            functools.partial(bulk_kernel, False, not odd, odd, radial, across), outs, 3, 2.0
        )(post, *rims_in)
    up, down = kernel_call(
        functools.partial(last_send_kernel, radial, across), [(2 * radial, along)] * 2, 3, 0.2
    )(post, *rims_in)
    below = shifted(up, "th", 1)
    above = shifted(down, "th", -1)
    parts = kernel_call(
        functools.partial(fields_kernel, radial, across), [(radial,) + plane] * 2, 3, 1.0
    )(post, *rims_in)
    drug_field, axial_flow = kernel_call(last_kernel, [(radial,) + plane] * 2, 4, 0.3)(*parts, below, above)
    return drug_field, axial_flow, free, bound


def solution(mesh):
    placed = (
        P(None, None, "th", "ax"),
        P(None, ("ax", "th")),
        P(None, ("ax", "th")),
        P(),
        P(),
        P(),
        P(("ax", "th"), None),
        P(("ax", "th")),
        P(("ax", "th")),
    )
    return jax.shard_map(
        per_device,
        mesh=mesh,
        in_specs=placed,
        out_specs=(
            P(None, "th", "ax"),
            P(None, "th", "ax"),
            P(None, ("ax", "th")),
            P(None, ("ax", "th")),
        ),
        check_vma=False,
    )
```

```python
import functools

import jax
import jax.numpy as jnp
from jax import lax
from jax.experimental import pallas as pl
from jax.experimental.pallas import tpu as pltpu
from jax.sharding import PartitionSpec as P


STEPS = 4
SUB = 2

VELOCITIES = [
    (0, 0, 0), (1, 0, 0), (-1, 0, 0), (0, 1, 0), (0, -1, 0), (0, 0, 1), (0, 0, -1),
    (1, 1, 0), (-1, -1, 0), (1, -1, 0), (-1, 1, 0),
    (1, 0, 1), (-1, 0, -1), (1, 0, -1), (-1, 0, 1),
    (0, 1, 1), (0, -1, -1), (0, 1, -1), (0, -1, 1),
    (0, 0, 0), (1, 0, 0), (-1, 0, 0), (0, 1, 0), (0, -1, 0), (0, 0, 1), (0, 0, -1),
]
WEIGHTS = [1.0 / 3.0] + [1.0 / 18.0] * 6 + [1.0 / 36.0] * 12 + [0.25] + [0.125] * 6
OPPOSITE = [0, 2, 1, 4, 3, 6, 5, 8, 7, 10, 9, 12, 11, 14, 13, 16, 15, 18, 17, 19, 21, 20, 23, 22, 25, 24]
MIRROR = [0, 1, 2, 3, 4, 6, 5, 7, 8, 9, 10, 13, 14, 11, 12, 17, 18, 15, 16, 19, 20, 21, 22, 23, 25, 24]
SECTOR_RISING = [3, 7, 10, 15, 17, 22]
SECTOR_FALLING = [4, 8, 9, 16, 18, 23]
SLAB_RISING = [1, 7, 9, 11, 13, 20]
SLAB_FALLING = [2, 8, 10, 12, 14, 21]
LEVEL_KEPT = [0, 3, 4, 5, 6, 15, 16, 17, 18, 19, 22, 23, 24, 25]
RISE_SLOTS = [(m, 0) for m in SLAB_RISING] + [(m, 0) for m in LEVEL_KEPT] + [(m, 1) for m in SLAB_RISING] + [(14, 0)]
FALL_SLOTS = [(m, 0) for m in SLAB_FALLING] + [(m, 0) for m in LEVEL_KEPT] + [(m, 1) for m in SLAB_FALLING] + [(11, 0)]
PAIRS = [(1, 2), (3, 4), (5, 6), (7, 8), (9, 10), (11, 12), (13, 14), (15, 16), (17, 18)]
FLOWS = 19
MEMBERS = 26
RELAX_FLOW = 1.25
RELAX_DRUG = 1.1
PUSH_AXIAL = 0.0001
PERMEABILITY = 0.3
RELEASE_RATE = 0.5

F32 = jnp.float32
BF16 = jnp.bfloat16
VMEM = pltpu.VMEM


def shifted(block, axis, distance):
    count = lax.axis_size(axis)
    return lax.ppermute(block, axis, [((i - distance) % count, i) for i in range(count)])


def paired(inner, outer):
    count = lax.axis_size("ax")
    near = [(i, i ^ 1) for i in range(count)]
    far = [(i, (i + 1) % count if i % 2 else (i - 1) % count) for i in range(count)]
    return lax.ppermute(inner, "ax", near), lax.ppermute(outer, "ax", far)


def by_parity(even, odd):
    return jnp.where(lax.axis_index("ax") % 2 == 0, even, odd)


def axial_rims(packed, first_ref, second_ref, across):
    first, second = first_ref[0:across, :], second_ref[0:across, :]
    if not packed:
        return first, second
    return by_parity(second, first), by_parity(first, second)


def lanes(shape):
    return lax.broadcasted_iota(jnp.int32, shape, len(shape) - 1)


def sublanes(shape):
    return lax.broadcasted_iota(jnp.int32, shape, len(shape) - 2)


def split3(value):
    high = value.astype(BF16)
    rest = value - high.astype(F32)
    middle = rest.astype(BF16)
    low = (rest - middle.astype(F32)).astype(BF16)
    return high, middle, low


def one_hot_lines(low_row, width):
    shape = (width, low_row.shape[-1])
    return jnp.where(sublanes(shape) == low_row, 1.0, 0.0).astype(BF16)


def scatter_rows(value_rows, code_rows, groups, width):
    terms, hots = [], []
    for value, code in zip(value_rows, code_rows, strict=True):
        group = code // width
        shape = (groups, value.shape[-1])
        hit = sublanes(shape) == group
        terms.append(jnp.concatenate([jnp.where(hit, part.astype(F32), 0.0) for part in split3(value)], axis=0).astype(BF16))
        hots.append(one_hot_lines(code - group * width, width))
    left = jnp.concatenate(terms, axis=1)
    right = jnp.concatenate(hots, axis=1)
    total = lax.dot_general(left, right, (((1,), (1,)), ((), ())), preferred_element_type=F32)
    return total[:groups] + total[groups:2 * groups] + total[2 * groups:3 * groups]


def gather_rows(table, code_rows, width):
    groups = table.shape[0]
    left = jnp.concatenate(split3(table), axis=0)
    lows = [code - (code // width) * width for code in code_rows]
    right = jnp.concatenate([one_hot_lines(low, width) for low in lows], axis=1)
    picked = jnp.dot(left, right, preferred_element_type=F32)
    picked = picked[:groups] + picked[groups:2 * groups] + picked[2 * groups:3 * groups]
    results, start = [], 0
    for code in code_rows:
        count = code.shape[-1]
        hit = sublanes((groups, count)) == code // width
        results.append(jnp.sum(jnp.where(hit, picked[:, start:start + count], 0.0), axis=0, keepdims=True))
        start += count
    return results


def source_plane(member, level, radial):
    step_r = VELOCITIES[member][2]
    if step_r == 1:
        return ((MIRROR[member], 0) if level == 0 else (member, level - 1)), True
    if step_r == -1:
        return ((OPPOSITE[member], radial - 1), False) if level == radial - 1 else ((member, level + 1), True)
    return (member, level), True


class Planes:
    def __init__(self, ref, radial, across):
        self.ref, self.radial, self.across = ref, radial, across

    def base(self, member, level):
        return (member * self.radial + level) * self.across

    def get(self, member, level):
        return self.ref[pl.ds(self.base(member, level), self.across), :]

    def put(self, member, level, value):
        self.ref[pl.ds(self.base(member, level), self.across), :] = value

    def rows(self, member, level, count, row):
        return self.ref[pl.ds(self.base(member, level) + row, count, stride=self.across), :]

    def put_rows(self, member, level, count, row, value):
        self.ref[pl.ds(self.base(member, level) + row, count, stride=self.across), :] = value


def axial_shift(value, step, member, level, radial, behind, ahead):
    along = value.shape[-1]
    lane = lanes(value.shape)
    if step == 1:
        slot = SLAB_RISING.index(member) * radial + level
        return jnp.where(lane == 0, pltpu.roll(behind, (-slot) % along, 1), pltpu.roll(value, 1, 1))
    slot = SLAB_FALLING.index(member) * radial + level
    return jnp.where(lane == along - 1, pltpu.roll(ahead, (along - 1 - slot) % along, 1), pltpu.roll(value, along - 1, 1))


def axial_shift_rows(post, member, step, side, behind, ahead):
    value = post.rows(member, 0, post.radial, side)
    along = value.shape[-1]
    tile, slots = (behind, SLAB_RISING) if step == 1 else (ahead, SLAB_FALLING)
    lane = lanes(value.shape)
    here = lane - sublanes(value.shape) == slots.index(member) * post.radial
    column = jnp.sum(jnp.where(here, tile[side:side + 1, :], 0.0), axis=1, keepdims=True)
    return jnp.where(lane == (0 if step == 1 else along - 1), column, pltpu.roll(value, step % along, 1))


def streamed(post, member, level, behind, ahead):
    radial, across = post.radial, post.across
    (origin, depth), moves = source_plane(member, level, radial)
    value = post.get(origin, depth)
    if not moves:
        return value
    step_z, step_s, _ = VELOCITIES[member]
    if step_z:
        value = axial_shift(value, step_z, origin, depth, radial, behind, ahead)
    if step_s:
        value = pltpu.roll(value, step_s % across, 0)
    return value


def incoming_rows(box, start, places, state, member, level, count, row):
    radial = state.radial
    step_r = VELOCITIES[member][2]
    here = start + places.index(member) * radial + level
    value = box[here - step_r:here - step_r + count, :]
    if step_r == 1 and level == 0:
        mirrored = start + places.index(MIRROR[member]) * radial
        value = jnp.where(sublanes(value.shape) == 0, box[mirrored:mirrored + 1, :], value)
    if step_r == -1 and level + count == radial:
        value = jnp.where(sublanes(value.shape) == count - 1, state.rows(member, level, count, row), value)
    return value


def relax_flow(members):
    def total(component):
        up, down = None, None
        for member in range(1, FLOWS):
            factor = VELOCITIES[member][component]
            if factor > 0:
                up = members[member] if up is None else up + members[member]
            elif factor < 0:
                down = members[member] if down is None else down + members[member]
        return up - down

    density = members[0]
    for member in range(1, FLOWS):
        density = density + members[member]
    inverse = 1.0 / density
    velocity = [(total(0) + PUSH_AXIAL) * inverse, total(1) * inverse, total(2) * inverse]
    speed_sq = velocity[0] * velocity[0] + velocity[1] * velocity[1] + velocity[2] * velocity[2]
    base = 1.0 - 1.5 * speed_sq
    weighted = {}
    for weight in sorted(set(WEIGHTS[:FLOWS])):
        weighted[weight] = (RELAX_FLOW * weight) * density

    def projected(member):
        result = None
        for component in range(3):
            factor = VELOCITIES[member][component]
            if factor == 0:
                continue
            if result is None:
                result = velocity[component] if factor > 0 else -velocity[component]
            else:
                result = result + velocity[component] if factor > 0 else result - velocity[component]
        return result

    results = [None] * FLOWS
    results[0] = (1.0 - RELAX_FLOW) * members[0] + weighted[WEIGHTS[0]] * base
    for first, second in PAIRS:
        along = projected(first)
        even = weighted[WEIGHTS[first]] * (base + 4.5 * along * along)
        odd = weighted[WEIGHTS[first]] * (3.0 * along)
        results[first] = (1.0 - RELAX_FLOW) * members[first] + (even + odd)
        results[second] = (1.0 - RELAX_FLOW) * members[second] + (even - odd)
    return results, velocity


def relax_drug(members, velocity):
    concentration = members[0]
    for member in members[1:]:
        concentration = concentration + member
    rest = (RELAX_DRUG * WEIGHTS[FLOWS]) * concentration
    results = [(1.0 - RELAX_DRUG) * members[0] + rest]
    even = (RELAX_DRUG * WEIGHTS[FLOWS + 1]) * concentration
    for component in range(3):
        odd = even * (4.0 * velocity[component])
        results.append((1.0 - RELAX_DRUG) * members[1 + 2 * component] + (even + odd))
        results.append((1.0 - RELAX_DRUG) * members[2 + 2 * component] + (even - odd))
    return results


def code_list(codes):
    return [codes[row:row + 1, :] for row in range(codes.shape[0])]


def pack_lines(row, width):
    return jnp.concatenate([row[:, start:start + width] for start in range(0, row.shape[-1], width)], axis=0)


def first_kernel(sectors, pops_ref, sector_ref, line_ref, strut_ref, free_ref, *refs):
    code_ref, boxes = refs[0], refs[1:1 + sectors]
    drug, sector, line, strut, top, sems = refs[1 + sectors:]
    across, width = code_ref.shape
    count = drug.shape[0]
    radial = pops_ref.shape[1]
    copies = [
        pltpu.make_async_copy(pops_ref.at[FLOWS:FLOWS + count, radial - 1], drug, sems.at[0]),
        pltpu.make_async_copy(sector_ref, sector, sems.at[1]),
        pltpu.make_async_copy(line_ref, line, sems.at[2]),
        pltpu.make_async_copy(strut_ref, strut, sems.at[3]),
        pltpu.make_async_copy(free_ref.at[0:across, :], top, sems.at[4]),
    ]
    for copy in copies:
        copy.start()
    for copy in copies:
        copy.wait()
    relative = sector[...] - lax.axis_index("th")
    relative = jnp.where(relative < 0, relative + sectors, relative)
    codes = relative * (across * width) + line[...]
    code_ref[...] = codes
    surface = drug[0]
    for member in range(1, count):
        surface = surface + drug[member]
    rows = code_list(codes)
    groups = sectors * across
    sums = scatter_rows(code_list(surface), rows, groups, width)
    counts = scatter_rows(code_list(jnp.ones_like(surface)), rows, groups, width)
    first = pack_lines(top[0:1, :], width)
    openness = PERMEABILITY * (1.0 - strut[...].astype(F32))
    for rel in range(sectors):
        out = boxes[rel]
        out[0:across] = sums[rel * across:(rel + 1) * across]
        out[across:2 * across] = counts[rel * across:(rel + 1) * across]
        out[2 * across:3 * across] = first
        out[3 * across:4 * across] = openness
        if rel in (1, sectors - 1):
            edge = codes[across - 1:across] if rel == 1 else codes[0:1]
            out[4 * across:5 * across] = jnp.broadcast_to(edge, (across, width)).astype(F32)


def bulk_kernel(first, packed, rims_too, radial, across, *refs):
    if rims_too:
        refs, rim_refs = refs[:-2], refs[-2:]
    if first:
        state_ref, post_ref, speed_ref = refs
    else:
        old_ref, inner_ref, outer_ref, state_ref, post_ref, speed_ref = refs
        old = Planes(old_ref, radial, across)
        behind, ahead = axial_rims(packed, inner_ref, outer_ref, across)
    state, post = Planes(state_ref, radial, across), Planes(post_ref, radial, across)
    for level in range(radial):
        if first:
            members = [state.get(member, level) for member in range(MEMBERS)]
        else:
            members = [streamed(old, member, level, behind, ahead) for member in range(MEMBERS)]
            for member in range(MEMBERS):
                state.put(member, level, members[member])
        results, velocity = relax_flow(members[:FLOWS])
        if level == radial - 1:
            for component in range(3):
                speed_ref[component * across:(component + 1) * across, :] = velocity[component]
        else:
            results = results + relax_drug(members[FLOWS:], velocity)
        for member, value in enumerate(results):
            post.put(member, level, value)
    if rims_too:
        for ref, slots, rising in ((rim_refs[0], RISE_SLOTS, True), (rim_refs[1], FALL_SLOTS, False)):
            for place, tile in enumerate(rim_tiles(post, slots, rising)):
                ref[place * across:(place + 1) * across, :] = tile


def slot_origin(column, along, rising):
    return along - 1 - column if rising else column


def rim_tiles(post, slots, rising):
    radial, across = post.radial, post.across
    along = post.ref.shape[-1]
    each = along // radial
    lane = lanes((across, along))
    tiles = []
    for place, (member, column) in enumerate(slots):
        if place % each == 0:
            tiles.append(jnp.zeros((across, along), F32))
        only_last = place == len(slots) - 1
        for level in range(radial - 1 if only_last else 0, radial - 1 if member >= FLOWS else radial):
            slot = (place % each) * radial + level
            value = pltpu.roll(post.get(member, level), (slot - slot_origin(column, along, rising)) % along, 1)
            tiles[-1] = jnp.where(lane == slot, value, tiles[-1])
    return tiles


def finished_tiles(ref, slots, rising, radial, across, drugs, fixed_rows):
    along = ref.shape[-1]
    each = along // radial
    lane, row = lanes((across, along)), sublanes((across, along))
    tiles = []
    for start in range(0, len(slots), each):
        tile = ref[(start // each) * across:(start // each + 1) * across, :]
        here = slots[start:start + each]
        for place, (member, column) in enumerate(here):
            if member >= FLOWS:
                slot = place * radial + radial - 1
                value = pltpu.roll(drugs[member - FLOWS], (slot - slot_origin(column, along, rising)) % along, 1)
                tile = jnp.where(lane == slot, value, tile)
        for side in sorted({side for side, _, _ in fixed_rows}):
            spread = jnp.zeros((across, along), F32)
            for other, level, blocks in fixed_rows:
                if other != side:
                    continue
                for place, (member, column) in enumerate(here):
                    origin = slot_origin(column, along, rising)
                    value = jnp.broadcast_to(blocks[member][:, origin:origin + 1], (across, along))
                    spread = jnp.where(lane - row == place * radial + level, value, spread)
            tile = jnp.where(row == side, jnp.sum(spread, axis=0, keepdims=True), tile)
        tiles.append(tile)
    return tiles


class Ghosts:
    def __init__(self, radial, across, along, behind, ahead, rise, fall):
        self.radial, self.across, self.along = radial, across, along
        self.behind, self.ahead, self.rise, self.fall = behind, ahead, rise, fall
        lane = lanes((across, along))
        self.is_behind = lane < radial
        self.level = jnp.where(self.is_behind, lane, lane - radial)

    def pick(self, message, slot, target):
        each = self.along // self.radial
        tile = message[(slot // each) * self.across:(slot // each + 1) * self.across, :]
        return pltpu.roll(tile, (target - (slot % each) * self.radial) % self.along, 1)

    def join(self, first, second):
        return jnp.where(self.is_behind, self.pick(*first, 0), self.pick(*second, self.radial))

    def arriving(self, member):
        step = VELOCITIES[member][0]
        rise, fall = RISE_SLOTS.index, FALL_SLOTS.index
        if step == 1:
            return self.join((self.behind, rise((member, 1))), (self.rise, rise((member, 0))))
        if step == -1:
            return self.join((self.fall, fall((member, 0))), (self.ahead, fall((member, 1))))
        return self.join((self.behind, rise((member, 0))), (self.ahead, fall((member, 0))))

    def own(self, member):
        return self.join((self.behind, RISE_SLOTS.index((member, 0))), (self.ahead, FALL_SLOTS.index((member, 0))))

    def risen(self, member):
        value = self.arriving(member)
        step = VELOCITIES[member][2]
        if step == 1:
            return jnp.where(self.level == 0, self.arriving(MIRROR[member]), pltpu.roll(value, 1, 1))
        if step == -1:
            return pltpu.roll(value, self.along - 1, 1)
        return value

    def streamed(self, member, below_rows, above_rows):
        value = self.risen(member)
        row = sublanes(value.shape)
        step = VELOCITIES[member][1]
        if step == 1:
            place = SECTOR_RISING.index(member)
            value = jnp.where(row == 0, below_rows[place:place + 1, :], pltpu.roll(value, 1, 0))
        elif step == -1:
            place = SECTOR_FALLING.index(member)
            value = jnp.where(row == self.across - 1, above_rows[place:place + 1, :], pltpu.roll(value, self.across - 1, 0))
        if VELOCITIES[member][2] == -1:
            value = jnp.where(self.level == self.radial - 1, self.own(OPPOSITE[member]), value)
        return value


def gather_cells(table, codes, width):
    group = codes // width
    low = codes - group * width
    row = jnp.zeros(codes.shape, F32)
    for place in range(table.shape[0]):
        row = jnp.where(group == place, table[place:place + 1, :], row)
    return jnp.sum(jnp.where(lanes(codes.shape) == low, row, 0.0), axis=1, keepdims=True)


def table_of(inbox, start, across):
    return jnp.concatenate([box[start:start + across, :] for box in inbox], axis=0)


def flux_kernel(sectors, step, radial, *refs):
    first, odd = step == 0, step % 2 == 1
    refs = list(refs)
    state_ref, bulk_ref, speed_ref, code_ref, strut_ref, coef_ref, on_ref, off_ref = refs[:8]
    inbox = refs[8:8 + sectors]
    refs = refs[8 + sectors:]
    open_ref = counts_ref = ghost_code_ref = ghost_open_ref = None
    if not first:
        open_ref, counts_ref = refs[:2]
        refs = refs[2:]
    if not odd:
        rim_refs, refs = refs[:2], refs[2:]
    if odd:
        sent_refs, got_refs = refs[:2], refs[2:4]
        refs = refs[4:]
        if step > 1:
            ghost_code_ref, ghost_open_ref = refs[:2]
            refs = refs[2:]
    last = step == STEPS - 1
    post_ref, one_ref, two_ref, added_ref = refs[:4]
    refs = refs[4:]
    if not last:
        top_ref, refs = refs[0], refs[1:]
    del bulk_ref
    across, along = code_ref.shape
    plane = (across, along)
    end = radial - 1
    state, post = Planes(state_ref, radial, across), Planes(post_ref, radial, across)
    codes = code_list(code_ref[...])
    below, above = inbox[sectors - 1], inbox[1]
    base = 2 * across if first else across
    picked = jnp.concatenate(gather_rows(table_of(inbox, base, across), codes, along), axis=0)
    if first:
        openness = jnp.concatenate(gather_rows(table_of(inbox, 3 * across, across), codes, along), axis=0)
        counts = inbox[0][across:2 * across, :]
        for box in inbox[1:]:
            counts = counts + box[across:2 * across, :]
        refs[0][...] = openness
        refs[1][...] = counts
        count, limit = across * along, sectors * across * along
        up = above[4 * across:5 * across, :].astype(jnp.int32) + count
        down = below[4 * across:5 * across, :].astype(jnp.int32) - count
        up = jnp.where(up >= limit, up - limit, up)
        down = jnp.where(down < 0, down + limit, down)
        refs[2][...] = jnp.where(sublanes(plane) == 0, up, down)
    else:
        openness, counts = open_ref[...], counts_ref[...]
    total = inbox[0][0:across, :]
    for box in inbox[1:]:
        total = total + box[0:across, :]
    strut = strut_ref[...].astype(F32)
    shut = PERMEABILITY * (1.0 - strut)
    added = shut * (total - counts * inbox[0][base:base + across, :]) + RELEASE_RATE * strut
    added_ref[...] = added
    if not last:
        free = coef_ref[0:across, :] + added * coef_ref[across:2 * across, :]
        bound = coef_ref[2 * across:3 * across, :] + added * coef_ref[3 * across:4 * across, :]
        top = free - (on_ref[0:1, 0:1] * free * (1.0 - bound) - off_ref[0:1, 0:1] * bound)
        top_ref[...] = top
    start = rims_start(step, across)
    row = sublanes(plane)
    drugs = [state.get(member, end) for member in range(FLOWS, MEMBERS)]
    if not first:
        place = start + SECTOR_RISING.index(FLOWS + 3) * radial + end
        drugs[3] = jnp.where(row == 0, below[place:place + 1, :], drugs[3])
        place = start + SECTOR_FALLING.index(FLOWS + 4) * radial + end
        drugs[4] = jnp.where(row == across - 1, above[place:place + 1, :], drugs[4])
    surface = drugs[0]
    for drug in drugs[1:]:
        surface = surface + drug
    flux = openness * (surface - picked)
    drugs = [drug - WEIGHTS[FLOWS + place] * flux for place, drug in enumerate(drugs)]
    velocity = [speed_ref[component * across:(component + 1) * across, :] for component in range(3)]
    drugs = relax_drug(drugs, velocity)
    for place, value in enumerate(drugs):
        post.put(FLOWS + place, end, value)
    fixed_rows = []
    if not first:
        block = across
        for side, box, places in ((0, below, SECTOR_RISING), (across - 1, above, SECTOR_FALLING)):
            moving = 1 if side == 0 else -1
            for level in range(0, radial, block):
                members = []
                for member in range(MEMBERS):
                    if VELOCITIES[member][1] == moving:
                        value = incoming_rows(box, start, places, state, member, level, block, side)
                    else:
                        value = state.rows(member, level, block, side)
                    if member >= FLOWS and level + block == radial:
                        lowered = value - WEIGHTS[member] * flux[side:side + 1, :]
                        value = jnp.where(sublanes(value.shape) == block - 1, lowered, value)
                    members.append(value)
                results, velocity = relax_flow(members[:FLOWS])
                results = results + relax_drug(members[FLOWS:], velocity)
                for member, value in enumerate(results):
                    post.put_rows(member, level, block, side, value)
                fixed_rows.append((side, level, results))
    if not odd:
        rise = finished_tiles(rim_refs[0], RISE_SLOTS, True, radial, across, drugs, fixed_rows) + [top]
        fall = finished_tiles(rim_refs[1], FALL_SLOTS, False, radial, across, drugs, fixed_rows) + [top]
        if first:
            own = code_ref[...].astype(F32)
            rise = rise + [shut, pltpu.roll(own, 1, 1)]
            fall = fall + [shut, own]
        for place, (up, down) in enumerate(zip(rise, fall, strict=True)):
            one_ref[place * across:(place + 1) * across, :] = by_parity(up, down)
            two_ref[place * across:(place + 1) * across, :] = by_parity(down, up)
        return
    rise, fall = by_parity(sent_refs[0][...], sent_refs[1][...]), by_parity(sent_refs[1][...], sent_refs[0][...])
    behind, ahead = by_parity(got_refs[1][...], got_refs[0][...]), by_parity(got_refs[0][...], got_refs[1][...])
    ghosts = Ghosts(radial, across, along, behind, ahead, rise, fall)
    tables = [table_of(inbox, (2 + side) * across, across) for side in range(2)]
    if step == 1:
        place = code_place(radial, across, along)
        sides = [message[place:place + across, 0:1].astype(jnp.int32) for message in (behind, ahead)]
        sides = [jnp.broadcast_to(side, plane) for side in sides]
        opens = [gather_cells(table_of(inbox, (4 + side) * across, across), sides[side], along) for side in range(2)]
        for side in range(2):
            refs[0][side * across:(side + 1) * across, :] = sides[side]
            refs[1][side * across:(side + 1) * across, :] = jnp.broadcast_to(opens[side], plane)
    else:
        sides = [ghost_code_ref[side * across:(side + 1) * across, :] for side in range(2)]
        opens = [ghost_open_ref[side * across:(side + 1) * across, 0:1] for side in range(2)]
    tops = [gather_cells(tables[side], sides[side], along) for side in range(2)]
    ghost_start = start + len(SECTOR_RISING) * radial
    below_rows = below[ghost_start:ghost_start + across, :]
    above_rows = above[ghost_start:ghost_start + across, :]
    members = [ghosts.streamed(member, below_rows, above_rows) for member in range(MEMBERS)]
    surface = members[FLOWS]
    for member in range(FLOWS + 1, MEMBERS):
        surface = surface + members[member]
    ghost_flux = jnp.where(ghosts.is_behind, opens[0] * (surface - tops[0]), opens[1] * (surface - tops[1]))
    ghost_flux = jnp.where(ghosts.level == end, ghost_flux, 0.0)
    members = members[:FLOWS] + [members[member] - WEIGHTS[member] * ghost_flux for member in range(FLOWS, MEMBERS)]
    results, velocity = relax_flow(members[:FLOWS])
    results = results + relax_drug(members[FLOWS:], velocity)
    lane = lanes(plane)
    behind, ahead = jnp.zeros(plane, F32), jnp.zeros(plane, F32)
    for place in range(len(SLAB_RISING)):
        here = (lane >= place * radial) & (lane < (place + 1) * radial)
        behind = jnp.where(here, pltpu.roll(results[SLAB_RISING[place]], (place * radial) % along, 1), behind)
        ahead = jnp.where(here, pltpu.roll(results[SLAB_FALLING[place]], ((place - 1) * radial) % along, 1), ahead)
    one_ref[...] = behind
    two_ref[...] = ahead


def code_place(radial, across, along):
    return (rim_rows(radial, across, along) // across + 2) * across


def rim_rows(radial, across, along):
    return -(-len(RISE_SLOTS) // (along // radial)) * across


def rims_start(step, across):
    return (6 if step == 1 else 4 if step % 2 else 2) * across


def wall_rates(spread_ref, on_ref, off_ref, width):
    depth = spread_ref.shape[0]
    shape = (depth, depth)
    rate_on = jnp.transpose(jnp.broadcast_to(on_ref[...], shape))[:, 0:1]
    rate_off = jnp.transpose(jnp.broadcast_to(off_ref[...], shape))[:, 0:1]
    top = jnp.transpose(jnp.broadcast_to(spread_ref[0:1, :], shape))[:, 0:1]
    return [jnp.broadcast_to(column, (depth, width)) for column in (rate_on, rate_off, spread_ref[:, 0:1], top)]


def split2(value):
    high = value.astype(BF16)
    return high, (value - high.astype(F32)).astype(BF16)


def left_terms(spread):
    high, low = split2(spread)
    return jnp.concatenate([high, high, low], axis=1)


def product(left, free):
    high, low = split2(free)
    return jnp.dot(left, jnp.concatenate([high, low, high], axis=0), preferred_element_type=F32)


def plan_ahead(left, rates, free, bound):
    rate_on, rate_off, entry, top = rates
    moved = product(left, free)
    room = rate_on * (1.0 - bound)
    rate = room * moved - rate_off * bound
    gain = room * entry
    first = jnp.sum(top * (moved - rate), axis=0, keepdims=True)
    slope = jnp.sum(top * (entry - gain), axis=0, keepdims=True)
    return moved, (first, slope, bound[0:1, :] + rate[0:1, :], gain[0:1, :])


def put_coefs(coef_ref, across, width, row, parts):
    for index, part in enumerate(parts):
        for step in range(part.shape[1] // width):
            place = index * across + row + step
            coef_ref[place:place + 1, :] = part[:, step * width:(step + 1) * width]


TOGETHER = 2


def plan_kernel(free_ref, bound_ref, spread_ref, on_ref, off_ref, moved_ref, coef_ref):
    width = coef_ref.shape[1]
    across = coef_ref.shape[0] // 4
    rates = wall_rates(spread_ref, on_ref, off_ref, TOGETHER * width)
    left = left_terms(spread_ref[...])
    for row in range(0, across, TOGETHER):
        place = slice(row * width, (row + TOGETHER) * width)
        moved, parts = plan_ahead(left, rates, free_ref[:, place], bound_ref[:, place])
        moved_ref[:, place] = moved
        put_coefs(coef_ref, across, width, row, parts)


def wall_kernel(last, moved_ref, bound_ref, added_ref, spread_ref, on_ref, off_ref, *outs):
    across, width = added_ref.shape
    rates = wall_rates(spread_ref, on_ref, off_ref, TOGETHER * width)
    rate_on, rate_off, entry, _ = rates
    left = left_terms(spread_ref[...])
    for row in range(0, across, TOGETHER):
        place = slice(row * width, (row + TOGETHER) * width)
        added = jnp.concatenate([added_ref[row + step:row + step + 1, :] for step in range(TOGETHER)], axis=1)
        free = moved_ref[:, place] + entry * added
        bound = bound_ref[:, place]
        for substep in range(SUB):
            if substep:
                free = product(left, free)
            rate = rate_on * free * (1.0 - bound) - rate_off * bound
            free = free - rate
            bound = bound + rate
        outs[1][:, place] = bound
        if last:
            outs[0][:, place] = free
        else:
            moved, parts = plan_ahead(left, rates, free, bound)
            outs[0][:, place] = moved
            put_coefs(outs[2], across, width, row, parts)


def send_kernel(sectors, step, radial, *refs):
    packed = step % 2 == 0
    post_ref, one_ref, two_ref, code_ref, edges_ref, top_ref = refs[:6]
    refs = refs[6:]
    if packed:
        sent_refs, outs = refs[:2], refs[2:]
    else:
        outs = refs
    across, along = code_ref.shape
    post = Planes(post_ref, radial, across)
    behind, ahead = axial_rims(packed, one_ref, two_ref, across)
    end = radial - 1
    row = sublanes((across, along))
    surface = post.get(FLOWS, end) + post.get(FLOWS + 5, end - 1) + post.get(FLOWS + 5, end)
    surface = surface + axial_shift(post.get(FLOWS + 1, end), 1, FLOWS + 1, end, radial, behind, ahead)
    surface = surface + axial_shift(post.get(FLOWS + 2, end), -1, FLOWS + 2, end, radial, behind, ahead)
    rising = post.get(FLOWS + 3, end)
    falling = post.get(FLOWS + 4, end)
    surface = surface + jnp.where(row == 0, 0.0, pltpu.roll(rising, 1, 0))
    surface = surface + jnp.where(row == across - 1, 0.0, pltpu.roll(falling, across - 1, 0))
    values = code_list(surface) + [rising[across - 1:across, :], falling[0:1, :]]
    codes = code_list(code_ref[...]) + [edges_ref[0:1, :], edges_ref[1:2, :]]
    sums = scatter_rows(values, codes, sectors * across, along)
    parts = [top_ref[...]]
    if packed:
        whole_behind = by_parity(two_ref[...], one_ref[...])
        whole_ahead = by_parity(one_ref[...], two_ref[...])
        skip = rim_rows(radial, across, along)
        for index in range(2 if step == 0 else 1):
            place = skip + index * across
            parts = parts + [whole_behind[place:place + across, :], whole_ahead[place:place + across, :]]
    for rel in range(sectors):
        outs[rel][0:across] = sums[rel * across:(rel + 1) * across]
        for index, part in enumerate(parts):
            outs[rel][(1 + index) * across:(2 + index) * across] = part
    start = rims_start(step + 1, across)
    for out, places, side in ((outs[1], SECTOR_RISING, across - 1), (outs[sectors - 1], SECTOR_FALLING, 0)):
        for place, member in enumerate(places):
            moving = VELOCITIES[member][0]
            base = start + place * radial
            if moving:
                out[base:base + radial, :] = axial_shift_rows(post, member, moving, side, behind, ahead)
            else:
                out[base:base + radial, :] = post.rows(member, 0, radial, side)
    if packed:
        rise, fall = by_parity(sent_refs[0][...], sent_refs[1][...]), by_parity(sent_refs[1][...], sent_refs[0][...])
        ghosts = Ghosts(radial, across, along, whole_behind, whole_ahead, rise, fall)
        base = start + len(SECTOR_RISING) * radial
        for out, places, side in ((outs[1], SECTOR_RISING, across - 1), (outs[sectors - 1], SECTOR_FALLING, 0)):
            for place, member in enumerate(places):
                out[base + place:base + place + 1, :] = ghosts.risen(member)[side:side + 1, :]
            for place in range(len(places), across):
                out[base + place:base + place + 1, :] = jnp.zeros((1, along), F32)


def last_send_kernel(radial, across, post_ref, inner_ref, outer_ref, up_ref, down_ref):
    post = Planes(post_ref, radial, across)
    behind, ahead = axial_rims(False, inner_ref, outer_ref, across)
    for out, drug, plus, minus, side in ((up_ref, FLOWS + 3, 7, 10, across - 1), (down_ref, FLOWS + 4, 9, 8, 0)):
        out[0:radial, :] = post.rows(drug, 0, radial, side)
        value = axial_shift_rows(post, plus, 1, side, behind, ahead)
        out[radial:2 * radial, :] = value - axial_shift_rows(post, minus, -1, side, behind, ahead)


def fields_kernel(radial, across, post_ref, inner_ref, outer_ref, drug_ref, flow_ref):
    post = Planes(post_ref, radial, across)
    behind, ahead = axial_rims(False, inner_ref, outer_ref, across)
    for level in range(radial):
        def member_of(member):
            value = streamed(post, member, level, behind, ahead)
            step = VELOCITIES[member][1]
            if step:
                edge = 0 if step > 0 else across - 1
                value = jnp.where(sublanes(value.shape) == edge, 0.0, value)
            return value

        drug = member_of(FLOWS)
        for member in range(FLOWS + 1, MEMBERS):
            drug = drug + member_of(member)
        drug_ref[level] = drug
        flow = None
        for member in range(FLOWS):
            factor = VELOCITIES[member][0]
            if factor:
                value = member_of(member)
                flow = (value if factor > 0 else -value) if flow is None else (flow + value if factor > 0 else flow - value)
        flow_ref[level] = flow


def last_kernel(drug_part, flow_part, below, above, drug_ref, flow_ref):
    radial, across, along = drug_ref.shape
    row = sublanes((across, along))
    for part, out, base in ((drug_part, drug_ref, 0), (flow_part, flow_ref, radial)):
        for level in range(radial):
            place = base + level
            value = part[level] + jnp.where(row == 0, below[place:place + 1, :], 0.0)
            out[level] = value + jnp.where(row == across - 1, above[place:place + 1, :], 0.0)


def kernel_call(body, outs, count, micros, aliases=None):
    shapes = [out if isinstance(out, jax.ShapeDtypeStruct) else jax.ShapeDtypeStruct(out, F32) for out in outs]
    return pl.pallas_call(
        body,
        out_shape=shapes,
        in_specs=[pl.BlockSpec(memory_space=VMEM)] * count,
        out_specs=[pl.BlockSpec(memory_space=VMEM)] * len(outs),
        input_output_aliases=aliases or {},
        cost_estimate=pl.CostEstimate(flops=0, bytes_accessed=int(micros * 3.0e6), transcendentals=0),
        compiler_params=pltpu.CompilerParams(vmem_limit_bytes=24 * 1024 * 1024),
    )


def first_call(sectors, populations, sector, line, strut, free):
    members, _, across, along = populations.shape
    plane = (across, along)
    sizes = [((5 if hop in (1, sectors - 1) else 4) * across, along) for hop in range(sectors)]
    return pl.pallas_call(
        functools.partial(first_kernel, sectors),
        name="first",
        out_shape=[jax.ShapeDtypeStruct(plane, jnp.int32)] + [jax.ShapeDtypeStruct(size, F32) for size in sizes],
        in_specs=[pl.BlockSpec(memory_space=pltpu.HBM)] * 5,
        out_specs=[pl.BlockSpec(memory_space=VMEM)] * (1 + sectors),
        scratch_shapes=[
            VMEM((members - FLOWS, across, along), F32),
            VMEM(plane, jnp.int32),
            VMEM(plane, jnp.int32),
            VMEM(plane, jnp.int32),
            VMEM((across, free.shape[1]), F32),
            pltpu.SemaphoreType.DMA((5,)),
        ],
        compiler_params=pltpu.CompilerParams(vmem_limit_bytes=24 * 1024 * 1024),
    )(*[pltpu.with_memory_space_constraint(x, pltpu.HBM) for x in (populations, sector, line, strut, free)])


def per_device(populations, wall_free, wall_bound, wall_propagator, bind_on, bind_off, iface_sector, iface_line, strut_mask):
    members, radial, across, along = populations.shape
    sectors = lax.axis_size("th")
    plane = (across, along)
    flat = (members * radial * across, along)
    rims = len(SECTOR_RISING) * radial
    strut = strut_mask.reshape(plane)
    rate_on = bind_on.reshape(1, -1)
    rate_off = bind_off.reshape(1, -1)

    def exchange(boxes):
        inbox = [boxes[0]] + [None] * (sectors - 1)
        for hop in range(1, sectors):
            inbox[sectors - hop] = shifted(boxes[hop], "th", hop)
        return inbox

    codes, *boxes = first_call(sectors, populations, iface_sector.reshape(plane), iface_line.reshape(plane), strut, wall_free)
    inbox = exchange(boxes)
    state = populations.reshape(flat)
    speeds = (3 * across, along)
    four = (4 * across, along)
    two = (2 * across, along)
    rim = rim_rows(radial, across, along)
    shapes = wall_free.shape
    bulk, speed, *tiles = kernel_call(
        functools.partial(bulk_kernel, True, True, True, radial, across), [flat, speeds, (rim, along), (rim, along)], 1, 1.5
    )(state)
    moved, coefs = kernel_call(plan_kernel, [shapes, four], 5, 1.0)(
        wall_free, wall_bound, wall_propagator, rate_on, rate_off
    )
    bound = wall_bound
    fixed, ghost = [], []
    edges = sent = got = None
    for step in range(STEPS):
        odd, last = step % 2 == 1, step == STEPS - 1
        if odd:
            pair = [plane, plane]
        else:
            pair = [(rim + (3 if step == 0 else 1) * across, along)] * 2
        outs = [flat] + pair + [plane] * (1 if last else 2)
        if step == 0:
            outs = outs + [plane, plane, jax.ShapeDtypeStruct(plane, jnp.int32)]
        if step == 1:
            outs = outs + [jax.ShapeDtypeStruct(two, jnp.int32), two]
        extra = fixed + ([*sent, *got, *ghost] if odd else tiles)
        post, one, other, added, *rest = kernel_call(
            functools.partial(flux_kernel, sectors, step, radial), outs, 8 + sectors + len(extra), 0.8, {1: 0}
        )(state, bulk, speed, codes, strut, coefs, rate_on, rate_off, *inbox, *extra)
        if not last:
            top, *rest = rest
        if step == 0:
            fixed, edges = rest[:2], rest[2]
        if step == 1:
            ghost = rest
        if odd:
            rims_in, own = [one, other], []
        else:
            sent = [one, other]
            got = paired(*sent)
            rims_in, own = [*got], sent
        results = kernel_call(
            functools.partial(wall_kernel, last), [shapes, shapes] + ([] if last else [four]), 6, 1.5
        )(moved, bound, added, wall_propagator, rate_on, rate_off)
        if last:
            free, bound = results
            continue
        moved, bound, coefs = results
        start = rims_start(step + 1, across)
        long = start + rims + (0 if odd else across)
        sizes = [(long if hop in (1, sectors - 1) else start, along) for hop in range(sectors)]
        boxes = kernel_call(
            functools.partial(send_kernel, sectors, step, radial), sizes, 6 + len(own), 0.3
        )(post, *rims_in, codes, edges, top, *own)
        inbox = exchange(boxes)
        outs = [flat, flat, speeds] + ([(rim, along)] * 2 if odd else [])
        state, bulk, speed, *tiles = kernel_call(
            functools.partial(bulk_kernel, False, not odd, odd, radial, across), outs, 3, 2.0
        )(post, *rims_in)
    up, down = kernel_call(
        functools.partial(last_send_kernel, radial, across), [(2 * radial, along)] * 2, 3, 0.2
    )(post, *rims_in)
    below = shifted(up, "th", 1)
    above = shifted(down, "th", -1)
    parts = kernel_call(
        functools.partial(fields_kernel, radial, across), [(radial,) + plane] * 2, 3, 1.0
    )(post, *rims_in)
    drug_field, axial_flow = kernel_call(last_kernel, [(radial,) + plane] * 2, 4, 0.3)(*parts, below, above)
    return drug_field, axial_flow, free, bound


def solution(mesh):
    placed = (
        P(None, None, "th", "ax"),
        P(None, ("ax", "th")),
        P(None, ("ax", "th")),
        P(),
        P(),
        P(),
        P(("ax", "th"), None),
        P(("ax", "th")),
        P(("ax", "th")),
    )
    return jax.shard_map(
        per_device,
        mesh=mesh,
        in_specs=placed,
        out_specs=(
            P(None, "th", "ax"),
            P(None, "th", "ax"),
            P(None, ("ax", "th")),
            P(None, ("ax", "th")),
        ),
        check_vma=False,
    )
```

```python
import functools

import jax
import jax.numpy as jnp
from jax import lax
from jax.experimental import pallas as pl
from jax.experimental.pallas import tpu as pltpu
from jax.sharding import PartitionSpec as P


STEPS = 4
SUB = 2

VELOCITIES = [
    (0, 0, 0), (1, 0, 0), (-1, 0, 0), (0, 1, 0), (0, -1, 0), (0, 0, 1), (0, 0, -1),
    (1, 1, 0), (-1, -1, 0), (1, -1, 0), (-1, 1, 0),
    (1, 0, 1), (-1, 0, -1), (1, 0, -1), (-1, 0, 1),
    (0, 1, 1), (0, -1, -1), (0, 1, -1), (0, -1, 1),
    (0, 0, 0), (1, 0, 0), (-1, 0, 0), (0, 1, 0), (0, -1, 0), (0, 0, 1), (0, 0, -1),
]
WEIGHTS = [1.0 / 3.0] + [1.0 / 18.0] * 6 + [1.0 / 36.0] * 12 + [0.25] + [0.125] * 6
OPPOSITE = [0, 2, 1, 4, 3, 6, 5, 8, 7, 10, 9, 12, 11, 14, 13, 16, 15, 18, 17, 19, 21, 20, 23, 22, 25, 24]
MIRROR = [0, 1, 2, 3, 4, 6, 5, 7, 8, 9, 10, 13, 14, 11, 12, 17, 18, 15, 16, 19, 20, 21, 22, 23, 25, 24]
SECTOR_RISING = [3, 7, 10, 15, 17, 22]
SECTOR_FALLING = [4, 8, 9, 16, 18, 23]
SLAB_RISING = [1, 7, 9, 11, 13, 20]
SLAB_FALLING = [2, 8, 10, 12, 14, 21]
LEVEL_KEPT = [0, 3, 4, 5, 6, 15, 16, 17, 18, 19, 22, 23, 24, 25]
RISE_SLOTS = [(m, 0) for m in SLAB_RISING] + [(m, 0) for m in LEVEL_KEPT] + [(m, 1) for m in SLAB_RISING] + [(14, 0)]
FALL_SLOTS = [(m, 0) for m in SLAB_FALLING] + [(m, 0) for m in LEVEL_KEPT] + [(m, 1) for m in SLAB_FALLING] + [(11, 0)]
PAIRS = [(1, 2), (3, 4), (5, 6), (7, 8), (9, 10), (11, 12), (13, 14), (15, 16), (17, 18)]
FLOWS = 19
MEMBERS = 26
RELAX_FLOW = 1.25
RELAX_DRUG = 1.1
PUSH_AXIAL = 0.0001
PERMEABILITY = 0.3
RELEASE_RATE = 0.5

F32 = jnp.float32
BF16 = jnp.bfloat16
VMEM = pltpu.VMEM


def shifted(block, axis, distance):
    count = lax.axis_size(axis)
    return lax.ppermute(block, axis, [((i - distance) % count, i) for i in range(count)])


def paired(inner, outer):
    count = lax.axis_size("ax")
    near = [(i, i ^ 1) for i in range(count)]
    far = [(i, (i + 1) % count if i % 2 else (i - 1) % count) for i in range(count)]
    return lax.ppermute(inner, "ax", near), lax.ppermute(outer, "ax", far)


def by_parity(even, odd):
    return jnp.where(lax.axis_index("ax") % 2 == 0, even, odd)


def axial_rims(packed, first_ref, second_ref, across):
    first, second = first_ref[0:across, :], second_ref[0:across, :]
    if not packed:
        return first, second
    return by_parity(second, first), by_parity(first, second)


def lanes(shape):
    return lax.broadcasted_iota(jnp.int32, shape, len(shape) - 1)


def sublanes(shape):
    return lax.broadcasted_iota(jnp.int32, shape, len(shape) - 2)


def split3(value):
    high = value.astype(BF16)
    rest = value - high.astype(F32)
    middle = rest.astype(BF16)
    low = (rest - middle.astype(F32)).astype(BF16)
    return high, middle, low


def one_hot_lines(low_row, width):
    shape = (width, low_row.shape[-1])
    return jnp.where(sublanes(shape) == low_row, 1.0, 0.0).astype(BF16)


def scatter_rows(value_rows, code_rows, groups, width, counted=False):
    terms, hots = [], []
    for value, code in zip(value_rows, code_rows, strict=True):
        group = code // width
        hit = sublanes((groups, value.shape[-1])) == group
        parts = [part.astype(F32) for part in split3(value)] + ([jnp.ones_like(value)] if counted else [])
        terms.append(jnp.concatenate([jnp.where(hit, part, 0.0) for part in parts], axis=0).astype(BF16))
        hots.append(one_hot_lines(code - group * width, width))
    left = jnp.concatenate(terms, axis=1)
    right = jnp.concatenate(hots, axis=1)
    total = lax.dot_general(left, right, (((1,), (1,)), ((), ())), preferred_element_type=F32)
    sums = total[:groups] + total[groups:2 * groups] + total[2 * groups:3 * groups]
    return (sums, total[3 * groups:]) if counted else sums


def gather_rows(table, code_rows, width):
    groups = table.shape[0]
    left = jnp.concatenate(split3(table), axis=0)
    lows = [code - (code // width) * width for code in code_rows]
    right = jnp.concatenate([one_hot_lines(low, width) for low in lows], axis=1)
    picked = jnp.dot(left, right, preferred_element_type=F32)
    picked = picked[:groups] + picked[groups:2 * groups] + picked[2 * groups:3 * groups]
    results, start = [], 0
    for code in code_rows:
        count = code.shape[-1]
        hit = sublanes((groups, count)) == code // width
        results.append(jnp.sum(jnp.where(hit, picked[:, start:start + count], 0.0), axis=0, keepdims=True))
        start += count
    return results


def source_plane(member, level, radial):
    step_r = VELOCITIES[member][2]
    if step_r == 1:
        return ((MIRROR[member], 0) if level == 0 else (member, level - 1)), True
    if step_r == -1:
        return ((OPPOSITE[member], radial - 1), False) if level == radial - 1 else ((member, level + 1), True)
    return (member, level), True


class Planes:
    def __init__(self, ref, radial, across):
        self.ref, self.radial, self.across = ref, radial, across

    def base(self, member, level):
        return (member * self.radial + level) * self.across

    def get(self, member, level):
        return self.ref[pl.ds(self.base(member, level), self.across), :]

    def put(self, member, level, value):
        self.ref[pl.ds(self.base(member, level), self.across), :] = value

    def rows(self, member, level, count, row):
        return self.ref[pl.ds(self.base(member, level) + row, count, stride=self.across), :]

    def put_rows(self, member, level, count, row, value):
        self.ref[pl.ds(self.base(member, level) + row, count, stride=self.across), :] = value


def axial_shift(value, step, member, level, radial, behind, ahead):
    along = value.shape[-1]
    lane = lanes(value.shape)
    if step == 1:
        slot = SLAB_RISING.index(member) * radial + level
        return jnp.where(lane == 0, pltpu.roll(behind, (-slot) % along, 1), pltpu.roll(value, 1, 1))
    slot = SLAB_FALLING.index(member) * radial + level
    return jnp.where(lane == along - 1, pltpu.roll(ahead, (along - 1 - slot) % along, 1), pltpu.roll(value, along - 1, 1))


def axial_shift_rows(post, member, step, side, behind, ahead):
    value = post.rows(member, 0, post.radial, side)
    along = value.shape[-1]
    tile, slots = (behind, SLAB_RISING) if step == 1 else (ahead, SLAB_FALLING)
    lane = lanes(value.shape)
    here = lane - sublanes(value.shape) == slots.index(member) * post.radial
    column = jnp.sum(jnp.where(here, tile[side:side + 1, :], 0.0), axis=1, keepdims=True)
    return jnp.where(lane == (0 if step == 1 else along - 1), column, pltpu.roll(value, step % along, 1))


def streamed(post, member, level, behind, ahead):
    radial, across = post.radial, post.across
    (origin, depth), moves = source_plane(member, level, radial)
    value = post.get(origin, depth)
    if not moves:
        return value
    step_z, step_s, _ = VELOCITIES[member]
    if step_z:
        value = axial_shift(value, step_z, origin, depth, radial, behind, ahead)
    if step_s:
        value = pltpu.roll(value, step_s % across, 0)
    return value


def incoming_rows(box, start, places, state, member, level, count, row):
    radial = state.radial
    step_r = VELOCITIES[member][2]
    here = start + places.index(member) * radial + level
    value = box[here - step_r:here - step_r + count, :]
    if step_r == 1 and level == 0:
        mirrored = start + places.index(MIRROR[member]) * radial
        value = jnp.where(sublanes(value.shape) == 0, box[mirrored:mirrored + 1, :], value)
    if step_r == -1 and level + count == radial:
        value = jnp.where(sublanes(value.shape) == count - 1, state.rows(member, level, count, row), value)
    return value


def relax_flow(members):
    def total(component):
        up, down = None, None
        for member in range(1, FLOWS):
            factor = VELOCITIES[member][component]
            if factor > 0:
                up = members[member] if up is None else up + members[member]
            elif factor < 0:
                down = members[member] if down is None else down + members[member]
        return up - down

    density = members[0]
    for member in range(1, FLOWS):
        density = density + members[member]
    inverse = 1.0 / density
    velocity = [(total(0) + PUSH_AXIAL) * inverse, total(1) * inverse, total(2) * inverse]
    speed_sq = velocity[0] * velocity[0] + velocity[1] * velocity[1] + velocity[2] * velocity[2]
    base = 1.0 - 1.5 * speed_sq
    weighted = {}
    for weight in sorted(set(WEIGHTS[:FLOWS])):
        weighted[weight] = (RELAX_FLOW * weight) * density

    def projected(member):
        result = None
        for component in range(3):
            factor = VELOCITIES[member][component]
            if factor == 0:
                continue
            if result is None:
                result = velocity[component] if factor > 0 else -velocity[component]
            else:
                result = result + velocity[component] if factor > 0 else result - velocity[component]
        return result

    results = [None] * FLOWS
    results[0] = (1.0 - RELAX_FLOW) * members[0] + weighted[WEIGHTS[0]] * base
    for first, second in PAIRS:
        along = projected(first)
        even = weighted[WEIGHTS[first]] * (base + 4.5 * along * along)
        odd = weighted[WEIGHTS[first]] * (3.0 * along)
        results[first] = (1.0 - RELAX_FLOW) * members[first] + (even + odd)
        results[second] = (1.0 - RELAX_FLOW) * members[second] + (even - odd)
    return results, velocity


def relax_drug(members, velocity):
    concentration = members[0]
    for member in members[1:]:
        concentration = concentration + member
    rest = (RELAX_DRUG * WEIGHTS[FLOWS]) * concentration
    results = [(1.0 - RELAX_DRUG) * members[0] + rest]
    even = (RELAX_DRUG * WEIGHTS[FLOWS + 1]) * concentration
    for component in range(3):
        odd = even * (4.0 * velocity[component])
        results.append((1.0 - RELAX_DRUG) * members[1 + 2 * component] + (even + odd))
        results.append((1.0 - RELAX_DRUG) * members[2 + 2 * component] + (even - odd))
    return results


def code_list(codes):
    return [codes[row:row + 1, :] for row in range(codes.shape[0])]


def pack_lines(row, width):
    return jnp.concatenate([row[:, start:start + width] for start in range(0, row.shape[-1], width)], axis=0)


def first_kernel(sectors, pops_ref, sector_ref, line_ref, strut_ref, free_ref, *refs):
    code_ref, boxes = refs[0], refs[1:1 + sectors]
    drug, sector, line, strut, top, sems = refs[1 + sectors:]
    across, width = code_ref.shape
    count = drug.shape[0]
    radial = pops_ref.shape[1]
    copies = [
        pltpu.make_async_copy(pops_ref.at[FLOWS:FLOWS + count, radial - 1], drug, sems.at[0]),
        pltpu.make_async_copy(sector_ref, sector, sems.at[1]),
        pltpu.make_async_copy(line_ref, line, sems.at[2]),
        pltpu.make_async_copy(strut_ref, strut, sems.at[3]),
        pltpu.make_async_copy(free_ref.at[0:across, :], top, sems.at[4]),
    ]
    for copy in copies:
        copy.start()
    for copy in copies:
        copy.wait()
    relative = sector[...] - lax.axis_index("th")
    relative = jnp.where(relative < 0, relative + sectors, relative)
    codes = relative * (across * width) + line[...]
    code_ref[...] = codes
    surface = drug[0]
    for member in range(1, count):
        surface = surface + drug[member]
    rows = code_list(codes)
    groups = sectors * across
    sums, counts = scatter_rows(code_list(surface), rows, groups, width, counted=True)
    first = pack_lines(top[0:1, :], width)
    openness = PERMEABILITY * (1.0 - strut[...].astype(F32))
    for rel in range(sectors):
        out = boxes[rel]
        out[0:across] = sums[rel * across:(rel + 1) * across]
        out[across:2 * across] = counts[rel * across:(rel + 1) * across]
        out[2 * across:3 * across] = first
        out[3 * across:4 * across] = openness
        if rel in (1, sectors - 1):
            edge = codes[across - 1:across] if rel == 1 else codes[0:1]
            out[4 * across:5 * across] = jnp.broadcast_to(edge, (across, width)).astype(F32)


def bulk_kernel(first, packed, rims_too, radial, across, *refs):
    if rims_too:
        refs, rim_refs = refs[:-2], refs[-2:]
    if first:
        state_ref, post_ref, speed_ref = refs
    else:
        old_ref, inner_ref, outer_ref, state_ref, post_ref, speed_ref = refs
        old = Planes(old_ref, radial, across)
        behind, ahead = axial_rims(packed, inner_ref, outer_ref, across)
    state, post = Planes(state_ref, radial, across), Planes(post_ref, radial, across)
    for level in range(radial):
        if first:
            members = [state.get(member, level) for member in range(MEMBERS)]
        else:
            members = [streamed(old, member, level, behind, ahead) for member in range(MEMBERS)]
            for member in range(MEMBERS):
                state.put(member, level, members[member])
        results, velocity = relax_flow(members[:FLOWS])
        if level == radial - 1:
            for component in range(3):
                speed_ref[component * across:(component + 1) * across, :] = velocity[component]
        else:
            results = results + relax_drug(members[FLOWS:], velocity)
        for member, value in enumerate(results):
            post.put(member, level, value)
    if rims_too:
        for ref, slots, rising in ((rim_refs[0], RISE_SLOTS, True), (rim_refs[1], FALL_SLOTS, False)):
            for place, tile in enumerate(rim_tiles(post, slots, rising)):
                ref[place * across:(place + 1) * across, :] = tile


def slot_origin(column, along, rising):
    return along - 1 - column if rising else column


def rim_tiles(post, slots, rising):
    radial, across = post.radial, post.across
    along = post.ref.shape[-1]
    each = along // radial
    lane = lanes((across, along))
    tiles = []
    for place, (member, column) in enumerate(slots):
        if place % each == 0:
            tiles.append(jnp.zeros((across, along), F32))
        only_last = place == len(slots) - 1
        for level in range(radial - 1 if only_last else 0, radial - 1 if member >= FLOWS else radial):
            slot = (place % each) * radial + level
            value = pltpu.roll(post.get(member, level), (slot - slot_origin(column, along, rising)) % along, 1)
            tiles[-1] = jnp.where(lane == slot, value, tiles[-1])
    return tiles


def finished_tiles(ref, slots, rising, radial, across, drugs, fixed_rows):
    along = ref.shape[-1]
    each = along // radial
    lane, row = lanes((across, along)), sublanes((across, along))
    tiles = []
    for start in range(0, len(slots), each):
        tile = ref[(start // each) * across:(start // each + 1) * across, :]
        here = slots[start:start + each]
        for place, (member, column) in enumerate(here):
            if member >= FLOWS:
                slot = place * radial + radial - 1
                value = pltpu.roll(drugs[member - FLOWS], (slot - slot_origin(column, along, rising)) % along, 1)
                tile = jnp.where(lane == slot, value, tile)
        for side in sorted({side for side, _, _ in fixed_rows}):
            spread = jnp.zeros((across, along), F32)
            for other, level, blocks in fixed_rows:
                if other != side:
                    continue
                for place, (member, column) in enumerate(here):
                    origin = slot_origin(column, along, rising)
                    value = jnp.broadcast_to(blocks[member][:, origin:origin + 1], (across, along))
                    spread = jnp.where(lane - row == place * radial + level, value, spread)
            tile = jnp.where(row == side, jnp.sum(spread, axis=0, keepdims=True), tile)
        tiles.append(tile)
    return tiles


class Ghosts:
    def __init__(self, radial, across, along, behind, ahead, rise, fall):
        self.radial, self.across, self.along = radial, across, along
        self.behind, self.ahead, self.rise, self.fall = behind, ahead, rise, fall
        lane = lanes((across, along))
        self.is_behind = lane < radial
        self.level = jnp.where(self.is_behind, lane, lane - radial)

    def pick(self, message, slot, target):
        each = self.along // self.radial
        tile = message[(slot // each) * self.across:(slot // each + 1) * self.across, :]
        return pltpu.roll(tile, (target - (slot % each) * self.radial) % self.along, 1)

    def join(self, first, second):
        return jnp.where(self.is_behind, self.pick(*first, 0), self.pick(*second, self.radial))

    def arriving(self, member):
        step = VELOCITIES[member][0]
        rise, fall = RISE_SLOTS.index, FALL_SLOTS.index
        if step == 1:
            return self.join((self.behind, rise((member, 1))), (self.rise, rise((member, 0))))
        if step == -1:
            return self.join((self.fall, fall((member, 0))), (self.ahead, fall((member, 1))))
        return self.join((self.behind, rise((member, 0))), (self.ahead, fall((member, 0))))

    def own(self, member):
        return self.join((self.behind, RISE_SLOTS.index((member, 0))), (self.ahead, FALL_SLOTS.index((member, 0))))

    def risen(self, member):
        value = self.arriving(member)
        step = VELOCITIES[member][2]
        if step == 1:
            return jnp.where(self.level == 0, self.arriving(MIRROR[member]), pltpu.roll(value, 1, 1))
        if step == -1:
            return pltpu.roll(value, self.along - 1, 1)
        return value

    def streamed(self, member, below_rows, above_rows):
        value = self.risen(member)
        row = sublanes(value.shape)
        step = VELOCITIES[member][1]
        if step == 1:
            place = SECTOR_RISING.index(member)
            value = jnp.where(row == 0, below_rows[place:place + 1, :], pltpu.roll(value, 1, 0))
        elif step == -1:
            place = SECTOR_FALLING.index(member)
            value = jnp.where(row == self.across - 1, above_rows[place:place + 1, :], pltpu.roll(value, self.across - 1, 0))
        if VELOCITIES[member][2] == -1:
            value = jnp.where(self.level == self.radial - 1, self.own(OPPOSITE[member]), value)
        return value


def gather_cells(table, codes, width):
    group = codes // width
    low = codes - group * width
    row = jnp.zeros(codes.shape, F32)
    for place in range(table.shape[0]):
        row = jnp.where(group == place, table[place:place + 1, :], row)
    return jnp.sum(jnp.where(lanes(codes.shape) == low, row, 0.0), axis=1, keepdims=True)


def table_of(inbox, start, across):
    return jnp.concatenate([box[start:start + across, :] for box in inbox], axis=0)


def flux_kernel(sectors, step, radial, *refs):
    first, odd = step == 0, step % 2 == 1
    refs = list(refs)
    state_ref, bulk_ref, speed_ref, code_ref, strut_ref, coef_ref, on_ref, off_ref = refs[:8]
    inbox = refs[8:8 + sectors]
    refs = refs[8 + sectors:]
    open_ref = counts_ref = ghost_code_ref = ghost_open_ref = None
    if not first:
        open_ref, counts_ref = refs[:2]
        refs = refs[2:]
    if not odd:
        rim_refs, refs = refs[:2], refs[2:]
    if odd:
        sent_refs, got_refs = refs[:2], refs[2:4]
        refs = refs[4:]
        if step > 1:
            ghost_code_ref, ghost_open_ref = refs[:2]
            refs = refs[2:]
    last = step == STEPS - 1
    post_ref, one_ref, two_ref, added_ref = refs[:4]
    refs = refs[4:]
    if not last:
        top_ref, refs = refs[0], refs[1:]
    del bulk_ref
    across, along = code_ref.shape
    plane = (across, along)
    end = radial - 1
    state, post = Planes(state_ref, radial, across), Planes(post_ref, radial, across)
    codes = code_list(code_ref[...])
    below, above = inbox[sectors - 1], inbox[1]
    base = 2 * across if first else across
    picked = jnp.concatenate(gather_rows(table_of(inbox, base, across), codes, along), axis=0)
    if first:
        openness = jnp.concatenate(gather_rows(table_of(inbox, 3 * across, across), codes, along), axis=0)
        counts = inbox[0][across:2 * across, :]
        for box in inbox[1:]:
            counts = counts + box[across:2 * across, :]
        refs[0][...] = openness
        refs[1][...] = counts
        count, limit = across * along, sectors * across * along
        up = above[4 * across:5 * across, :].astype(jnp.int32) + count
        down = below[4 * across:5 * across, :].astype(jnp.int32) - count
        up = jnp.where(up >= limit, up - limit, up)
        down = jnp.where(down < 0, down + limit, down)
        refs[2][...] = jnp.where(sublanes(plane) == 0, up, down)
    else:
        openness, counts = open_ref[...], counts_ref[...]
    total = inbox[0][0:across, :]
    for box in inbox[1:]:
        total = total + box[0:across, :]
    strut = strut_ref[...].astype(F32)
    shut = PERMEABILITY * (1.0 - strut)
    added = shut * (total - counts * inbox[0][base:base + across, :]) + RELEASE_RATE * strut
    added_ref[...] = added
    if not last:
        free = coef_ref[0:across, :] + added * coef_ref[across:2 * across, :]
        bound = coef_ref[2 * across:3 * across, :] + added * coef_ref[3 * across:4 * across, :]
        top = free - (on_ref[0:1, 0:1] * free * (1.0 - bound) - off_ref[0:1, 0:1] * bound)
        top_ref[...] = top
    start = rims_start(step, across)
    row = sublanes(plane)
    drugs = [state.get(member, end) for member in range(FLOWS, MEMBERS)]
    if not first:
        place = start + SECTOR_RISING.index(FLOWS + 3) * radial + end
        drugs[3] = jnp.where(row == 0, below[place:place + 1, :], drugs[3])
        place = start + SECTOR_FALLING.index(FLOWS + 4) * radial + end
        drugs[4] = jnp.where(row == across - 1, above[place:place + 1, :], drugs[4])
    surface = drugs[0]
    for drug in drugs[1:]:
        surface = surface + drug
    flux = openness * (surface - picked)
    drugs = [drug - WEIGHTS[FLOWS + place] * flux for place, drug in enumerate(drugs)]
    velocity = [speed_ref[component * across:(component + 1) * across, :] for component in range(3)]
    drugs = relax_drug(drugs, velocity)
    for place, value in enumerate(drugs):
        post.put(FLOWS + place, end, value)
    fixed_rows = []
    if not first:
        block = across
        for side, box, places in ((0, below, SECTOR_RISING), (across - 1, above, SECTOR_FALLING)):
            moving = 1 if side == 0 else -1
            for level in range(0, radial, block):
                members = []
                for member in range(MEMBERS):
                    if VELOCITIES[member][1] == moving:
                        value = incoming_rows(box, start, places, state, member, level, block, side)
                    else:
                        value = state.rows(member, level, block, side)
                    if member >= FLOWS and level + block == radial:
                        lowered = value - WEIGHTS[member] * flux[side:side + 1, :]
                        value = jnp.where(sublanes(value.shape) == block - 1, lowered, value)
                    members.append(value)
                results, velocity = relax_flow(members[:FLOWS])
                results = results + relax_drug(members[FLOWS:], velocity)
                for member, value in enumerate(results):
                    post.put_rows(member, level, block, side, value)
                fixed_rows.append((side, level, results))
    if not odd:
        rise = finished_tiles(rim_refs[0], RISE_SLOTS, True, radial, across, drugs, fixed_rows) + [top]
        fall = finished_tiles(rim_refs[1], FALL_SLOTS, False, radial, across, drugs, fixed_rows) + [top]
        if first:
            own = code_ref[...].astype(F32)
            spare, free_lane = len(rise) - 2, lanes(plane) == along - 1
            rise[spare] = jnp.where(free_lane, own, rise[spare])
            fall[spare] = jnp.where(free_lane, pltpu.roll(own, along - 1, 1), fall[spare])
            rise, fall = rise + [shut], fall + [shut]
        for place, (up, down) in enumerate(zip(rise, fall, strict=True)):
            one_ref[place * across:(place + 1) * across, :] = by_parity(up, down)
            two_ref[place * across:(place + 1) * across, :] = by_parity(down, up)
        return
    rise, fall = by_parity(sent_refs[0][...], sent_refs[1][...]), by_parity(sent_refs[1][...], sent_refs[0][...])
    behind, ahead = by_parity(got_refs[1][...], got_refs[0][...]), by_parity(got_refs[0][...], got_refs[1][...])
    ghosts = Ghosts(radial, across, along, behind, ahead, rise, fall)
    tables = [table_of(inbox, (2 + side) * across, across) for side in range(2)]
    if step == 1:
        place = code_place(radial, across, along)
        sides = [message[place:place + across, along - 1:along].astype(jnp.int32) for message in (behind, ahead)]
        sides = [jnp.broadcast_to(side, plane) for side in sides]
        opens = [gather_cells(table_of(inbox, (4 + side) * across, across), sides[side], along) for side in range(2)]
        for side in range(2):
            refs[0][side * across:(side + 1) * across, :] = sides[side]
            refs[1][side * across:(side + 1) * across, :] = jnp.broadcast_to(opens[side], plane)
    else:
        sides = [ghost_code_ref[side * across:(side + 1) * across, :] for side in range(2)]
        opens = [ghost_open_ref[side * across:(side + 1) * across, 0:1] for side in range(2)]
    tops = [gather_cells(tables[side], sides[side], along) for side in range(2)]
    ghost_start = start + len(SECTOR_RISING) * radial
    below_rows = below[ghost_start:ghost_start + across, :]
    above_rows = above[ghost_start:ghost_start + across, :]
    members = [ghosts.streamed(member, below_rows, above_rows) for member in range(MEMBERS)]
    surface = members[FLOWS]
    for member in range(FLOWS + 1, MEMBERS):
        surface = surface + members[member]
    ghost_flux = jnp.where(ghosts.is_behind, opens[0] * (surface - tops[0]), opens[1] * (surface - tops[1]))
    ghost_flux = jnp.where(ghosts.level == end, ghost_flux, 0.0)
    members = members[:FLOWS] + [members[member] - WEIGHTS[member] * ghost_flux for member in range(FLOWS, MEMBERS)]
    results, velocity = relax_flow(members[:FLOWS])
    results = results + relax_drug(members[FLOWS:], velocity)
    lane = lanes(plane)
    behind, ahead = jnp.zeros(plane, F32), jnp.zeros(plane, F32)
    for place in range(len(SLAB_RISING)):
        here = (lane >= place * radial) & (lane < (place + 1) * radial)
        behind = jnp.where(here, pltpu.roll(results[SLAB_RISING[place]], (place * radial) % along, 1), behind)
        ahead = jnp.where(here, pltpu.roll(results[SLAB_FALLING[place]], ((place - 1) * radial) % along, 1), ahead)
    one_ref[...] = behind
    two_ref[...] = ahead


def code_place(radial, across, along):
    return rim_rows(radial, across, along) - across


def rim_rows(radial, across, along):
    return -(-len(RISE_SLOTS) // (along // radial)) * across


def rims_start(step, across):
    return (6 if step == 1 else 4 if step % 2 else 2) * across


def wall_rates(spread_ref, on_ref, off_ref, width):
    depth = spread_ref.shape[0]
    shape = (depth, depth)
    rate_on = jnp.transpose(jnp.broadcast_to(on_ref[...], shape))[:, 0:1]
    rate_off = jnp.transpose(jnp.broadcast_to(off_ref[...], shape))[:, 0:1]
    top = jnp.transpose(jnp.broadcast_to(spread_ref[0:1, :], shape))[:, 0:1]
    return [jnp.broadcast_to(column, (depth, width)) for column in (rate_on, rate_off, spread_ref[:, 0:1], top)]


def split2(value):
    high = value.astype(BF16)
    return high, (value - high.astype(F32)).astype(BF16)


def left_terms(spread):
    high, low = split2(spread)
    return jnp.concatenate([high, high, low], axis=1)


def product(left, free):
    high, low = split2(free)
    return jnp.dot(left, jnp.concatenate([high, low, high], axis=0), preferred_element_type=F32)


def plan_ahead(left, rates, free, bound):
    rate_on, rate_off, entry, top = rates
    moved = product(left, free)
    room = rate_on * (1.0 - bound)
    rate = room * moved - rate_off * bound
    gain = room * entry
    first = jnp.sum(top * (moved - rate), axis=0, keepdims=True)
    slope = jnp.sum(top * (entry - gain), axis=0, keepdims=True)
    return moved, (first, slope, bound[0:1, :] + rate[0:1, :], gain[0:1, :])


def put_coefs(coef_ref, across, width, row, parts):
    for index, part in enumerate(parts):
        for step in range(part.shape[1] // width):
            place = index * across + row + step
            coef_ref[place:place + 1, :] = part[:, step * width:(step + 1) * width]


TOGETHER = 4


def plan_kernel(free_ref, bound_ref, spread_ref, on_ref, off_ref, moved_ref, coef_ref):
    width = coef_ref.shape[1]
    across = coef_ref.shape[0] // 4
    rates = wall_rates(spread_ref, on_ref, off_ref, TOGETHER * width)
    left = left_terms(spread_ref[...])
    for row in range(0, across, TOGETHER):
        place = slice(row * width, (row + TOGETHER) * width)
        moved, parts = plan_ahead(left, rates, free_ref[:, place], bound_ref[:, place])
        moved_ref[:, place] = moved
        put_coefs(coef_ref, across, width, row, parts)


def wall_kernel(last, moved_ref, bound_ref, added_ref, spread_ref, on_ref, off_ref, *outs):
    across, width = added_ref.shape
    rates = wall_rates(spread_ref, on_ref, off_ref, TOGETHER * width)
    rate_on, rate_off, entry, _ = rates
    left = left_terms(spread_ref[...])
    for row in range(0, across, TOGETHER):
        place = slice(row * width, (row + TOGETHER) * width)
        added = jnp.concatenate([added_ref[row + step:row + step + 1, :] for step in range(TOGETHER)], axis=1)
        free = moved_ref[:, place] + entry * added
        bound = bound_ref[:, place]
        for substep in range(SUB):
            if substep:
                free = product(left, free)
            rate = rate_on * free * (1.0 - bound) - rate_off * bound
            free = free - rate
            bound = bound + rate
        outs[1][:, place] = bound
        if last:
            outs[0][:, place] = free
        else:
            moved, parts = plan_ahead(left, rates, free, bound)
            outs[0][:, place] = moved
            put_coefs(outs[2], across, width, row, parts)


def send_kernel(sectors, step, radial, *refs):
    packed = step % 2 == 0
    post_ref, one_ref, two_ref, code_ref, edges_ref, top_ref = refs[:6]
    refs = refs[6:]
    if packed:
        sent_refs, outs = refs[:2], refs[2:]
    else:
        outs = refs
    across, along = code_ref.shape
    post = Planes(post_ref, radial, across)
    behind, ahead = axial_rims(packed, one_ref, two_ref, across)
    end = radial - 1
    row = sublanes((across, along))
    surface = post.get(FLOWS, end) + post.get(FLOWS + 5, end - 1) + post.get(FLOWS + 5, end)
    surface = surface + axial_shift(post.get(FLOWS + 1, end), 1, FLOWS + 1, end, radial, behind, ahead)
    surface = surface + axial_shift(post.get(FLOWS + 2, end), -1, FLOWS + 2, end, radial, behind, ahead)
    rising = post.get(FLOWS + 3, end)
    falling = post.get(FLOWS + 4, end)
    surface = surface + jnp.where(row == 0, 0.0, pltpu.roll(rising, 1, 0))
    surface = surface + jnp.where(row == across - 1, 0.0, pltpu.roll(falling, across - 1, 0))
    values = code_list(surface) + [rising[across - 1:across, :], falling[0:1, :]]
    codes = code_list(code_ref[...]) + [edges_ref[0:1, :], edges_ref[1:2, :]]
    sums = scatter_rows(values, codes, sectors * across, along)
    parts = [top_ref[...]]
    if packed:
        whole_behind = by_parity(two_ref[...], one_ref[...])
        whole_ahead = by_parity(one_ref[...], two_ref[...])
        skip = rim_rows(radial, across, along)
        for index in range(2 if step == 0 else 1):
            place = skip + index * across
            parts = parts + [whole_behind[place:place + across, :], whole_ahead[place:place + across, :]]
    for rel in range(sectors):
        outs[rel][0:across] = sums[rel * across:(rel + 1) * across]
        for index, part in enumerate(parts):
            outs[rel][(1 + index) * across:(2 + index) * across] = part
    start = rims_start(step + 1, across)
    for out, places, side in ((outs[1], SECTOR_RISING, across - 1), (outs[sectors - 1], SECTOR_FALLING, 0)):
        for place, member in enumerate(places):
            moving = VELOCITIES[member][0]
            base = start + place * radial
            if moving:
                out[base:base + radial, :] = axial_shift_rows(post, member, moving, side, behind, ahead)
            else:
                out[base:base + radial, :] = post.rows(member, 0, radial, side)
    if packed:
        rise, fall = by_parity(sent_refs[0][...], sent_refs[1][...]), by_parity(sent_refs[1][...], sent_refs[0][...])
        ghosts = Ghosts(radial, across, along, whole_behind, whole_ahead, rise, fall)
        base = start + len(SECTOR_RISING) * radial
        for out, places, side in ((outs[1], SECTOR_RISING, across - 1), (outs[sectors - 1], SECTOR_FALLING, 0)):
            for place, member in enumerate(places):
                out[base + place:base + place + 1, :] = ghosts.risen(member)[side:side + 1, :]
            for place in range(len(places), across):
                out[base + place:base + place + 1, :] = jnp.zeros((1, along), F32)


def last_send_kernel(radial, across, post_ref, inner_ref, outer_ref, up_ref, down_ref):
    post = Planes(post_ref, radial, across)
    behind, ahead = axial_rims(False, inner_ref, outer_ref, across)
    for out, drug, plus, minus, side in ((up_ref, FLOWS + 3, 7, 10, across - 1), (down_ref, FLOWS + 4, 9, 8, 0)):
        out[0:radial, :] = post.rows(drug, 0, radial, side)
        value = axial_shift_rows(post, plus, 1, side, behind, ahead)
        out[radial:2 * radial, :] = value - axial_shift_rows(post, minus, -1, side, behind, ahead)


def fields_kernel(radial, across, post_ref, inner_ref, outer_ref, drug_ref, flow_ref):
    post = Planes(post_ref, radial, across)
    behind, ahead = axial_rims(False, inner_ref, outer_ref, across)
    for level in range(radial):
        def member_of(member):
            value = streamed(post, member, level, behind, ahead)
            step = VELOCITIES[member][1]
            if step:
                edge = 0 if step > 0 else across - 1
                value = jnp.where(sublanes(value.shape) == edge, 0.0, value)
            return value

        drug = member_of(FLOWS)
        for member in range(FLOWS + 1, MEMBERS):
            drug = drug + member_of(member)
        drug_ref[level] = drug
        flow = None
        for member in range(FLOWS):
            factor = VELOCITIES[member][0]
            if factor:
                value = member_of(member)
                flow = (value if factor > 0 else -value) if flow is None else (flow + value if factor > 0 else flow - value)
        flow_ref[level] = flow


def last_kernel(drug_part, flow_part, below, above, drug_ref, flow_ref):
    radial, across, along = drug_ref.shape
    row = sublanes((across, along))
    for part, out, base in ((drug_part, drug_ref, 0), (flow_part, flow_ref, radial)):
        for level in range(radial):
            place = base + level
            value = part[level] + jnp.where(row == 0, below[place:place + 1, :], 0.0)
            out[level] = value + jnp.where(row == across - 1, above[place:place + 1, :], 0.0)


def kernel_call(body, outs, count, micros, aliases=None):
    shapes = [out if isinstance(out, jax.ShapeDtypeStruct) else jax.ShapeDtypeStruct(out, F32) for out in outs]
    return pl.pallas_call(
        body,
        out_shape=shapes,
        in_specs=[pl.BlockSpec(memory_space=VMEM)] * count,
        out_specs=[pl.BlockSpec(memory_space=VMEM)] * len(outs),
        input_output_aliases=aliases or {},
        cost_estimate=pl.CostEstimate(flops=0, bytes_accessed=int(micros * 3.0e6), transcendentals=0),
        compiler_params=pltpu.CompilerParams(vmem_limit_bytes=24 * 1024 * 1024),
    )


def first_call(sectors, populations, sector, line, strut, free):
    members, _, across, along = populations.shape
    plane = (across, along)
    sizes = [((5 if hop in (1, sectors - 1) else 4) * across, along) for hop in range(sectors)]
    return pl.pallas_call(
        functools.partial(first_kernel, sectors),
        name="first",
        out_shape=[jax.ShapeDtypeStruct(plane, jnp.int32)] + [jax.ShapeDtypeStruct(size, F32) for size in sizes],
        in_specs=[pl.BlockSpec(memory_space=pltpu.HBM)] * 5,
        out_specs=[pl.BlockSpec(memory_space=VMEM)] * (1 + sectors),
        scratch_shapes=[
            VMEM((members - FLOWS, across, along), F32),
            VMEM(plane, jnp.int32),
            VMEM(plane, jnp.int32),
            VMEM(plane, jnp.int32),
            VMEM((across, free.shape[1]), F32),
            pltpu.SemaphoreType.DMA((5,)),
        ],
        compiler_params=pltpu.CompilerParams(vmem_limit_bytes=24 * 1024 * 1024),
    )(*[pltpu.with_memory_space_constraint(x, pltpu.HBM) for x in (populations, sector, line, strut, free)])


def per_device(populations, wall_free, wall_bound, wall_propagator, bind_on, bind_off, iface_sector, iface_line, strut_mask):
    members, radial, across, along = populations.shape
    sectors = lax.axis_size("th")
    plane = (across, along)
    flat = (members * radial * across, along)
    rims = len(SECTOR_RISING) * radial
    strut = strut_mask.reshape(plane)
    rate_on = bind_on.reshape(1, -1)
    rate_off = bind_off.reshape(1, -1)

    def exchange(boxes):
        inbox = [boxes[0]] + [None] * (sectors - 1)
        for hop in range(1, sectors):
            inbox[sectors - hop] = shifted(boxes[hop], "th", hop)
        return inbox

    codes, *boxes = first_call(sectors, populations, iface_sector.reshape(plane), iface_line.reshape(plane), strut, wall_free)
    inbox = exchange(boxes)
    state = populations.reshape(flat)
    speeds = (3 * across, along)
    four = (4 * across, along)
    two = (2 * across, along)
    rim = rim_rows(radial, across, along)
    shapes = wall_free.shape
    bulk, speed, *tiles = kernel_call(
        functools.partial(bulk_kernel, True, True, True, radial, across), [flat, speeds, (rim, along), (rim, along)], 1, 1.5
    )(state)
    moved, coefs = kernel_call(plan_kernel, [shapes, four], 5, 1.0)(
        wall_free, wall_bound, wall_propagator, rate_on, rate_off
    )
    bound = wall_bound
    fixed, ghost = [], []
    edges = sent = got = None
    for step in range(STEPS):
        odd, last = step % 2 == 1, step == STEPS - 1
        if odd:
            pair = [plane, plane]
        else:
            pair = [(rim + (2 if step == 0 else 1) * across, along)] * 2
        outs = [flat] + pair + [plane] * (1 if last else 2)
        if step == 0:
            outs = outs + [plane, plane, jax.ShapeDtypeStruct(plane, jnp.int32)]
        if step == 1:
            outs = outs + [jax.ShapeDtypeStruct(two, jnp.int32), two]
        extra = fixed + ([*sent, *got, *ghost] if odd else tiles)
        post, one, other, added, *rest = kernel_call(
            functools.partial(flux_kernel, sectors, step, radial), outs, 8 + sectors + len(extra), 0.8, {1: 0}
        )(state, bulk, speed, codes, strut, coefs, rate_on, rate_off, *inbox, *extra)
        if not last:
            top, *rest = rest
        if step == 0:
            fixed, edges = rest[:2], rest[2]
        if step == 1:
            ghost = rest
        if odd:
            rims_in, own = [one, other], []
        else:
            sent = [one, other]
            got = paired(*sent)
            rims_in, own = [*got], sent
        results = kernel_call(
            functools.partial(wall_kernel, last), [shapes, shapes] + ([] if last else [four]), 6, 1.5
        )(moved, bound, added, wall_propagator, rate_on, rate_off)
        if last:
            free, bound = results
            continue
        moved, bound, coefs = results
        start = rims_start(step + 1, across)
        long = start + rims + (0 if odd else across)
        sizes = [(long if hop in (1, sectors - 1) else start, along) for hop in range(sectors)]
        boxes = kernel_call(
            functools.partial(send_kernel, sectors, step, radial), sizes, 6 + len(own), 0.3
        )(post, *rims_in, codes, edges, top, *own)
        inbox = exchange(boxes)
        outs = [flat, flat, speeds] + ([(rim, along)] * 2 if odd else [])
        state, bulk, speed, *tiles = kernel_call(
            functools.partial(bulk_kernel, False, not odd, odd, radial, across), outs, 3, 2.0
        )(post, *rims_in)
    up, down = kernel_call(
        functools.partial(last_send_kernel, radial, across), [(2 * radial, along)] * 2, 3, 0.2
    )(post, *rims_in)
    below = shifted(up, "th", 1)
    above = shifted(down, "th", -1)
    parts = kernel_call(
        functools.partial(fields_kernel, radial, across), [(radial,) + plane] * 2, 3, 1.0
    )(post, *rims_in)
    drug_field, axial_flow = kernel_call(last_kernel, [(radial,) + plane] * 2, 4, 0.3)(*parts, below, above)
    return drug_field, axial_flow, free, bound


def solution(mesh):
    placed = (
        P(None, None, "th", "ax"),
        P(None, ("ax", "th")),
        P(None, ("ax", "th")),
        P(),
        P(),
        P(),
        P(("ax", "th"), None),
        P(("ax", "th")),
        P(("ax", "th")),
    )
    return jax.shard_map(
        per_device,
        mesh=mesh,
        in_specs=placed,
        out_specs=(
            P(None, "th", "ax"),
            P(None, "th", "ax"),
            P(None, ("ax", "th")),
            P(None, ("ax", "th")),
        ),
        check_vma=False,
    )
```
